32 devices in a mesh: grp: 4 (over y, x), dev: 8 (over z, core).
Axes of the slice: x: 2, y: 2, z: 4, core: 2. Of those that a mesh axis runs over, the one named last changes fastest.
Arguments:
- features: bfloat16 [4096, 768], P(('grp', 'dev')), may hold values from -6 to 6
- neighbours: int32 [4096, 25], P(('grp', 'dev')), may hold values from 0 to 4095, as said below
- neighbour_mask: int32 [4096, 25], P(('grp', 'dev')), may hold values from 0 to 1, as said below
- layer2_position: int32 [4096], P(('grp', 'dev')), may hold values from 0 to 4095, as said below
- self_weight1: bfloat16 [768, 1024], replicated, may hold values from -0.21875 to 0.21875
- neigh_weight1: bfloat16 [768, 1024], replicated, may hold values from -0.4375 to 0.4375
- self_weight2: bfloat16 [1024, 1024], replicated, may hold values from -0.1875 to 0.1875
- neigh_weight2: bfloat16 [1024, 1024], replicated, may hold values from -0.375 to 0.375
Outputs:
- embeddings: bfloat16 [4096, 1024], P(('grp', 'dev'))
The draws below stay inside these ranges and needn't reach their ends.
Inputs may be any that keep to these rules, and one draw needn't show every extreme that they name: `neighbours`: node n is owned by device n // 128 (devices numbered grp-major). Slot 0 of every node is valid. Of one device's nodes, at most 6 valid slots name nodes of any one other device, and exactly 6 do for some other device; 93 slots of one device name other devices' nodes, all of them valid. Invalid slots hold ids of the device's own nodes. `neighbour_mask`: values 0 or 1; 1 at slot 0 and wherever the neighbour lies on another device. A permutation of the nodes; a node's new owner, layer2_position // 128, is in the same group as its old one. One device hands exactly 32 nodes to each owner of its group whose index within the group differs from its own by an even number, and none to the others.
All inputs are finite; a program needn't handle non-finite values.
Results may differ from the reference program's by a relative error of at most 0.0052.
Values may be sent and summed in bfloat16 or wider, within the bound.
No kernel may reach another device: no remote copies, remote signals or barrier semaphores. Data moves between devices by JAX's collectives and lax.ppermute only.
A program may use at most 64 MiB of HBM per device.

```python
import jax
import jax.numpy as jnp
from jax import lax

F_IN = 768
HID = 1024
DEG = 25
ROWS = 128
CAP = 6
REMOTE = 93
CAP2 = 32
NODES = 4096
N_GRP = 4
N_DEV = 8


def edge_plan(key):
    device_count = N_GRP * N_DEV
    edge_count = ROWS * DEG

    def one_device(device_index):
        device_key = jax.random.fold_in(key, device_index)
        key_list = jax.random.split(device_key, 7)
        offsets = jnp.repeat(jnp.arange(1, device_count, dtype=jnp.int32), CAP)
        mixed = jax.random.permutation(key_list[0], offsets)
        forced = jax.random.randint(key_list[1], (), 1, device_count)
        ordering = jnp.argsort((mixed != forced).astype(jnp.int32), stable=True)
        chosen = mixed[ordering][:REMOTE]
        owners = (device_index + chosen) % device_count
        remote_ids = owners * ROWS + jax.random.randint(key_list[2], (REMOTE,), 0, ROWS)
        local_ids = device_index * ROWS + jax.random.randint(key_list[3], (edge_count,), 0, ROWS)
        places = jax.random.permutation(key_list[4], edge_count)[:REMOTE]
        neighbour_ids = local_ids.at[places].set(remote_ids)
        remote_flag = jnp.zeros((edge_count,), jnp.int32).at[places].set(1)
        keep_level = jax.random.randint(key_list[5], (), 3, 10)
        coin_flips = jax.random.randint(key_list[6], (edge_count,), 0, 10)
        leading = jnp.arange(edge_count) % DEG == 0
        usable = (coin_flips < keep_level) | (remote_flag == 1) | leading
        return (neighbour_ids.astype(jnp.int32), jnp.where(usable, 1, 0).astype(jnp.int32))
    neighbour_ids, usable = jax.vmap(one_device)(jnp.arange(device_count, dtype=jnp.int32))
    return (neighbour_ids.reshape(NODES, DEG), usable.reshape(NODES, DEG))


def draw_neighbours(key, part):
    return edge_plan(jax.random.fold_in(key, 11))[0]


def draw_neighbour_mask(key, part):
    return edge_plan(jax.random.fold_in(key, 11))[1]


def draw_layer2_position(key, part):
    block_total = N_DEV // 2

    def one_group(group_index):
        group_key = jax.random.fold_in(key, group_index)
        key_list = jax.random.split(group_key, 3)
        offsets = 2 * jax.random.permutation(key_list[0], block_total).astype(jnp.int32)
        sender_order = jax.vmap(lambda single: jax.random.permutation(single, ROWS))(jax.random.split(key_list[1], N_DEV))
        target_order = jax.vmap(lambda single: jax.random.permutation(single, ROWS))(jax.random.split(key_list[2], N_DEV))
        slot_index = jnp.arange(ROWS, dtype=jnp.int32)
        block_ids = slot_index // CAP2
        receiver = (jnp.arange(N_DEV, dtype=jnp.int32)[:, None] + offsets[block_ids][None, :]) % N_DEV
        position = (group_index * N_DEV + receiver) * ROWS + target_order[receiver, slot_index[None, :]]
        sender_rows = jnp.arange(N_DEV, dtype=jnp.int32)[:, None]
        return jnp.zeros((N_DEV, ROWS), jnp.int32).at[sender_rows, sender_order].set(position.astype(jnp.int32))
    return jax.vmap(one_group)(jnp.arange(N_GRP, dtype=jnp.int32)).reshape(NODES)


def block_scale(key, extent, shards, least, high):
    def one(dim, blocks):
        heights = jax.random.uniform(jax.random.fold_in(jax.random.fold_in(key, 6), dim), (blocks,), jnp.float32, least / len(shards), high / len(shards))
        return jnp.repeat(jnp.exp(heights), extent[dim] // blocks).reshape((-1,) + (1,) * (len(extent) - dim - 1))

    factor_of = one(*shards[0])
    for cut in shards[1:]:
        factor_of = factor_of * one(*cut)
    return factor_of


def scatter_about(stream_key, extent, scale, bound, pieces=(), kind=jnp.bfloat16):
    values = jax.random.normal(stream_key, extent, jnp.float32) * scale
    if len(pieces) > 0:
        values = block_scale(stream_key, extent, pieces, -0.22, 0.18) * values
    return jnp.clip(values, min=-bound, max=bound).astype(kind)


def setup_inputs(seed: int = 0) -> dict:
    seeds = jax.random.split(jax.random.key(seed), 9)
    return {
        "features": scatter_about(seeds[0], (NODES, F_IN), 1.0, 6.0, ((0, 32),)),
        "neighbours": draw_neighbours(jax.random.fold_in(seeds[8], 71), 0),
        "neighbour_mask": draw_neighbour_mask(jax.random.fold_in(seeds[8], 71), 0),
        "layer2_position": draw_layer2_position(jax.random.fold_in(seeds[8], 71), 0),
        "self_weight1": scatter_about(seeds[4], (F_IN, HID), F_IN ** -0.5, 0.21875),
        "neigh_weight1": scatter_about(seeds[5], (F_IN, HID), (F_IN // 4) ** -0.5, 0.4375),
        "self_weight2": scatter_about(seeds[6], (HID, HID), HID ** -0.5, 0.1875),
        "neigh_weight2": scatter_about(seeds[7], (HID, HID), (HID // 4) ** -0.5, 0.375),
    }


def aggregate_layer(table, self_rows, neighbours, neighbour_mask, self_weight, neigh_weight):
    device_count = neighbours.shape[0] // ROWS
    ids_blocks = neighbours.reshape(device_count, ROWS, DEG)
    mask_blocks = neighbour_mask.reshape(device_count, ROWS, DEG)
    self_blocks = self_rows.reshape(device_count, ROWS, self_rows.shape[1])

    def one_block(packed):
        block_ids, block_mask, block_self = packed
        picked = table[block_ids].astype(jnp.float32)
        weights = block_mask.astype(jnp.float32)
        summed = jnp.sum(picked * weights[:, :, None], axis=1)
        degree_count = jnp.sum(weights, axis=1)
        mean_rows = (summed / degree_count[:, None]).astype(jnp.bfloat16)
        return jnp.dot(block_self, self_weight, preferred_element_type=jnp.float32) + jnp.dot(mean_rows, neigh_weight, preferred_element_type=jnp.float32)

    result = lax.map(one_block, (ids_blocks, mask_blocks, self_blocks))
    return result.reshape(-1, self_weight.shape[1])


def reference(features, neighbours, neighbour_mask, layer2_position, self_weight1, neigh_weight1, self_weight2, neigh_weight2):
    hidden = jax.nn.relu(aggregate_layer(features, features, neighbours, neighbour_mask, self_weight1, neigh_weight1)).astype(jnp.bfloat16)
    final = aggregate_layer(hidden, hidden, neighbours, neighbour_mask, self_weight2, neigh_weight2).astype(jnp.bfloat16)
    embeddings = jnp.zeros_like(final).at[layer2_position.astype(jnp.int32)].set(final)
    return embeddings
```

```python
import functools

import jax
import jax.numpy as jnp
from jax import lax
from jax.experimental import pallas as pl
from jax.experimental.pallas import tpu as pltpu
from jax.sharding import PartitionSpec as P

CAP = 6
BOTH = ("grp", "dev")
F32 = jnp.float32
BF16 = jnp.bfloat16
I32 = jnp.int32


def divide(values, by):
    if by & (by - 1) == 0:
        return values >> (by.bit_length() - 1)
    return (values * (-(-(1 << 16) // by))) >> 16


def iota(shape, dim):
    return lax.broadcasted_iota(I32, shape, dim)


def bits(condition):
    return jnp.where(condition, 1.0, 0.0)


def earlier(count):
    return bits(iota((count, count), 0) < iota((count, count), 1)).astype(BF16)


def dot(left, right):
    return jnp.dot(left, right, preferred_element_type=F32)


def dot_lanes(left, right):
    return lax.dot_general(left, right, (((1,), (1,)), ((), ())), preferred_element_type=F32)


def whole(n):
    return [pl.BlockSpec(memory_space=pltpu.VMEM)] * n


def call(kernel, outs, operands, flops, name, limit=24 << 20):
    moved = sum(a.size * a.dtype.itemsize for a in (*operands, *outs))
    return pl.pallas_call(
        kernel,
        out_shape=outs,
        in_specs=whole(len(operands)),
        out_specs=whole(len(outs)) if isinstance(outs, (list, tuple)) else whole(1)[0],
        compiler_params=pltpu.CompilerParams(vmem_limit_bytes=limit),
        cost_estimate=pl.CostEstimate(flops=flops, bytes_accessed=moved, transcendentals=0),
        name=name,
    )(*operands)


def ask_kernel(members, peers, ids_ref, mask_ref, pos_ref, ask_ref, key_ref, local_ref, span_ref, wide):
    rows, degree = ids_ref.shape
    own = lax.axis_index("grp") * members + lax.axis_index("dev")
    wide[...] = jnp.zeros_like(wide)
    wide[:, :degree] = jnp.where(mask_ref[...] > 0, ids_ref[...], -1)
    slots = wide[...].T
    owner = divide(slots, rows)
    row = slots - owner * rows
    live = slots >= 0
    here = owner == own
    key = jnp.where(live & jnp.logical_not(here), owner, -1)
    peer = iota((peers, rows), 0)
    total = jnp.zeros((peers, rows), I32)
    for s in range(degree):
        total += jnp.where(key[s : s + 1] == peer, 1, 0)
    before = dot(total.astype(F32).astype(BF16), earlier(rows)).astype(I32)
    width = (rows - 1).bit_length()
    per_word = 30 // width if width <= 10 else 1
    per_word = min(per_word, CAP, 24 // width)
    words = -(-CAP // per_word)
    packed = [jnp.zeros((peers, rows), I32) for _ in range(words)]
    running = before
    for s in range(degree):
        hit = key[s : s + 1] == peer
        for w in range(words):
            shift = running - w * per_word
            fits = hit & (shift >= 0) & (shift < per_word)
            packed[w] += jnp.where(fits, row[s : s + 1] << (jnp.clip(shift, 0, per_word - 1) * width), 0)
        running += jnp.where(hit, 1, 0)
    lane = iota((peers, rows), 1)
    wanted = jnp.zeros((peers, rows), I32)
    for w in range(words):
        word = jnp.sum(packed[w].astype(F32), axis=1, keepdims=True).astype(I32)
        slot = lane - w * per_word
        mine = (slot >= 0) & (slot < per_word) & (lane < CAP)
        word = jnp.broadcast_to(word, (peers, rows))
        wanted += jnp.where(mine, (word >> (jnp.clip(slot, 0, per_word - 1) * width)) & ((1 << width) - 1), 0)
    pos = pos_ref[...]
    place = jnp.where(divide(pos, rows) == peer, (pos & (rows - 1)) + 1, 0) if rows & (rows - 1) == 0 else jnp.where(
        divide(pos, rows) == peer, pos - divide(pos, rows) * rows + 1, 0
    )
    ask_ref[...] = (place + wanted * (2 * rows)).reshape(peers, 1, rows)
    key_ref[...] = key
    local_ref[...] = jnp.where(live & here, row, -1)
    span_ref[0] = before
    span_ref[1] = total


def plan_kernel(
    members, peers, degree, key_ref, local_ref, span_ref, mask_ref, pos_ref, features_ref, weight_ref,
    near_ref, far_ref, near_moved_ref, far_moved_ref, move_ref, order_ref, count_ref, sum_ref, own_ref,
):
    rows = features_ref.shape[0]
    capacity = 2 * rows // members
    local = local_ref[...]
    node = iota((rows, rows), 0)
    near = jnp.zeros((rows, rows), F32)
    for s in range(degree):
        near += bits(local[s : s + 1] == node)
    near = near.T.astype(BF16)
    near_ref[...] = near
    before, total = span_ref[0], span_ref[1]
    far = [bits((before <= k) & (k < before + total)).astype(BF16) for k in range(CAP)]
    far = jnp.concatenate(far, axis=0)
    size = peers * CAP
    line = iota((size, size), 0)
    peer = divide(line, CAP)
    order = bits(iota((size, size), 1) == (line - peer * CAP) * peers + peer).astype(BF16)
    order_ref[...] = order
    far = dot(order, far).T.astype(BF16)
    far_ref[...] = far
    pos = pos_ref[...]
    owner = divide(pos, rows)
    member = owner - lax.axis_index("grp") * members
    line = iota((rows, rows), 0)
    step = divide(line, capacity)
    target = lax.axis_index("dev") + 2 * step
    target = jnp.where(target >= members, target - members, target)
    goes = target == member
    place = dot(bits(goes).astype(BF16), earlier(rows))
    move = bits(goes & (place.astype(I32) == line - step * capacity)).astype(BF16)
    move_ref[...] = move
    near_moved_ref[...] = dot(move, near).astype(BF16)
    far_moved_ref[...] = dot(move, far).astype(BF16)
    count = jnp.sum(mask_ref[...].astype(F32), axis=1, keepdims=True)
    count_ref[0] = jnp.broadcast_to(count, (rows, 128))
    moved = dot(move, jnp.broadcast_to(count, (rows, 128)).astype(BF16))
    count_ref[1] = moved
    features = features_ref[...]
    sum_ref[...] = dot(near, features)
    own_ref[...] = dot(features, weight_ref[...])


def store_rows(reply_ref, rows):
    peers, pairs, two, width = reply_ref.shape
    reply_ref[...] = rows.reshape(peers, pairs, two, width)


def serve_kernel(asked_ref, order_ref, source_ref, reply_ref, pick_ref):
    peers, _, rows = asked_ref.shape
    asked = asked_ref[...].reshape(peers, rows)
    wanted = divide(asked, 2 * rows)
    lane = iota((peers, rows), 1)
    picks = [bits(wanted[:, k : k + 1] == lane).astype(BF16) for k in range(CAP)]
    pick = dot(order_ref[...], jnp.concatenate(picks, axis=0)).astype(BF16)
    pick_ref[...] = pick
    store_rows(reply_ref, dot(pick, source_ref[...]).astype(BF16))


def place_kernel(members, asked_ref, place_ref):
    _, _, rows = asked_ref.shape
    capacity = 2 * rows // members
    me = lax.axis_index("dev")
    first = lax.axis_index("grp") * members
    line = iota((rows, rows), 0)
    step = divide(line, capacity)
    result = jnp.zeros((rows, rows), F32)
    before = earlier(rows)
    for q in range(members // 2):
        source = me - 2 * q
        source = first + jnp.where(source < 0, source + members, source)
        sent = asked_ref[source] & (2 * rows - 1)
        valid = jnp.broadcast_to(sent > 0, (rows, rows))
        rank = dot(bits(valid).astype(BF16), before).astype(I32)
        lands = bits(sent - 1 == line).astype(BF16)
        comes = bits(valid & (step == q) & (rank == line - step * capacity)).astype(BF16)
        result += dot_lanes(lands, comes)
    place_ref[...] = result.astype(BF16)


def layer_one_kernel(answer_ref, far_ref, sum_ref, own_ref, count_ref, weight_ref, pick_ref, hidden_ref, reply_ref):
    peers, pairs, two, width = answer_ref.shape
    answer = answer_ref[...].reshape(peers * pairs * two, width)
    summed = sum_ref[...] + dot(far_ref[...], answer)
    mean = (summed / count_ref[0][:, :1]).astype(BF16)
    hidden = jnp.maximum(own_ref[...] + dot(mean, weight_ref[...]), 0.0).astype(BF16)
    hidden_ref[...] = hidden
    store_rows(reply_ref, dot(pick_ref[...], hidden).astype(BF16))


def own_two_kernel(hidden_ref, near_ref, move_ref, weight_ref, sum_ref, own_ref):
    hidden = hidden_ref[...]
    sum_ref[...] = dot(near_ref[...], hidden)
    own_ref[...] = dot(dot(move_ref[...], hidden).astype(BF16), weight_ref[...])


def layer_two_kernel(answer_ref, far_ref, sum_ref, own_ref, count_ref, weight_ref, *final_refs):
    peers, pairs, two, width = answer_ref.shape
    answer = answer_ref[...].reshape(peers * pairs * two, width)
    summed = sum_ref[...] + dot(far_ref[...], answer)
    mean = (summed / count_ref[1][:, :1]).astype(BF16)
    final = (own_ref[...] + dot(mean, weight_ref[...])).astype(BF16)
    capacity = final_refs[0].shape[0]
    for q, ref in enumerate(final_refs):
        ref[...] = final[q * capacity : (q + 1) * capacity]


def scatter_kernel(place_ref, *refs):
    out_ref = refs[-1]
    arrived = jnp.concatenate([ref[...] for ref in refs[:-1]], axis=0)
    out_ref[...] = dot(place_ref[...], arrived).astype(BF16)


def body(features, neighbours, neighbour_mask, layer2_position, self_weight1, neigh_weight1, self_weight2, neigh_weight2):
    rows, degree = neighbours.shape
    members = lax.axis_size("dev")
    peers = lax.axis_size("grp") * members
    width_in, width = self_weight1.shape
    steps = members // 2
    capacity = rows // steps
    size = peers * CAP
    shape = jax.ShapeDtypeStruct
    pos = layer2_position.reshape(1, rows)

    ask, key, local, span = pl.pallas_call(
        functools.partial(ask_kernel, members, peers),
        out_shape=(
            shape((peers, 1, rows), I32),
            shape((rows, rows), I32),
            shape((rows, rows), I32),
            shape((2, peers, rows), I32),
        ),
        in_specs=whole(3),
        out_specs=whole(4),
        scratch_shapes=[pltpu.VMEM((rows, rows), I32)],
        compiler_params=pltpu.CompilerParams(vmem_limit_bytes=16 << 20),
        name="ask",
    )(neighbours, neighbour_mask, pos)
    asked = lax.all_to_all(ask, BOTH, 0, 0, tiled=True)
    near, far, near_moved, far_moved, move, order, count, sum_one, own_one = call(
        functools.partial(plan_kernel, members, peers, degree),
        (
            shape((rows, rows), BF16),
            shape((rows, size), BF16),
            shape((rows, rows), BF16),
            shape((rows, size), BF16),
            shape((rows, rows), BF16),
            shape((size, size), BF16),
            shape((2, rows, 128), F32),
            shape((rows, width_in), F32),
            shape((rows, width), F32),
        ),
        (key, local, span, neighbour_mask, pos, features, self_weight1),
        2 * rows * width_in * (rows + width),
        "plan",
        limit=40 << 20,
    )
    reply, pick = call(
        serve_kernel,
        (shape((peers, CAP // 2, 2, width_in), BF16), shape((size, rows), BF16)),
        (asked, order, features),
        2 * size * rows * width_in,
        "serve",
    )
    answer = lax.all_to_all(reply, BOTH, 0, 0, tiled=True)
    place = pl.pallas_call(
        functools.partial(place_kernel, members),
        out_shape=shape((rows, rows), BF16),
        in_specs=whole(1),
        out_specs=whole(1)[0],
        compiler_params=pltpu.CompilerParams(vmem_limit_bytes=16 << 20),
        cost_estimate=pl.CostEstimate(flops=4 * steps * rows**3, bytes_accessed=4 * peers * rows, transcendentals=0),
        name="place",
    )(asked)
    hidden, reply_two = call(
        layer_one_kernel,
        (shape((rows, width), BF16), shape((peers, CAP // 2, 2, width), BF16)),
        (answer, far, sum_one, own_one, count, neigh_weight1, pick),
        2 * rows * width_in * (size + width) + 2 * size * rows * width,
        "layer_one",
    )
    answer_two = lax.all_to_all(reply_two, BOTH, 0, 0, tiled=True)
    sum_two, own_two = call(
        own_two_kernel,
        (shape((rows, width), F32), shape((rows, width), F32)),
        (hidden, near_moved, move, self_weight2),
        2 * rows * width * (2 * rows + width),
        "own_two",
    )
    finals = call(
        layer_two_kernel,
        tuple(shape((capacity, width), BF16) for _ in range(steps)),
        (answer_two, far_moved, sum_two, own_two, count, neigh_weight2),
        2 * rows * width * (size + width),
        "layer_two",
    )
    arrived = [finals[0]]
    for q in range(1, steps):
        arrived.append(lax.ppermute(finals[q], "dev", [(i, (i + 2 * q) % members) for i in range(members)]))
    return pl.pallas_call(
        scatter_kernel,
        out_shape=shape((rows, width), BF16),
        in_specs=whole(1 + steps),
        out_specs=whole(1)[0],
        compiler_params=pltpu.CompilerParams(vmem_limit_bytes=16 << 20),
        cost_estimate=pl.CostEstimate(flops=2 * rows * rows * width, bytes_accessed=4 * rows * width, transcendentals=0),
        name="scatter",
    )(place, *arrived)


def solution(mesh):
    return jax.shard_map(
        body,
        mesh=mesh,
        in_specs=(
            P(BOTH, None),
            P(BOTH, None),
            P(BOTH, None),
            P(BOTH),
            P(),
            P(),
            P(),
            P(),
        ),
        out_specs=P(BOTH, None),
        check_vma=False,
    )
```

```python
import functools

import jax
import jax.numpy as jnp
from jax import lax
from jax.experimental import pallas as pl
from jax.experimental.pallas import tpu as pltpu
from jax.sharding import PartitionSpec as P

CAP = 6
BOTH = ("grp", "dev")
F32 = jnp.float32
BF16 = jnp.bfloat16
I32 = jnp.int32


def divide(values, by):
    if by & (by - 1) == 0:
        return values >> (by.bit_length() - 1)
    return (values * (-(-(1 << 16) // by))) >> 16


def iota(shape, dim):
    return lax.broadcasted_iota(I32, shape, dim)


def bits(condition):
    return jnp.where(condition, 1.0, 0.0)


def earlier(count):
    return bits(iota((count, count), 0) < iota((count, count), 1)).astype(BF16)


def dot(left, right):
    return jnp.dot(left, right, preferred_element_type=F32)


def dot_lanes(left, right):
    return lax.dot_general(left, right, (((1,), (1,)), ((), ())), preferred_element_type=F32)


def near_by(n):
    return [pl.BlockSpec(memory_space=pltpu.VMEM)] * n


def far_off(n):
    return [pl.BlockSpec(memory_space=pltpu.HBM)] * n


def call(kernel, outs, remote, operands, scratch, flops, name, limit=24 << 20):
    single = not isinstance(outs, tuple)
    leaves = (outs,) if single else outs
    moved = sum(a.size * a.dtype.itemsize for a in (*remote, *operands, *leaves))
    return pl.pallas_call(
        kernel,
        out_shape=outs,
        in_specs=far_off(len(remote)) + near_by(len(operands)),
        out_specs=near_by(1)[0] if single else near_by(len(leaves)),
        scratch_shapes=scratch,
        compiler_params=pltpu.CompilerParams(vmem_limit_bytes=limit),
        cost_estimate=pl.CostEstimate(flops=flops, bytes_accessed=moved, transcendentals=0),
        name=name,
    )(*(pltpu.with_memory_space_constraint(a, pltpu.HBM) for a in remote), *operands)


def fetches(weight_ref, held, sems):
    pieces = sems.shape[0]
    depth = weight_ref.shape[0] // pieces
    return [
        pltpu.make_async_copy(
            weight_ref.at[pl.ds(i * depth, depth)], held.at[pl.ds(i * depth, depth)], sems.at[i]
        )
        for i in range(pieces)
    ]


def dot_fetched(left, held, copies):
    depth = held.shape[0] // len(copies)
    result = None
    for i, copy in enumerate(copies):
        copy.wait()
        part = dot(left[:, i * depth : (i + 1) * depth], held[i * depth : (i + 1) * depth])
        result = part if result is None else result + part
    return result


def ask_kernel(members, peers, ids_hbm, mask_hbm, pos_hbm, ask_ref, key_ref, local_ref, span_ref, pos_ref, ids, mask, sems):
    degree, rows = ids.shape
    copies = [
        pltpu.make_async_copy(ids_hbm, ids, sems.at[0]),
        pltpu.make_async_copy(mask_hbm, mask, sems.at[1]),
        pltpu.make_async_copy(pos_hbm, pos_ref, sems.at[2]),
    ]
    for copy in copies:
        copy.start()
    own = lax.axis_index("grp") * members + lax.axis_index("dev")
    peer = iota((peers, rows), 0)
    prefix = earlier(rows)
    for copy in copies:
        copy.wait()
    slots = jnp.where(mask[...] > 0, ids[...], -1)
    owner = divide(jnp.maximum(slots, 0), rows)
    row = slots - owner * rows
    live = slots >= 0
    here = owner == own
    key = jnp.where(live & jnp.logical_not(here), owner, -1)
    total = jnp.zeros((peers, rows), I32)
    for s in range(degree):
        total += jnp.where(key[s : s + 1] == peer, 1, 0)
    before = dot(total.astype(F32).astype(BF16), prefix).astype(I32)
    width = (rows - 1).bit_length()
    per_word = max(1, min(CAP, 24 // width))
    words = -(-CAP // per_word)
    packed = [jnp.zeros((peers, rows), I32) for _ in range(words)]
    running = before
    for s in range(degree):
        hit = key[s : s + 1] == peer
        for w in range(words):
            shift = running - w * per_word
            fits = hit & (shift >= 0) & (shift < per_word)
            packed[w] += jnp.where(fits, row[s : s + 1] << (jnp.clip(shift, 0, per_word - 1) * width), 0)
        running += jnp.where(hit, 1, 0)
    lane = iota((peers, rows), 1)
    wanted = jnp.zeros((peers, rows), I32)
    for w in range(words):
        word = jnp.sum(packed[w].astype(F32), axis=1, keepdims=True).astype(I32)
        slot = lane - w * per_word
        mine = (slot >= 0) & (slot < per_word) & (lane < CAP)
        word = jnp.broadcast_to(word, (peers, rows))
        wanted += jnp.where(mine, (word >> (jnp.clip(slot, 0, per_word - 1) * width)) & ((1 << width) - 1), 0)
    pos = pos_ref[...]
    place = jnp.where(divide(pos, rows) == peer, pos - divide(pos, rows) * rows + 1, 0)
    ask_ref[...] = (place + wanted * (2 * rows)).reshape(peers, 1, rows)
    key_ref[...] = key
    local_ref[...] = jnp.where(live & here, row, -1)
    span_ref[0] = before
    span_ref[1] = total


def plan_kernel(
    peers, degree, weight_hbm, key_ref, local_ref, span_ref, features_ref,
    near_ref, far_ref, order_ref, count_ref, sum_ref, own_ref, held, sems,
):
    copies = fetches(weight_hbm, held, sems)
    for copy in copies:
        copy.start()
    rows = features_ref.shape[0]
    local = local_ref[...]
    node = iota((rows, rows), 0)
    near = jnp.zeros((rows, rows), F32)
    for s in range(degree):
        near += bits(local[s : s + 1] == node)
    near = near.T.astype(BF16)
    near_ref[...] = near
    before, total = span_ref[0], span_ref[1]
    far = [bits((before <= k) & (k < before + total)).astype(BF16) for k in range(CAP)]
    far = jnp.concatenate(far, axis=0)
    size = peers * CAP
    line = iota((size, size), 0)
    peer = divide(line, CAP)
    order = bits(iota((size, size), 1) == (line - peer * CAP) * peers + peer).astype(BF16)
    order_ref[...] = order
    far_ref[...] = dot(order, far).T.astype(BF16)
    live = bits((local >= 0) | (key_ref[...] >= 0))
    count_ref[...] = jnp.broadcast_to(jnp.sum(live, axis=0, keepdims=True), (rows, rows)).T
    features = features_ref[...]
    sum_ref[...] = dot(near, features)
    own_ref[...] = dot_fetched(features, held, copies)


def store_rows(reply_ref, rows):
    peers, pairs, two, width = reply_ref.shape
    reply_ref[...] = rows.reshape(peers, pairs, two, width)


def load_rows(answer_ref):
    peers, pairs, two, width = answer_ref.shape
    return answer_ref[...].reshape(peers * pairs * two, width)


def serve_kernel(asked_ref, order_ref, source_ref, reply_ref, pick_ref):
    peers, _, rows = asked_ref.shape
    asked = asked_ref[...].reshape(peers, rows)
    wanted = divide(asked, 2 * rows)
    lane = iota((peers, rows), 1)
    picks = [bits(wanted[:, k : k + 1] == lane).astype(BF16) for k in range(CAP)]
    pick = dot(order_ref[...], jnp.concatenate(picks, axis=0)).astype(BF16)
    pick_ref[...] = pick
    store_rows(reply_ref, dot(pick, source_ref[...]).astype(BF16))


def layer_one_kernel(weight_hbm, answer_ref, far_ref, sum_ref, own_ref, count_ref, pick_ref, hidden_ref, reply_ref, held, sems):
    copies = fetches(weight_hbm, held, sems)
    for copy in copies:
        copy.start()
    summed = sum_ref[...] + dot(far_ref[...], load_rows(answer_ref))
    mean = (summed / count_ref[:, :1]).astype(BF16)
    hidden = jnp.maximum(own_ref[...] + dot_fetched(mean, held, copies), 0.0).astype(BF16)
    hidden_ref[...] = hidden
    store_rows(reply_ref, dot(pick_ref[...], hidden).astype(BF16))


def own_two_kernel(
    members, weight_hbm, hidden_ref, near_ref, far_ref, count_ref, pos_ref, asked_ref,
    sum_ref, own_ref, far_moved_ref, count_moved_ref, place_ref, held, sems,
):
    copies = fetches(weight_hbm, held, sems)
    for copy in copies:
        copy.start()
    rows = hidden_ref.shape[0]
    capacity = 2 * rows // members
    me = lax.axis_index("dev")
    first = lax.axis_index("grp") * members
    line = iota((rows, rows), 0)
    step = divide(line, capacity)
    rank = line - step * capacity
    target = me + 2 * step
    target = jnp.where(target >= members, target - members, target)
    goes = target == divide(pos_ref[...], rows) - first
    prefix = earlier(rows)
    before = dot(bits(goes).astype(BF16), prefix).astype(I32)
    move = bits(goes & (before == rank)).astype(BF16)
    hidden = hidden_ref[...]
    sum_ref[...] = dot(dot(move, near_ref[...]).astype(BF16), hidden)
    far_moved_ref[...] = dot(move, far_ref[...]).astype(BF16)
    count_moved_ref[...] = dot(move, count_ref[...].astype(BF16))
    own_ref[...] = dot_fetched(dot(move, hidden).astype(BF16), held, copies)
    place = jnp.zeros((rows, rows), F32)
    for q in range(members // 2):
        source = me - 2 * q
        source = first + jnp.where(source < 0, source + members, source)
        sent = asked_ref[source] & (2 * rows - 1)
        valid = jnp.broadcast_to(sent > 0, (rows, rows))
        before = dot(bits(valid).astype(BF16), prefix).astype(I32)
        lands = bits(sent - 1 == line).astype(BF16)
        comes = bits(valid & (step == q) & (before == rank)).astype(BF16)
        place += dot_lanes(lands, comes)
    place_ref[...] = place.astype(BF16)


def layer_two_kernel(weight_hbm, answer_ref, far_ref, sum_ref, own_ref, count_ref, *refs):
    final_refs, held, sems = refs[:-2], refs[-2], refs[-1]
    copies = fetches(weight_hbm, held, sems)
    for copy in copies:
        copy.start()
    summed = sum_ref[...] + dot(far_ref[...], load_rows(answer_ref))
    mean = (summed / count_ref[:, :1]).astype(BF16)
    final = (own_ref[...] + dot_fetched(mean, held, copies)).astype(BF16)
    capacity = final_refs[0].shape[0]
    for q, ref in enumerate(final_refs):
        ref[...] = final[q * capacity : (q + 1) * capacity]


def scatter_kernel(place_ref, *refs):
    out_ref = refs[-1]
    arrived = jnp.concatenate([ref[...] for ref in refs[:-1]], axis=0)
    out_ref[...] = dot(place_ref[...], arrived).astype(BF16)


def body(features, neighbours, neighbour_mask, layer2_position, self_weight1, neigh_weight1, self_weight2, neigh_weight2):
    rows, degree = neighbours.shape
    members = lax.axis_size("dev")
    peers = lax.axis_size("grp") * members
    width_in, width = self_weight1.shape
    steps = members // 2
    capacity = rows // steps
    size = peers * CAP
    shape = jax.ShapeDtypeStruct
    copies = pltpu.SemaphoreType.DMA

    ask, key, local, span, pos = call(
        functools.partial(ask_kernel, members, peers),
        (
            shape((peers, 1, rows), I32),
            shape((degree, rows), I32),
            shape((degree, rows), I32),
            shape((2, peers, rows), I32),
            shape((1, rows), I32),
        ),
        (neighbours.T, neighbour_mask.T, layer2_position.reshape(1, rows)),
        (),
        [pltpu.VMEM((degree, rows), I32), pltpu.VMEM((degree, rows), I32), copies((3,))],
        2 * peers * rows * rows,
        "ask",
    )
    asked = lax.all_to_all(ask, BOTH, 0, 0, tiled=True)
    near, far, order, count, sum_one, own_one = call(
        functools.partial(plan_kernel, peers, degree),
        (
            shape((rows, rows), BF16),
            shape((rows, size), BF16),
            shape((size, size), BF16),
            shape((rows, rows), F32),
            shape((rows, width_in), F32),
            shape((rows, width), F32),
        ),
        (self_weight1,),
        (key, local, span, features),
        [pltpu.VMEM((width_in, width), BF16), copies((1,))],
        2 * rows * width_in * (rows + width),
        "plan",
        limit=40 << 20,
    )
    reply, pick = call(
        serve_kernel,
        (shape((peers, CAP // 2, 2, width_in), BF16), shape((size, rows), BF16)),
        (),
        (asked, order, features),
        [],
        2 * size * rows * width_in,
        "serve",
    )
    answer = lax.all_to_all(reply, BOTH, 0, 0, tiled=True)
    hidden, reply_two = call(
        layer_one_kernel,
        (shape((rows, width), BF16), shape((peers, CAP // 2, 2, width), BF16)),
        (neigh_weight1,),
        (answer, far, sum_one, own_one, count, pick),
        [pltpu.VMEM((width_in, width), BF16), copies((3,))],
        2 * rows * width_in * (size + width) + 2 * size * rows * width,
        "layer_one",
    )
    answer_two = lax.all_to_all(reply_two, BOTH, 0, 0, tiled=True)
    sum_two, own_two, far_moved, count_moved, place = call(
        functools.partial(own_two_kernel, members),
        (
            shape((rows, width), F32),
            shape((rows, width), F32),
            shape((rows, size), BF16),
            shape((rows, rows), F32),
            shape((rows, rows), BF16),
        ),
        (self_weight2,),
        (hidden, near, far, count, pos, asked),
        [pltpu.VMEM((width, width), BF16), copies((1,))],
        2 * rows * width * (2 * rows + width),
        "own_two",
    )
    finals = call(
        layer_two_kernel,
        tuple(shape((capacity, width), BF16) for _ in range(steps)),
        (neigh_weight2,),
        (answer_two, far_moved, sum_two, own_two, count_moved),
        [pltpu.VMEM((width, width), BF16), copies((4,))],
        2 * rows * width * (size + width),
        "layer_two",
    )
    arrived = [finals[0]]
    for q in range(1, steps):
        arrived.append(lax.ppermute(finals[q], "dev", [(i, (i + 2 * q) % members) for i in range(members)]))
    return call(
        scatter_kernel,
        shape((rows, width), BF16),
        (),
        (place, *arrived),
        [],
        2 * rows * rows * width,
        "scatter",
    )


def solution(mesh):
    return jax.shard_map(
        body,
        mesh=mesh,
        in_specs=(
            P(BOTH, None),
            P(BOTH, None),
            P(BOTH, None),
            P(BOTH),
            P(),
            P(),
            P(),
            P(),
        ),
        out_specs=P(BOTH, None),
        check_vma=False,
    )
```

```python
import functools

import jax
import jax.numpy as jnp
from jax import lax
from jax.experimental import pallas as pl
from jax.experimental.pallas import tpu as pltpu
from jax.sharding import PartitionSpec as P

CAP = 6
BOTH = ("grp", "dev")
F32 = jnp.float32
BF16 = jnp.bfloat16
I32 = jnp.int32


def divide(values, by):
    if by & (by - 1) == 0:
        return values >> (by.bit_length() - 1)
    return (values * (-(-(1 << 16) // by))) >> 16


def iota(shape, dim):
    return lax.broadcasted_iota(I32, shape, dim)


def bits(condition):
    return jnp.where(condition, 1.0, 0.0)


def earlier(count):
    return bits(iota((count, count), 0) < iota((count, count), 1)).astype(BF16)


def dot(left, right):
    return jnp.dot(left, right, preferred_element_type=F32)


def dot_lanes(left, right):
    return lax.dot_general(left, right, (((1,), (1,)), ((), ())), preferred_element_type=F32)


def near_by(n):
    return [pl.BlockSpec(memory_space=pltpu.VMEM)] * n


def far_off(n):
    return [pl.BlockSpec(memory_space=pltpu.HBM)] * n


def call(kernel, outs, remote, operands, scratch, flops, name, limit=24 << 20):
    single = not isinstance(outs, tuple)
    leaves = (outs,) if single else outs
    moved = sum(a.size * a.dtype.itemsize for a in (*remote, *operands, *leaves))
    return pl.pallas_call(
        kernel,
        out_shape=outs,
        in_specs=far_off(len(remote)) + near_by(len(operands)),
        out_specs=near_by(1)[0] if single else near_by(len(leaves)),
        scratch_shapes=scratch,
        compiler_params=pltpu.CompilerParams(vmem_limit_bytes=limit),
        cost_estimate=pl.CostEstimate(flops=flops, bytes_accessed=moved, transcendentals=0),
        name=name,
    )(*(pltpu.with_memory_space_constraint(a, pltpu.HBM) for a in remote), *operands)


def fetches(weight_ref, held, sems):
    pieces = sems.shape[0]
    depth = weight_ref.shape[0] // pieces
    return [
        pltpu.make_async_copy(
            weight_ref.at[pl.ds(i * depth, depth)], held.at[pl.ds(i * depth, depth)], sems.at[i]
        )
        for i in range(pieces)
    ]


def dot_fetched(left, held, copies):
    depth = held.shape[0] // len(copies)
    result = None
    for i, copy in enumerate(copies):
        copy.wait()
        part = dot(left[:, i * depth : (i + 1) * depth], held[i * depth : (i + 1) * depth])
        result = part if result is None else result + part
    return result


def ask_kernel(members, peers, ids_hbm, mask_hbm, pos_hbm, ask_ref, key_ref, local_ref, span_ref, ids, mask, pos_ref, sems):
    degree, rows = ids.shape
    copies = [
        pltpu.make_async_copy(ids_hbm, ids, sems.at[0]),
        pltpu.make_async_copy(mask_hbm, mask, sems.at[1]),
        pltpu.make_async_copy(pos_hbm, pos_ref, sems.at[2]),
    ]
    for copy in copies:
        copy.start()
    own = lax.axis_index("grp") * members + lax.axis_index("dev")
    peer = iota((peers, rows), 0)
    prefix = earlier(rows)
    for copy in copies:
        copy.wait()
    slots = jnp.where(mask[...] > 0, ids[...], -1)
    owner = divide(jnp.maximum(slots, 0), rows)
    row = slots - owner * rows
    live = slots >= 0
    here = owner == own
    key = jnp.where(live & jnp.logical_not(here), owner, -1)
    half = CAP // 2
    width = (rows - 1).bit_length()
    top = width * (half - 1)
    low = jnp.zeros((peers, rows), I32)
    high = jnp.zeros((peers, rows), I32)
    total = jnp.zeros((peers, rows), I32)
    for s in range(degree):
        hit = key[s : s + 1] == peer
        high = jnp.where(hit, (high << width) | (low >> top), high)
        low = jnp.where(hit, ((low & ((1 << top) - 1)) << width) | row[s : s + 1], low)
        total += jnp.where(hit, 1, 0)
    before = dot(total.astype(F32).astype(BF16), prefix).astype(I32)
    packed = [jnp.where(before == 0, low, 0), jnp.where(before == 0, high, jnp.where(before == half, low, 0))]
    for k in range(1, half):
        shift, rest = width * k, width * (half - k)
        inside = before == k
        packed[0] = jnp.where(inside, (low & ((1 << rest) - 1)) << shift, packed[0])
        packed[1] = jnp.where(inside, (high << shift) | (low >> rest), packed[1])
        packed[1] = jnp.where(before == half + k, low << shift, packed[1])
    lane = iota((peers, rows), 1)
    wanted = jnp.zeros((peers, rows), I32)
    for w, word in enumerate(packed):
        word = jnp.broadcast_to(jnp.sum(word.astype(F32), axis=1, keepdims=True).astype(I32), (peers, rows))
        for k in range(half):
            wanted = jnp.where(lane == w * half + k, (word >> (width * k)) & ((1 << width) - 1), wanted)
    pos = pos_ref[...]
    place = jnp.where(divide(pos, rows) == peer, pos - divide(pos, rows) * rows + 1, 0)
    ask_ref[...] = (place + wanted * (2 * rows)).reshape(peers, 1, rows)
    key_ref[...] = key
    local_ref[...] = jnp.where(live & here, row, -1)
    span_ref[0] = before
    span_ref[1] = total


def plan_kernel(
    peers, degree, features_hbm, weight_hbm, later_hbm, key_ref, local_ref, span_ref,
    near_ref, far_ref, order_ref, count_ref, sum_ref, own_ref, features_ref, later_ref, held, sems,
):
    taken = pltpu.make_async_copy(features_hbm, features_ref, sems.at[1])
    later = pltpu.make_async_copy(later_hbm.at[pl.ds(0, later_ref.shape[0])], later_ref, sems.at[2])
    copies = fetches(weight_hbm, held, sems.at[pl.ds(0, 1)])
    for copy in (taken, *copies, later):
        copy.start()
    rows = features_ref.shape[0]
    local = local_ref[...]
    node = iota((rows, rows), 0)
    near = jnp.zeros((rows, rows), F32)
    for s in range(degree):
        near += bits(local[s : s + 1] == node)
    near = near.T.astype(BF16)
    near_ref[...] = near
    before, total = span_ref[0], span_ref[1]
    far = [bits((before <= k) & (k < before + total)).astype(BF16) for k in range(CAP)]
    far = jnp.concatenate(far, axis=0)
    size = peers * CAP
    line = iota((size, size), 0)
    peer = divide(line, CAP)
    order = bits(iota((size, size), 1) == (line - peer * CAP) * peers + peer).astype(BF16)
    order_ref[...] = order
    far_ref[...] = dot(order, far).T.astype(BF16)
    live = bits((local >= 0) | (key_ref[...] >= 0))
    count_ref[...] = jnp.broadcast_to(jnp.sum(live, axis=0, keepdims=True), (rows, rows)).T.astype(BF16)
    taken.wait()
    features = features_ref[...]
    sum_ref[...] = dot(near, features)
    own_ref[...] = dot_fetched(features, held, copies)
    later.wait()


def store_rows(reply_ref, rows):
    peers, pairs, two, width = reply_ref.shape
    reply_ref[...] = rows.reshape(peers, pairs, two, width)


def load_rows(answer_ref):
    peers, pairs, two, width = answer_ref.shape
    return answer_ref[...].reshape(peers * pairs * two, width)


def serve_kernel(asked_ref, order_ref, source_ref, reply_ref, pick_ref):
    peers, _, rows = asked_ref.shape
    asked = asked_ref[...].reshape(peers, rows)
    wanted = divide(asked, 2 * rows)
    lane = iota((peers, rows), 1)
    picks = [bits(wanted[:, k : k + 1] == lane).astype(BF16) for k in range(CAP)]
    pick = dot(order_ref[...], jnp.concatenate(picks, axis=0)).astype(BF16)
    pick_ref[...] = pick
    store_rows(reply_ref, dot(pick, source_ref[...]).astype(BF16))


def mean_product(weight_hbm, weight_ref, held, sems, answer_ref, far_ref, sum_ref, own_ref, count_ref):
    ready = weight_ref.shape[0]
    rest = pltpu.make_async_copy(weight_hbm.at[pl.ds(ready, held.shape[0])], held, sems.at[0])
    rest.start()
    summed = sum_ref[...] + dot(far_ref[...], load_rows(answer_ref))
    mean = (summed / count_ref[:, :1].astype(F32)).astype(BF16)
    result = own_ref[...] + dot(mean[:, :ready], weight_ref[...])
    rest.wait()
    return result + dot(mean[:, ready:], held[...])


def layer_one_kernel(
    weight_hbm, weight_ref, answer_ref, far_ref, sum_ref, own_ref, count_ref, pick_ref, hidden_ref, reply_ref, held, sems
):
    hidden = mean_product(weight_hbm, weight_ref, held, sems, answer_ref, far_ref, sum_ref, own_ref, count_ref)
    hidden = jnp.maximum(hidden, 0.0).astype(BF16)
    hidden_ref[...] = hidden
    store_rows(reply_ref, dot(pick_ref[...], hidden).astype(BF16))


def own_two_kernel(
    members, weight_hbm, later_hbm, pos_hbm, hidden_ref, near_ref, far_ref, count_ref, asked_ref,
    sum_ref, own_ref, far_moved_ref, count_moved_ref, place_ref, later_ref, held, pos_ref, sems,
):
    copies = fetches(weight_hbm, held, sems.at[pl.ds(0, 1)])
    later = pltpu.make_async_copy(later_hbm.at[pl.ds(0, later_ref.shape[0])], later_ref, sems.at[1])
    taken = pltpu.make_async_copy(pos_hbm, pos_ref, sems.at[2])
    for copy in (taken, *copies, later):
        copy.start()
    rows = hidden_ref.shape[0]
    capacity = 2 * rows // members
    me = lax.axis_index("dev")
    first = lax.axis_index("grp") * members
    line = iota((rows, rows), 0)
    step = divide(line, capacity)
    rank = line - step * capacity
    target = me + 2 * step
    target = jnp.where(target >= members, target - members, target)
    taken.wait()
    goes = target == divide(pos_ref[...], rows) - first
    prefix = earlier(rows)
    before = dot(bits(goes).astype(BF16), prefix).astype(I32)
    move = bits(goes & (before == rank)).astype(BF16)
    hidden = hidden_ref[...]
    sum_ref[...] = dot(dot(move, near_ref[...]).astype(BF16), hidden)
    far_moved_ref[...] = dot(move, far_ref[...]).astype(BF16)
    count_moved_ref[...] = dot(move, count_ref[...]).astype(BF16)
    own_ref[...] = dot_fetched(dot(move, hidden).astype(BF16), held, copies)
    place = jnp.zeros((rows, rows), F32)
    for q in range(members // 2):
        source = me - 2 * q
        source = first + jnp.where(source < 0, source + members, source)
        sent = asked_ref[source] & (2 * rows - 1)
        valid = jnp.broadcast_to(sent > 0, (rows, rows))
        before = dot(bits(valid).astype(BF16), prefix).astype(I32)
        lands = bits(sent - 1 == line).astype(BF16)
        comes = bits(valid & (step == q) & (before == rank)).astype(BF16)
        place += dot_lanes(lands, comes)
    place_ref[...] = place.astype(BF16)
    later.wait()


def layer_two_kernel(weight_hbm, weight_ref, answer_ref, far_ref, sum_ref, own_ref, count_ref, *refs):
    final_refs, held, sems = refs[:-2], refs[-2], refs[-1]
    final = mean_product(weight_hbm, weight_ref, held, sems, answer_ref, far_ref, sum_ref, own_ref, count_ref)
    final = final.astype(BF16)
    capacity = final_refs[0].shape[0]
    for q, ref in enumerate(final_refs):
        ref[...] = final[q * capacity : (q + 1) * capacity]


def scatter_kernel(place_ref, *refs):
    out_ref = refs[-1]
    arrived = jnp.concatenate([ref[...] for ref in refs[:-1]], axis=0)
    out_ref[...] = dot(place_ref[...], arrived).astype(BF16)


def body(features, neighbours, neighbour_mask, layer2_position, self_weight1, neigh_weight1, self_weight2, neigh_weight2):
    rows, degree = neighbours.shape
    members = lax.axis_size("dev")
    peers = lax.axis_size("grp") * members
    width_in, width = self_weight1.shape
    steps = members // 2
    capacity = rows // steps
    size = peers * CAP
    ready, ready_two = width_in * 2 // 3, width * 3 // 4
    shape = jax.ShapeDtypeStruct
    copies = pltpu.SemaphoreType.DMA

    pos = layer2_position.reshape(1, rows)
    ask, key, local, span = call(
        functools.partial(ask_kernel, members, peers),
        (
            shape((peers, 1, rows), I32),
            shape((degree, rows), I32),
            shape((degree, rows), I32),
            shape((2, peers, rows), I32),
        ),
        (neighbours.T, neighbour_mask.T, pos),
        (),
        [pltpu.VMEM((degree, rows), I32), pltpu.VMEM((degree, rows), I32), pltpu.VMEM((1, rows), I32), copies((3,))],
        2 * peers * rows * rows,
        "ask",
    )
    asked = lax.all_to_all(ask, BOTH, 0, 0, tiled=True)
    near, far, order, count, sum_one, own_one, features, weight = call(
        functools.partial(plan_kernel, peers, degree),
        (
            shape((rows, rows), BF16),
            shape((rows, size), BF16),
            shape((size, size), BF16),
            shape((rows, rows), BF16),
            shape((rows, width_in), F32),
            shape((rows, width), F32),
            shape((rows, width_in), BF16),
            shape((ready, width), BF16),
        ),
        (features, self_weight1, neigh_weight1),
        (key, local, span),
        [pltpu.VMEM((width_in, width), BF16), copies((3,))],
        2 * rows * width_in * (rows + width),
        "plan",
        limit=40 << 20,
    )
    reply, pick = call(
        serve_kernel,
        (shape((peers, CAP // 2, 2, width_in), BF16), shape((size, rows), BF16)),
        (),
        (asked, order, features),
        [],
        2 * size * rows * width_in,
        "serve",
    )
    answer = lax.all_to_all(reply, BOTH, 0, 0, tiled=True)
    hidden, reply_two = call(
        layer_one_kernel,
        (shape((rows, width), BF16), shape((peers, CAP // 2, 2, width), BF16)),
        (neigh_weight1,),
        (weight, answer, far, sum_one, own_one, count, pick),
        [pltpu.VMEM((width_in - ready, width), BF16), copies((1,))],
        2 * rows * width_in * (size + width) + 2 * size * rows * width,
        "layer_one",
    )
    answer_two = lax.all_to_all(reply_two, BOTH, 0, 0, tiled=True)
    sum_two, own_two, far_moved, count_moved, place, weight = call(
        functools.partial(own_two_kernel, members),
        (
            shape((rows, width), F32),
            shape((rows, width), F32),
            shape((rows, size), BF16),
            shape((rows, rows), BF16),
            shape((rows, rows), BF16),
            shape((ready_two, width), BF16),
        ),
        (self_weight2, neigh_weight2, pos),
        (hidden, near, far, count, asked),
        [pltpu.VMEM((width, width), BF16), pltpu.VMEM((1, rows), I32), copies((3,))],
        2 * rows * width * (2 * rows + width),
        "own_two",
    )
    finals = call(
        layer_two_kernel,
        tuple(shape((capacity, width), BF16) for _ in range(steps)),
        (neigh_weight2,),
        (weight, answer_two, far_moved, sum_two, own_two, count_moved),
        [pltpu.VMEM((width - ready_two, width), BF16), copies((1,))],
        2 * rows * width * (size + width),
        "layer_two",
    )
    arrived = [finals[0]]
    for q in range(1, steps):
        arrived.append(lax.ppermute(finals[q], "dev", [(i, (i + 2 * q) % members) for i in range(members)]))
    return call(
        scatter_kernel,
        shape((rows, width), BF16),
        (),
        (place, *arrived),
        [],
        2 * rows * rows * width,
        "scatter",
    )


def solution(mesh):
    return jax.shard_map(
        body,
        mesh=mesh,
        in_specs=(
            P(BOTH, None),
            P(BOTH, None),
            P(BOTH, None),
            P(BOTH),
            P(),
            P(),
            P(),
            P(),
        ),
        out_specs=P(BOTH, None),
        check_vma=False,
    )
```

```python
import functools

import jax
import jax.numpy as jnp
from jax import lax
from jax.experimental import pallas as pl
from jax.experimental.pallas import tpu as pltpu
from jax.sharding import PartitionSpec as P

CAP = 6
BOTH = ("grp", "dev")
F32 = jnp.float32
BF16 = jnp.bfloat16
I32 = jnp.int32


def divide(values, by):
    if by & (by - 1) == 0:
        return values >> (by.bit_length() - 1)
    return (values * (-(-(1 << 16) // by))) >> 16


def iota(shape, dim):
    return lax.broadcasted_iota(I32, shape, dim)


def bits(condition):
    return jnp.where(condition, 1.0, 0.0)


def earlier(count):
    return bits(iota((count, count), 0) < iota((count, count), 1)).astype(BF16)


def dot(left, right):
    return jnp.dot(left, right, preferred_element_type=F32)


def dot_lanes(left, right):
    return lax.dot_general(left, right, (((1,), (1,)), ((), ())), preferred_element_type=F32)


def near_by(n):
    return [pl.BlockSpec(memory_space=pltpu.VMEM)] * n


def far_off(n):
    return [pl.BlockSpec(memory_space=pltpu.HBM)] * n


def call(kernel, outs, remote, operands, scratch, flops, name, limit=24 << 20):
    single = not isinstance(outs, tuple)
    leaves = (outs,) if single else outs
    moved = sum(a.size * a.dtype.itemsize for a in (*remote, *operands, *leaves))
    return pl.pallas_call(
        kernel,
        out_shape=outs,
        in_specs=far_off(len(remote)) + near_by(len(operands)),
        out_specs=near_by(1)[0] if single else near_by(len(leaves)),
        scratch_shapes=scratch,
        compiler_params=pltpu.CompilerParams(vmem_limit_bytes=limit),
        cost_estimate=pl.CostEstimate(flops=flops, bytes_accessed=moved, transcendentals=0),
        name=name,
    )(*(pltpu.with_memory_space_constraint(a, pltpu.HBM) for a in remote), *operands)


def fetches(weight_ref, held, sems):
    pieces = sems.shape[0]
    depth = weight_ref.shape[0] // pieces
    return [
        pltpu.make_async_copy(
            weight_ref.at[pl.ds(i * depth, depth)], held.at[pl.ds(i * depth, depth)], sems.at[i]
        )
        for i in range(pieces)
    ]


def dot_fetched(left, held, copies):
    depth = held.shape[0] // len(copies)
    result = None
    for i, copy in enumerate(copies):
        copy.wait()
        part = dot(left[:, i * depth : (i + 1) * depth], held[i * depth : (i + 1) * depth])
        result = part if result is None else result + part
    return result


def ask_kernel(members, peers, ids_hbm, mask_hbm, pos_hbm, ask_ref, key_ref, local_ref, span_ref, ids, mask, pos_ref, sems):
    degree, rows = ids.shape
    copies = [
        pltpu.make_async_copy(ids_hbm, ids, sems.at[0]),
        pltpu.make_async_copy(mask_hbm, mask, sems.at[1]),
        pltpu.make_async_copy(pos_hbm, pos_ref, sems.at[2]),
    ]
    for copy in copies:
        copy.start()
    own = lax.axis_index("grp") * members + lax.axis_index("dev")
    peer = iota((peers, rows), 0)
    prefix = earlier(rows)
    for copy in copies:
        copy.wait()
    slots = jnp.where(mask[...] > 0, ids[...], -1)
    owner = divide(jnp.maximum(slots, 0), rows)
    row = slots - owner * rows
    live = slots >= 0
    here = owner == own
    key = jnp.where(live & jnp.logical_not(here), owner, -1)
    half = CAP // 2
    width = (rows - 1).bit_length()
    top = width * (half - 1)
    low = jnp.zeros((peers, rows), I32)
    high = jnp.zeros((peers, rows), I32)
    total = jnp.zeros((peers, rows), I32)
    for s in range(degree):
        hit = key[s : s + 1] == peer
        high = jnp.where(hit, (high << width) | (low >> top), high)
        low = jnp.where(hit, ((low & ((1 << top) - 1)) << width) | row[s : s + 1], low)
        total += jnp.where(hit, 1, 0)
    before = dot(total.astype(F32).astype(BF16), prefix).astype(I32)
    packed = [jnp.where(before == 0, low, 0), jnp.where(before == 0, high, jnp.where(before == half, low, 0))]
    for k in range(1, half):
        shift, rest = width * k, width * (half - k)
        inside = before == k
        packed[0] = jnp.where(inside, (low & ((1 << rest) - 1)) << shift, packed[0])
        packed[1] = jnp.where(inside, (high << shift) | (low >> rest), packed[1])
        packed[1] = jnp.where(before == half + k, low << shift, packed[1])
    lane = iota((peers, rows), 1)
    wanted = jnp.zeros((peers, rows), I32)
    for w, word in enumerate(packed):
        word = jnp.broadcast_to(jnp.sum(word.astype(F32), axis=1, keepdims=True).astype(I32), (peers, rows))
        for k in range(half):
            wanted = jnp.where(lane == w * half + k, (word >> (width * k)) & ((1 << width) - 1), wanted)
    pos = pos_ref[...]
    place = jnp.where(divide(pos, rows) == peer, pos - divide(pos, rows) * rows + 1, 0)
    ask_ref[...] = (place + wanted * (2 * rows)).reshape(peers, 1, rows)
    key_ref[...] = key
    local_ref[...] = jnp.where(live & here, row, -1)
    span_ref[0] = before
    span_ref[1] = total


def plan_kernel(
    peers, degree, features_hbm, weight_hbm, later_hbm, key_ref, local_ref, span_ref,
    near_ref, far_ref, order_ref, own_ref, features_ref, later_ref, held, sems,
):
    taken = pltpu.make_async_copy(features_hbm, features_ref, sems.at[1])
    later = pltpu.make_async_copy(later_hbm.at[pl.ds(0, later_ref.shape[0])], later_ref, sems.at[2])
    copies = fetches(weight_hbm, held, sems.at[pl.ds(0, 1)])
    for copy in (taken, *copies, later):
        copy.start()
    rows = features_ref.shape[0]
    local = local_ref[...]
    node = iota((rows, rows), 0)
    near = jnp.zeros((rows, rows), F32)
    for s in range(degree):
        near += bits(local[s : s + 1] == node)
    near = near.T.astype(BF16)
    near_ref[...] = near
    before, total = span_ref[0], span_ref[1]
    far = [bits((before <= k) & (k < before + total)).astype(BF16) for k in range(CAP)]
    far = jnp.concatenate(far, axis=0)
    size = peers * CAP
    line = iota((size, size), 0)
    peer = divide(line, CAP)
    order = bits(iota((size, size), 1) == (line - peer * CAP) * peers + peer).astype(BF16)
    order_ref[...] = order
    far_ref[:, :size] = dot(order, far).T.astype(BF16)
    live = bits((local >= 0) | (key_ref[...] >= 0))
    count = jnp.broadcast_to(jnp.sum(live, axis=0, keepdims=True), (rows, rows)).T.astype(BF16)
    far_ref[:, size:] = count[:, : far_ref.shape[1] - size]
    taken.wait()
    own_ref[...] = dot_fetched(features_ref[...], held, copies)
    later.wait()


def store_rows(reply_ref, rows):
    peers, pairs, two, width = reply_ref.shape
    reply_ref[...] = rows.reshape(peers, pairs, two, width)


def load_rows(answer_ref):
    peers, pairs, two, width = answer_ref.shape
    return answer_ref[...].reshape(peers * pairs * two, width)


def serve_kernel(asked_ref, order_ref, source_ref, reply_ref, pick_ref):
    peers, _, rows = asked_ref.shape
    asked = asked_ref[...].reshape(peers, rows)
    wanted = divide(asked, 2 * rows)
    lane = iota((peers, rows), 1)
    picks = [bits(wanted[:, k : k + 1] == lane).astype(BF16) for k in range(CAP)]
    pick = dot(order_ref[...], jnp.concatenate(picks, axis=0)).astype(BF16)
    pick_ref[...] = pick
    store_rows(reply_ref, dot(pick, source_ref[...]).astype(BF16))


def mean_product(weight_ref, table_ref, near_ref, answer_ref, far_ref, own_ref):
    answer = load_rows(answer_ref)
    size = answer.shape[0]
    summed = dot(near_ref[...], table_ref[...]) + dot(far_ref[:, :size], answer)
    mean = (summed / far_ref[:, size : size + 1].astype(F32)).astype(BF16)
    return own_ref[...] + dot(mean, weight_ref[...])


def layer_one_kernel(
    weight_ref, features_ref, near_ref, answer_ref, far_ref, own_ref, pick_ref, hidden_ref, reply_ref
):
    hidden = mean_product(weight_ref, features_ref, near_ref, answer_ref, far_ref, own_ref)
    hidden = jnp.maximum(hidden, 0.0).astype(BF16)
    hidden_ref[...] = hidden
    store_rows(reply_ref, dot(pick_ref[...], hidden).astype(BF16))


def own_two_kernel(
    members, weight_hbm, later_hbm, pos_hbm, hidden_ref, near_ref, far_ref, asked_ref,
    own_ref, near_moved_ref, far_moved_ref, place_ref, later_ref, held, pos_ref, sems,
):
    copies = fetches(weight_hbm, held, sems.at[pl.ds(0, 1)])
    later = pltpu.make_async_copy(later_hbm.at[pl.ds(0, later_ref.shape[0])], later_ref, sems.at[1])
    taken = pltpu.make_async_copy(pos_hbm, pos_ref, sems.at[2])
    for copy in (taken, *copies, later):
        copy.start()
    rows = hidden_ref.shape[0]
    capacity = 2 * rows // members
    me = lax.axis_index("dev")
    first = lax.axis_index("grp") * members
    line = iota((rows, rows), 0)
    step = divide(line, capacity)
    rank = line - step * capacity
    target = me + 2 * step
    target = jnp.where(target >= members, target - members, target)
    taken.wait()
    goes = target == divide(pos_ref[...], rows) - first
    prefix = earlier(rows)
    before = dot(bits(goes).astype(BF16), prefix).astype(I32)
    move = bits(goes & (before == rank)).astype(BF16)
    hidden = hidden_ref[...]
    near_moved_ref[...] = dot(move, near_ref[...]).astype(BF16)
    far_moved_ref[...] = dot(move, far_ref[...]).astype(BF16)
    own_ref[...] = dot_fetched(dot(move, hidden).astype(BF16), held, copies)
    place = jnp.zeros((rows, rows), F32)
    for q in range(members // 2):
        source = me - 2 * q
        source = first + jnp.where(source < 0, source + members, source)
        sent = asked_ref[source] & (2 * rows - 1)
        valid = jnp.broadcast_to(sent > 0, (rows, rows))
        before = dot(bits(valid).astype(BF16), prefix).astype(I32)
        lands = bits(sent - 1 == line).astype(BF16)
        comes = bits(valid & (step == q) & (before == rank)).astype(BF16)
        place += dot_lanes(lands, comes)
    place_ref[...] = place.astype(BF16)
    later.wait()


def layer_two_kernel(weight_ref, hidden_ref, near_ref, answer_ref, far_ref, own_ref, *final_refs):
    final = mean_product(weight_ref, hidden_ref, near_ref, answer_ref, far_ref, own_ref).astype(BF16)
    capacity = final_refs[0].shape[0]
    for q, ref in enumerate(final_refs):
        ref[...] = final[q * capacity : (q + 1) * capacity]


def scatter_kernel(place_ref, *refs):
    out_ref = refs[-1]
    arrived = jnp.concatenate([ref[...] for ref in refs[:-1]], axis=0)
    out_ref[...] = dot(place_ref[...], arrived).astype(BF16)


def body(features, neighbours, neighbour_mask, layer2_position, self_weight1, neigh_weight1, self_weight2, neigh_weight2):
    rows, degree = neighbours.shape
    members = lax.axis_size("dev")
    peers = lax.axis_size("grp") * members
    width_in, width = self_weight1.shape
    steps = members // 2
    capacity = rows // steps
    size = peers * CAP
    shape = jax.ShapeDtypeStruct
    copies = pltpu.SemaphoreType.DMA

    pos = layer2_position.reshape(1, rows)
    ask, key, local, span = call(
        functools.partial(ask_kernel, members, peers),
        (
            shape((peers, 1, rows), I32),
            shape((degree, rows), I32),
            shape((degree, rows), I32),
            shape((2, peers, rows), I32),
        ),
        (neighbours.T, neighbour_mask.T, pos),
        (),
        [pltpu.VMEM((degree, rows), I32), pltpu.VMEM((degree, rows), I32), pltpu.VMEM((1, rows), I32), copies((3,))],
        2 * peers * rows * rows,
        "ask",
    )
    asked = lax.all_to_all(ask, BOTH, 0, 0, tiled=True)
    near, far, order, own_one, features, weight = call(
        functools.partial(plan_kernel, peers, degree),
        (
            shape((rows, rows), BF16),
            shape((rows, size + 8), BF16),
            shape((size, size), BF16),
            shape((rows, width), F32),
            shape((rows, width_in), BF16),
            shape((width_in, width), BF16),
        ),
        (features, self_weight1, neigh_weight1),
        (key, local, span),
        [pltpu.VMEM((width_in, width), BF16), copies((3,))],
        2 * rows * width_in * (rows + width),
        "plan",
        limit=40 << 20,
    )
    reply, pick = call(
        serve_kernel,
        (shape((peers, CAP // 2, 2, width_in), BF16), shape((size, rows), BF16)),
        (),
        (asked, order, features),
        [],
        2 * size * rows * width_in,
        "serve",
    )
    answer = lax.all_to_all(reply, BOTH, 0, 0, tiled=True)
    hidden, reply_two = call(
        layer_one_kernel,
        (shape((rows, width), BF16), shape((peers, CAP // 2, 2, width), BF16)),
        (),
        (weight, features, near, answer, far, own_one, pick),
        [],
        2 * rows * width_in * (size + width) + 2 * size * rows * width,
        "layer_one",
    )
    answer_two = lax.all_to_all(reply_two, BOTH, 0, 0, tiled=True)
    own_two, near_moved, far_moved, place, weight = call(
        functools.partial(own_two_kernel, members),
        (
            shape((rows, width), F32),
            shape((rows, rows), BF16),
            shape((rows, size + 8), BF16),
            shape((rows, rows), BF16),
            shape((width, width), BF16),
        ),
        (self_weight2, neigh_weight2, pos),
        (hidden, near, far, asked),
        [pltpu.VMEM((width, width), BF16), pltpu.VMEM((1, rows), I32), copies((3,))],
        2 * rows * width * (2 * rows + width),
        "own_two",
    )
    finals = call(
        layer_two_kernel,
        tuple(shape((capacity, width), BF16) for _ in range(steps)),
        (),
        (weight, hidden, near_moved, answer_two, far_moved, own_two),
        [],
        2 * rows * width * (size + width),
        "layer_two",
    )
    arrived = [finals[0]]
    for q in range(1, steps):
        arrived.append(lax.ppermute(finals[q], "dev", [(i, (i + 2 * q) % members) for i in range(members)]))
    return call(
        scatter_kernel,
        shape((rows, width), BF16),
        (),
        (place, *arrived),
        [],
        2 * rows * rows * width,
        "scatter",
    )


def solution(mesh):
    return jax.shard_map(
        body,
        mesh=mesh,
        in_specs=(
            P(BOTH, None),
            P(BOTH, None),
            P(BOTH, None),
            P(BOTH),
            P(),
            P(),
            P(),
            P(),
        ),
        out_specs=P(BOTH, None),
        check_vma=False,
    )
```

```python
import functools

import jax
import jax.numpy as jnp
from jax import lax
from jax.experimental import pallas as pl
from jax.experimental.pallas import tpu as pltpu
from jax.sharding import PartitionSpec as P

CAP = 6
BOTH = ("grp", "dev")
F32 = jnp.float32
BF16 = jnp.bfloat16
I32 = jnp.int32


def divide(values, by):
    if by & (by - 1) == 0:
        return values >> (by.bit_length() - 1)
    return (values * (-(-(1 << 16) // by))) >> 16


def iota(shape, dim):
    return lax.broadcasted_iota(I32, shape, dim)


def bits(condition):
    return jnp.where(condition, 1.0, 0.0)


def earlier(count):
    return bits(iota((count, count), 0) < iota((count, count), 1)).astype(BF16)


def dot(left, right):
    return jnp.dot(left, right, preferred_element_type=F32)


def dot_lanes(left, right):
    return lax.dot_general(left, right, (((1,), (1,)), ((), ())), preferred_element_type=F32)


def near_by(n):
    return [pl.BlockSpec(memory_space=pltpu.VMEM)] * n


def far_off(n):
    return [pl.BlockSpec(memory_space=pltpu.HBM)] * n


def call(kernel, outs, remote, operands, scratch, flops, name, limit=24 << 20, away=0):
    single = not isinstance(outs, tuple)
    leaves = (outs,) if single else outs
    moved = sum(a.size * a.dtype.itemsize for a in (*remote, *operands, *leaves))
    return pl.pallas_call(
        kernel,
        out_shape=outs if single else (*(pltpu.HBM(a.shape, a.dtype) for a in leaves[:away]), *leaves[away:]),
        in_specs=far_off(len(remote)) + near_by(len(operands)),
        out_specs=near_by(1)[0] if single else far_off(away) + near_by(len(leaves) - away),
        scratch_shapes=scratch,
        compiler_params=pltpu.CompilerParams(vmem_limit_bytes=limit),
        cost_estimate=pl.CostEstimate(flops=flops, bytes_accessed=moved, transcendentals=0),
        name=name,
    )(*(pltpu.with_memory_space_constraint(a, pltpu.HBM) for a in remote), *operands)


def fetches(weight_ref, held, sems):
    pieces = sems.shape[0]
    depth = weight_ref.shape[0] // pieces
    return [
        pltpu.make_async_copy(
            weight_ref.at[pl.ds(i * depth, depth)], held.at[pl.ds(i * depth, depth)], sems.at[i]
        )
        for i in range(pieces)
    ]


def dot_fetched(left, held, copies):
    depth = held.shape[0] // len(copies)
    result = None
    for i, copy in enumerate(copies):
        copy.wait()
        part = dot(left[:, i * depth : (i + 1) * depth], held[i * depth : (i + 1) * depth])
        result = part if result is None else result + part
    return result


def ask_kernel(members, peers, ids_hbm, mask_hbm, pos_hbm, ask_ref, key_ref, local_ref, span_ref, ids, mask, pos_ref, sems):
    degree, rows = ids.shape
    copies = [
        pltpu.make_async_copy(ids_hbm, ids, sems.at[0]),
        pltpu.make_async_copy(mask_hbm, mask, sems.at[1]),
        pltpu.make_async_copy(pos_hbm, pos_ref, sems.at[2]),
    ]
    for copy in copies:
        copy.start()
    own = lax.axis_index("grp") * members + lax.axis_index("dev")
    peer = iota((peers, rows), 0)
    prefix = earlier(rows)
    for copy in copies:
        copy.wait()
    slots = jnp.where(mask[...] > 0, ids[...], -1)
    owner = divide(jnp.maximum(slots, 0), rows)
    row = slots - owner * rows
    live = slots >= 0
    here = owner == own
    key = jnp.where(live & jnp.logical_not(here), owner, -1)
    half = CAP // 2
    width = (rows - 1).bit_length()
    top = width * (half - 1)
    low = jnp.zeros((peers, rows), I32)
    high = jnp.zeros((peers, rows), I32)
    total = jnp.zeros((peers, rows), I32)
    for s in range(degree):
        hit = key[s : s + 1] == peer
        high = jnp.where(hit, (high << width) | (low >> top), high)
        low = jnp.where(hit, ((low & ((1 << top) - 1)) << width) | row[s : s + 1], low)
        total += jnp.where(hit, 1, 0)
    before = dot(total.astype(F32).astype(BF16), prefix).astype(I32)
    packed = [jnp.where(before == 0, low, 0), jnp.where(before == 0, high, jnp.where(before == half, low, 0))]
    for k in range(1, half):
        shift, rest = width * k, width * (half - k)
        inside = before == k
        packed[0] = jnp.where(inside, (low & ((1 << rest) - 1)) << shift, packed[0])
        packed[1] = jnp.where(inside, (high << shift) | (low >> rest), packed[1])
        packed[1] = jnp.where(before == half + k, low << shift, packed[1])
    lane = iota((peers, rows), 1)
    wanted = jnp.zeros((peers, rows), I32)
    for w, word in enumerate(packed):
        word = jnp.broadcast_to(jnp.sum(word.astype(F32), axis=1, keepdims=True).astype(I32), (peers, rows))
        for k in range(half):
            wanted = jnp.where(lane == w * half + k, (word >> (width * k)) & ((1 << width) - 1), wanted)
    pos = pos_ref[...]
    place = jnp.where(divide(pos, rows) == peer, pos - divide(pos, rows) * rows + 1, 0)
    ask_ref[...] = (place + wanted * (2 * rows)).reshape(peers, 1, rows)
    key_ref[...] = key
    local_ref[...] = jnp.where(live & here, row, -1)
    span_ref[0] = before
    span_ref[1] = total


def plan_kernel(
    peers, degree, features_hbm, key_ref, local_ref, span_ref, near_ref, far_ref, order_ref, features_ref, sems
):
    taken = pltpu.make_async_copy(features_hbm, features_ref, sems.at[0])
    taken.start()
    rows = features_ref.shape[0]
    local = local_ref[...]
    node = iota((rows, rows), 0)
    near = jnp.zeros((rows, rows), F32)
    for s in range(degree):
        near += bits(local[s : s + 1] == node)
    near = near.T.astype(BF16)
    near_ref[...] = near
    before, total = span_ref[0], span_ref[1]
    far = [bits((before <= k) & (k < before + total)).astype(BF16) for k in range(CAP)]
    far = jnp.concatenate(far, axis=0)
    size = peers * CAP
    line = iota((size, size), 0)
    peer = divide(line, CAP)
    order = bits(iota((size, size), 1) == (line - peer * CAP) * peers + peer).astype(BF16)
    order_ref[...] = order
    far_ref[:, :size] = dot(order, far).T.astype(BF16)
    live = bits((local >= 0) | (key_ref[...] >= 0))
    count = jnp.broadcast_to(jnp.sum(live, axis=0, keepdims=True), (rows, rows)).T.astype(BF16)
    far_ref[:, size:] = count[:, : far_ref.shape[1] - size]
    taken.wait()


def store_rows(reply_ref, rows):
    peers, pairs, two, width = reply_ref.shape
    reply_ref[...] = rows.reshape(peers, pairs, two, width)


def load_rows(answer_ref):
    peers, pairs, two, width = answer_ref.shape
    return answer_ref[...].reshape(peers * pairs * two, width)


def serve_kernel(asked_ref, order_ref, source_ref, reply_ref, pick_ref):
    peers, _, rows = asked_ref.shape
    asked = asked_ref[...].reshape(peers, rows)
    wanted = divide(asked, 2 * rows)
    lane = iota((peers, rows), 1)
    picks = [bits(wanted[:, k : k + 1] == lane).astype(BF16) for k in range(CAP)]
    pick = dot(order_ref[...], jnp.concatenate(picks, axis=0)).astype(BF16)
    pick_ref[...] = pick
    store_rows(reply_ref, dot(pick, source_ref[...]).astype(BF16))


def mean_of(near_ref, own, far_ref, other):
    size = other.shape[0]
    summed = dot(near_ref[...], own) + dot(far_ref[:, :size], other)
    return (summed / far_ref[:, size : size + 1].astype(F32)).astype(BF16)


def layer_one_kernel(
    features_ref, near_ref, answer_ref, far_ref, pick_ref, answer_hbm, mean_hbm, reply_ref, mean_ref, sems
):
    kept = pltpu.make_async_copy(answer_ref, answer_hbm, sems.at[0])
    kept.start()
    mean = mean_of(near_ref, features_ref[...], far_ref, load_rows(answer_ref))
    mean_ref[...] = mean
    saved = pltpu.make_async_copy(mean_ref, mean_hbm, sems.at[1])
    saved.start()
    store_rows(reply_ref, dot(pick_ref[...], mean).astype(BF16))
    kept.wait()
    saved.wait()


def between_kernel(
    members, self_one_hbm, neigh_one_hbm, self_two_hbm, neigh_two_hbm, pos_hbm, features_hbm, answer_hbm, mean_hbm,
    near_ref, far_ref, asked_ref,
    final_hbm, hidden_ref, base_ref, near_moved_ref, far_moved_ref, place_ref, neigh_one_ref, later_ref,
    held_one, held_two, features_ref, answer_ref, mean_ref, final_ref, pos_ref, sems,
):
    copies = [
        pltpu.make_async_copy(pos_hbm, pos_ref, sems.at[0]),
        pltpu.make_async_copy(self_one_hbm, held_one, sems.at[1]),
        pltpu.make_async_copy(neigh_one_hbm, neigh_one_ref, sems.at[2]),
        pltpu.make_async_copy(self_two_hbm, held_two, sems.at[3]),
        pltpu.make_async_copy(neigh_two_hbm.at[pl.ds(0, later_ref.shape[0])], later_ref, sems.at[4]),
    ]
    inputs = [
        pltpu.make_async_copy(features_hbm, features_ref, sems.at[6]),
        pltpu.make_async_copy(answer_hbm, answer_ref, sems.at[7]),
        pltpu.make_async_copy(mean_hbm, mean_ref, sems.at[8]),
    ]
    for copy in (*inputs, *copies):
        copy.start()
    rows = features_ref.shape[0]
    capacity = 2 * rows // members
    me = lax.axis_index("dev")
    first = lax.axis_index("grp") * members
    line = iota((rows, rows), 0)
    step = divide(line, capacity)
    rank = line - step * capacity
    target = me + 2 * step
    target = jnp.where(target >= members, target - members, target)
    prefix = earlier(rows)
    copies[0].wait()
    goes = target == divide(pos_ref[...], rows) - first
    before = dot(bits(goes).astype(BF16), prefix).astype(I32)
    move = bits(goes & (before == rank)).astype(BF16)
    near_moved_ref[...] = dot(move, near_ref[...]).astype(BF16)
    far_moved_ref[...] = dot(move, far_ref[...]).astype(BF16)
    place = jnp.zeros((rows, rows), F32)
    for q in range(members // 2):
        source = me - 2 * q
        source = first + jnp.where(source < 0, source + members, source)
        sent = asked_ref[source] & (2 * rows - 1)
        valid = jnp.broadcast_to(sent > 0, (rows, rows))
        before = dot(bits(valid).astype(BF16), prefix).astype(I32)
        lands = bits(sent - 1 == line).astype(BF16)
        comes = bits(valid & (step == q) & (before == rank)).astype(BF16)
        place += dot_lanes(lands, comes)
    place_ref[...] = place.astype(BF16)
    for copy in (*inputs, copies[1]):
        copy.wait()
    own = dot(features_ref[...], held_one[...])
    base_ref[...] = dot(load_rows(answer_ref), held_one[...]).astype(BF16)
    copies[2].wait()
    hidden = jnp.maximum(own + dot(mean_ref[...], neigh_one_ref[...]), 0.0).astype(BF16)
    hidden_ref[...] = hidden
    moved = dot(move, hidden).astype(BF16)
    copies[3].wait()
    final_ref[...] = dot(moved, held_two[...])
    away = pltpu.make_async_copy(final_ref, final_hbm, sems.at[5])
    away.start()
    copies[4].wait()
    away.wait()


def layer_two_kernel(
    neigh_two_hbm, final_hbm, neigh_one_ref, ready_ref, base_ref, hidden_ref, near_ref, answer_ref, far_ref, *refs
):
    outs, held, final_ref, sems = refs[:-3], refs[-3], refs[-2], refs[-1]
    ready = ready_ref.shape[0]
    copies = fetches(neigh_two_hbm.at[pl.ds(ready, held.shape[0])], held, sems.at[pl.ds(0, sems.shape[0] - 1)])
    last = pltpu.make_async_copy(final_hbm, final_ref, sems.at[sems.shape[0] - 1])
    for copy in (*copies, last):
        copy.start()
    other = jnp.maximum(base_ref[...].astype(F32) + dot(load_rows(answer_ref), neigh_one_ref[...]), 0.0).astype(BF16)
    mean = mean_of(near_ref, hidden_ref[...], far_ref, other)
    final = dot(mean[:, :ready], ready_ref[...]) + dot_fetched(mean[:, ready:], held, copies)
    last.wait()
    final = (final + final_ref[...]).astype(BF16)
    capacity = outs[0].shape[0]
    for q, ref in enumerate(outs):
        ref[...] = final[q * capacity : (q + 1) * capacity]


def scatter_kernel(place_ref, *refs):
    out_ref = refs[-1]
    arrived = jnp.concatenate([ref[...] for ref in refs[:-1]], axis=0)
    out_ref[...] = dot(place_ref[...], arrived).astype(BF16)


def body(features, neighbours, neighbour_mask, layer2_position, self_weight1, neigh_weight1, self_weight2, neigh_weight2):
    rows, degree = neighbours.shape
    members = lax.axis_size("dev")
    peers = lax.axis_size("grp") * members
    width_in, width = self_weight1.shape
    steps = members // 2
    capacity = rows // steps
    size = peers * CAP
    early = width // 4
    shape = jax.ShapeDtypeStruct
    copies = pltpu.SemaphoreType.DMA

    pos = layer2_position.reshape(1, rows)
    ask, key, local, span = call(
        functools.partial(ask_kernel, members, peers),
        (
            shape((peers, 1, rows), I32),
            shape((degree, rows), I32),
            shape((degree, rows), I32),
            shape((2, peers, rows), I32),
        ),
        (neighbours.T, neighbour_mask.T, pos),
        (),
        [pltpu.VMEM((degree, rows), I32), pltpu.VMEM((degree, rows), I32), pltpu.VMEM((1, rows), I32), copies((3,))],
        2 * peers * rows * rows,
        "ask",
    )
    asked = lax.all_to_all(ask, BOTH, 0, 0, tiled=True)
    near, far, order, table = call(
        functools.partial(plan_kernel, peers, degree),
        (
            shape((rows, rows), BF16),
            shape((rows, size + 8), BF16),
            shape((size, size), BF16),
            shape((rows, width_in), BF16),
        ),
        (features,),
        (key, local, span),
        [copies((1,))],
        2 * size * size * rows,
        "plan",
        limit=40 << 20,
    )
    reply, pick = call(
        serve_kernel,
        (shape((peers, CAP // 2, 2, width_in), BF16), shape((size, rows), BF16)),
        (),
        (asked, order, table),
        [],
        2 * size * rows * width_in,
        "serve",
    )
    answer = lax.all_to_all(reply, BOTH, 0, 0, tiled=True)
    kept, mean, reply_two = call(
        layer_one_kernel,
        (
            shape((peers, CAP // 2, 2, width_in), BF16),
            shape((rows, width_in), BF16),
            shape((peers, CAP // 2, 2, width_in), BF16),
        ),
        (),
        (table, near, answer, far, pick),
        [pltpu.VMEM((rows, width_in), BF16), copies((2,))],
        2 * rows * width_in * (size + rows) + 2 * size * rows * width_in,
        "layer_one",
        away=2,
    )
    answer_two = lax.all_to_all(reply_two, BOTH, 0, 0, tiled=True)
    final, hidden, base, near_moved, far_moved, place, weight, ready = call(
        functools.partial(between_kernel, members),
        (
            shape((rows, width), F32),
            shape((rows, width), BF16),
            shape((size, width), BF16),
            shape((rows, rows), BF16),
            shape((rows, size + 8), BF16),
            shape((rows, rows), BF16),
            shape((width_in, width), BF16),
            shape((early, width), BF16),
        ),
        (self_weight1, neigh_weight1, self_weight2, neigh_weight2, pos, features, kept, mean),
        (near, far, asked),
        [
            pltpu.VMEM((width_in, width), BF16),
            pltpu.VMEM((width, width), BF16),
            pltpu.VMEM((rows, width_in), BF16),
            pltpu.VMEM((peers, CAP // 2, 2, width_in), BF16),
            pltpu.VMEM((rows, width_in), BF16),
            pltpu.VMEM((rows, width), F32),
            pltpu.VMEM((1, rows), I32),
            copies((9,)),
        ],
        2 * width * (rows * (2 * width_in + rows + width) + size * width_in),
        "between",
        limit=48 << 20,
        away=1,
    )
    finals = call(
        layer_two_kernel,
        tuple(shape((capacity, width), BF16) for _ in range(steps)),
        (neigh_weight2, final),
        (weight, ready, base, hidden, near_moved, answer_two, far_moved),
        [pltpu.VMEM((width - early, width), BF16), pltpu.VMEM((rows, width), F32), copies((3,))],
        2 * width * (size * width_in + rows * (size + rows + width)),
        "layer_two",
        limit=48 << 20,
    )
    arrived = [finals[0]]
    for q in range(1, steps):
        arrived.append(lax.ppermute(finals[q], "dev", [(i, (i + 2 * q) % members) for i in range(members)]))
    return call(
        scatter_kernel,
        shape((rows, width), BF16),
        (),
        (place, *arrived),
        [],
        2 * rows * rows * width,
        "scatter",
    )


def solution(mesh):
    return jax.shard_map(
        body,
        mesh=mesh,
        in_specs=(
            P(BOTH, None),
            P(BOTH, None),
            P(BOTH, None),
            P(BOTH),
            P(),
            P(),
            P(),
            P(),
        ),
        out_specs=P(BOTH, None),
        check_vma=False,
    )
```

```python
import functools

import jax
import jax.numpy as jnp
from jax import lax
from jax.experimental import pallas as pl
from jax.experimental.pallas import tpu as pltpu
from jax.sharding import PartitionSpec as P

CAP = 6
BOTH = ("grp", "dev")
F32 = jnp.float32
BF16 = jnp.bfloat16
I32 = jnp.int32


def divide(values, by):
    if by & (by - 1) == 0:
        return values >> (by.bit_length() - 1)
    return (values * (-(-(1 << 16) // by))) >> 16


def iota(shape, dim):
    return lax.broadcasted_iota(I32, shape, dim)


def bits(condition):
    return jnp.where(condition, 1.0, 0.0)


def earlier(count):
    return bits(iota((count, count), 0) < iota((count, count), 1)).astype(BF16)


def dot(left, right):
    return jnp.dot(left, right, preferred_element_type=F32)


def dot_lanes(left, right):
    return lax.dot_general(left, right, (((1,), (1,)), ((), ())), preferred_element_type=F32)


def near_by(n):
    return [pl.BlockSpec(memory_space=pltpu.VMEM)] * n


def far_off(n):
    return [pl.BlockSpec(memory_space=pltpu.HBM)] * n


def call(kernel, outs, remote, operands, scratch, flops, name, limit=24 << 20, away=0):
    single = not isinstance(outs, tuple)
    leaves = (outs,) if single else outs
    moved = sum(a.size * a.dtype.itemsize for a in (*remote, *operands, *leaves))
    return pl.pallas_call(
        kernel,
        out_shape=outs if single else (*(pltpu.HBM(a.shape, a.dtype) for a in leaves[:away]), *leaves[away:]),
        in_specs=far_off(len(remote)) + near_by(len(operands)),
        out_specs=near_by(1)[0] if single else far_off(away) + near_by(len(leaves) - away),
        scratch_shapes=scratch,
        compiler_params=pltpu.CompilerParams(vmem_limit_bytes=limit),
        cost_estimate=pl.CostEstimate(flops=flops, bytes_accessed=moved, transcendentals=0),
        name=name,
    )(*(pltpu.with_memory_space_constraint(a, pltpu.HBM) for a in remote), *operands)


def fetches(weight_ref, held, sems):
    pieces = sems.shape[0]
    depth = weight_ref.shape[0] // pieces
    return [
        pltpu.make_async_copy(
            weight_ref.at[pl.ds(i * depth, depth)], held.at[pl.ds(i * depth, depth)], sems.at[i]
        )
        for i in range(pieces)
    ]


def dot_fetched(left, held, copies):
    depth = held.shape[0] // len(copies)
    result = None
    for i, copy in enumerate(copies):
        copy.wait()
        part = dot(left[:, i * depth : (i + 1) * depth], held[i * depth : (i + 1) * depth])
        result = part if result is None else result + part
    return result


def ask_kernel(members, peers, ids_hbm, mask_hbm, pos_hbm, ask_ref, key_ref, local_ref, span_ref, ids, mask, pos_ref, sems):
    degree, rows = ids.shape
    copies = [
        pltpu.make_async_copy(ids_hbm, ids, sems.at[0]),
        pltpu.make_async_copy(mask_hbm, mask, sems.at[1]),
        pltpu.make_async_copy(pos_hbm, pos_ref, sems.at[2]),
    ]
    for copy in copies:
        copy.start()
    own = lax.axis_index("grp") * members + lax.axis_index("dev")
    peer = iota((peers, rows), 0)
    prefix = earlier(rows)
    for copy in copies:
        copy.wait()
    slots = jnp.where(mask[...] > 0, ids[...], -1)
    owner = divide(jnp.maximum(slots, 0), rows)
    row = slots - owner * rows
    live = slots >= 0
    here = owner == own
    key = jnp.where(live & jnp.logical_not(here), owner, -1)
    half = CAP // 2
    width = (rows - 1).bit_length()
    top = width * (half - 1)
    low = jnp.zeros((peers, rows), I32)
    high = jnp.zeros((peers, rows), I32)
    total = jnp.zeros((peers, rows), I32)
    for s in range(degree):
        hit = key[s : s + 1] == peer
        high = jnp.where(hit, (high << width) | (low >> top), high)
        low = jnp.where(hit, ((low & ((1 << top) - 1)) << width) | row[s : s + 1], low)
        total += jnp.where(hit, 1, 0)
    before = dot(total.astype(F32).astype(BF16), prefix).astype(I32)
    packed = [jnp.where(before == 0, low, 0), jnp.where(before == 0, high, jnp.where(before == half, low, 0))]
    for k in range(1, half):
        shift, rest = width * k, width * (half - k)
        inside = before == k
        packed[0] = jnp.where(inside, (low & ((1 << rest) - 1)) << shift, packed[0])
        packed[1] = jnp.where(inside, (high << shift) | (low >> rest), packed[1])
        packed[1] = jnp.where(before == half + k, low << shift, packed[1])
    lane = iota((peers, rows), 1)
    wanted = jnp.zeros((peers, rows), I32)
    for w, word in enumerate(packed):
        word = jnp.broadcast_to(jnp.sum(word.astype(F32), axis=1, keepdims=True).astype(I32), (peers, rows))
        for k in range(half):
            wanted = jnp.where(lane == w * half + k, (word >> (width * k)) & ((1 << width) - 1), wanted)
    pos = pos_ref[...]
    place = jnp.where(divide(pos, rows) == peer, pos - divide(pos, rows) * rows + 1, 0)
    ask_ref[...] = (place + wanted * (2 * rows)).reshape(peers, 1, rows)
    key_ref[...] = key
    local_ref[...] = jnp.where(live & here, row, -1)
    span_ref[0] = before
    span_ref[1] = total


def plan_kernel(
    peers, degree, features_hbm, key_ref, local_ref, span_ref, near_ref, far_ref, order_ref, features_ref, sems
):
    taken = pltpu.make_async_copy(features_hbm, features_ref, sems.at[0])
    taken.start()
    rows = features_ref.shape[0]
    local = local_ref[...]
    node = iota((rows, rows), 0)
    near = jnp.zeros((rows, rows), F32)
    for s in range(degree):
        near += bits(local[s : s + 1] == node)
    near = near.T.astype(BF16)
    near_ref[...] = near
    before, total = span_ref[0], span_ref[1]
    far = [bits((before <= k) & (k < before + total)).astype(BF16) for k in range(CAP)]
    far = jnp.concatenate(far, axis=0)
    size = peers * CAP
    line = iota((size, size), 0)
    peer = divide(line, CAP)
    order = bits(iota((size, size), 1) == (line - peer * CAP) * peers + peer).astype(BF16)
    order_ref[...] = order
    far_ref[:, :size] = dot(order, far).T.astype(BF16)
    live = bits((local >= 0) | (key_ref[...] >= 0))
    count = jnp.broadcast_to(jnp.sum(live, axis=0, keepdims=True), (rows, rows)).T.astype(BF16)
    far_ref[:, size:] = count[:, : far_ref.shape[1] - size]
    taken.wait()


def store_rows(reply_ref, rows):
    peers, pairs, two, width = reply_ref.shape
    reply_ref[...] = rows.reshape(peers, pairs, two, width)


def load_rows(answer_ref):
    peers, pairs, two, width = answer_ref.shape
    return answer_ref[...].reshape(peers * pairs * two, width)


def serve_kernel(asked_ref, order_ref, source_ref, reply_ref, pick_ref):
    peers, _, rows = asked_ref.shape
    asked = asked_ref[...].reshape(peers, rows)
    wanted = divide(asked, 2 * rows)
    lane = iota((peers, rows), 1)
    picks = [bits(wanted[:, k : k + 1] == lane).astype(BF16) for k in range(CAP)]
    pick = dot(order_ref[...], jnp.concatenate(picks, axis=0)).astype(BF16)
    pick_ref[...] = pick
    store_rows(reply_ref, dot(pick, source_ref[...]).astype(BF16))


def over_count(summed, far):
    size = far.shape[1] - 8
    return (summed / far[:, size : size + 1].astype(F32)).astype(BF16)


def layer_one_kernel(
    features_ref, near_ref, answer_ref, far_ref, pick_ref, answer_hbm, mean_hbm, reply_ref, mean_ref, sems
):
    kept = pltpu.make_async_copy(answer_ref, answer_hbm, sems.at[0])
    kept.start()
    answer = load_rows(answer_ref)
    far = far_ref[...]
    mean = over_count(dot(near_ref[...], features_ref[...]) + dot(far[:, : answer.shape[0]], answer), far)
    mean_ref[...] = mean
    saved = pltpu.make_async_copy(mean_ref, mean_hbm, sems.at[1])
    saved.start()
    store_rows(reply_ref, dot(pick_ref[...], mean).astype(BF16))
    kept.wait()
    saved.wait()


def between_kernel(
    members, self_one_hbm, neigh_one_hbm, self_two_hbm, neigh_two_hbm, pos_hbm, features_hbm, answer_hbm, mean_hbm,
    near_ref, far_ref, asked_ref,
    final_hbm, place_hbm, base_ref, far_moved_ref, neigh_one_ref, ready_ref,
    held_one, held_two, rest, features_ref, answer_ref, mean_ref, final_ref, place_ref, pos_ref, sems,
):
    ready = ready_ref.shape[0]
    copies = [
        pltpu.make_async_copy(pos_hbm, pos_ref, sems.at[0]),
        pltpu.make_async_copy(self_one_hbm, held_one, sems.at[1]),
        pltpu.make_async_copy(neigh_one_hbm, neigh_one_ref, sems.at[2]),
        pltpu.make_async_copy(self_two_hbm, held_two, sems.at[3]),
        pltpu.make_async_copy(neigh_two_hbm.at[pl.ds(0, ready)], ready_ref, sems.at[4]),
        pltpu.make_async_copy(neigh_two_hbm.at[pl.ds(ready, rest.shape[0])], rest, sems.at[5]),
    ]
    inputs = [
        pltpu.make_async_copy(features_hbm, features_ref, sems.at[6]),
        pltpu.make_async_copy(answer_hbm, answer_ref, sems.at[7]),
        pltpu.make_async_copy(mean_hbm, mean_ref, sems.at[8]),
    ]
    for copy in (*inputs, *copies):
        copy.start()
    rows = features_ref.shape[0]
    capacity = 2 * rows // members
    me = lax.axis_index("dev")
    first = lax.axis_index("grp") * members
    line = iota((rows, rows), 0)
    step = divide(line, capacity)
    rank = line - step * capacity
    target = me + 2 * step
    target = jnp.where(target >= members, target - members, target)
    prefix = earlier(rows)
    copies[0].wait()
    goes = target == divide(pos_ref[...], rows) - first
    before = dot(bits(goes).astype(BF16), prefix).astype(I32)
    move = bits(goes & (before == rank)).astype(BF16)
    near = dot(move, near_ref[...]).astype(BF16)
    far = dot(move, far_ref[...]).astype(BF16)
    far_moved_ref[...] = far
    place = jnp.zeros((rows, rows), F32)
    for q in range(members // 2):
        source = me - 2 * q
        source = first + jnp.where(source < 0, source + members, source)
        sent = asked_ref[source] & (2 * rows - 1)
        valid = jnp.broadcast_to(sent > 0, (rows, rows))
        before = dot(bits(valid).astype(BF16), prefix).astype(I32)
        lands = bits(sent - 1 == line).astype(BF16)
        comes = bits(valid & (step == q) & (before == rank)).astype(BF16)
        place += dot_lanes(lands, comes)
    place_ref[...] = place.astype(BF16)
    placed = pltpu.make_async_copy(place_ref, place_hbm, sems.at[9])
    placed.start()
    for copy in (*inputs, copies[1]):
        copy.wait()
    own = dot(features_ref[...], held_one[...])
    base_ref[...] = dot(load_rows(answer_ref), held_one[...]).astype(BF16)
    copies[2].wait()
    hidden = jnp.maximum(own + dot(mean_ref[...], neigh_one_ref[...]), 0.0).astype(BF16)
    mean = over_count(dot(near, hidden), far)
    moved = dot(move, hidden).astype(BF16)
    copies[3].wait()
    final = dot(moved, held_two[...])
    copies[4].wait()
    final += dot(mean[:, :ready], ready_ref[...])
    copies[5].wait()
    final_ref[...] = final + dot(mean[:, ready:], rest[...])
    away = pltpu.make_async_copy(final_ref, final_hbm, sems.at[10])
    away.start()
    away.wait()
    placed.wait()


def layer_two_kernel(neigh_two_hbm, final_hbm, neigh_one_ref, ready_ref, base_ref, answer_ref, far_ref, *refs):
    outs, held, final_ref, sems = refs[:-3], refs[-3], refs[-2], refs[-1]
    ready = ready_ref.shape[0]
    pieces = sems.shape[0] - 1
    copies = fetches(neigh_two_hbm.at[pl.ds(ready, held.shape[0])], held, sems.at[pl.ds(0, pieces)])
    last = pltpu.make_async_copy(final_hbm, final_ref, sems.at[pieces])
    for copy in (*copies, last):
        copy.start()
    far = far_ref[...]
    other = jnp.maximum(base_ref[...].astype(F32) + dot(load_rows(answer_ref), neigh_one_ref[...]), 0.0).astype(BF16)
    mean = over_count(dot(far[:, : other.shape[0]], other), far)
    final = dot(mean[:, :ready], ready_ref[...]) + dot_fetched(mean[:, ready:], held, copies)
    last.wait()
    final = (final + final_ref[...]).astype(BF16)
    capacity = outs[0].shape[0]
    for q, ref in enumerate(outs):
        ref[...] = final[q * capacity : (q + 1) * capacity]


def scatter_kernel(place_ref, *refs):
    out_ref = refs[-1]
    arrived = jnp.concatenate([ref[...] for ref in refs[:-1]], axis=0)
    out_ref[...] = dot(place_ref[...], arrived).astype(BF16)


def body(features, neighbours, neighbour_mask, layer2_position, self_weight1, neigh_weight1, self_weight2, neigh_weight2):
    rows, degree = neighbours.shape
    members = lax.axis_size("dev")
    peers = lax.axis_size("grp") * members
    width_in, width = self_weight1.shape
    steps = members // 2
    capacity = rows // steps
    size = peers * CAP
    early = width // 2
    shape = jax.ShapeDtypeStruct
    copies = pltpu.SemaphoreType.DMA

    pos = layer2_position.reshape(1, rows)
    ask, key, local, span = call(
        functools.partial(ask_kernel, members, peers),
        (
            shape((peers, 1, rows), I32),
            shape((degree, rows), I32),
            shape((degree, rows), I32),
            shape((2, peers, rows), I32),
        ),
        (neighbours.T, neighbour_mask.T, pos),
        (),
        [pltpu.VMEM((degree, rows), I32), pltpu.VMEM((degree, rows), I32), pltpu.VMEM((1, rows), I32), copies((3,))],
        2 * peers * rows * rows,
        "ask",
    )
    asked = lax.all_to_all(ask, BOTH, 0, 0, tiled=True)
    near, far, order, table = call(
        functools.partial(plan_kernel, peers, degree),
        (
            shape((rows, rows), BF16),
            shape((rows, size + 8), BF16),
            shape((size, size), BF16),
            shape((rows, width_in), BF16),
        ),
        (features,),
        (key, local, span),
        [copies((1,))],
        2 * size * size * rows,
        "plan",
        limit=40 << 20,
    )
    reply, pick = call(
        serve_kernel,
        (shape((peers, CAP // 2, 2, width_in), BF16), shape((size, rows), BF16)),
        (),
        (asked, order, table),
        [],
        2 * size * rows * width_in,
        "serve",
    )
    answer = lax.all_to_all(reply, BOTH, 0, 0, tiled=True)
    kept, mean, reply_two = call(
        layer_one_kernel,
        (
            shape((peers, CAP // 2, 2, width_in), BF16),
            shape((rows, width_in), BF16),
            shape((peers, CAP // 2, 2, width_in), BF16),
        ),
        (),
        (table, near, answer, far, pick),
        [pltpu.VMEM((rows, width_in), BF16), copies((2,))],
        2 * rows * width_in * (size + rows) + 2 * size * rows * width_in,
        "layer_one",
        away=2,
    )
    answer_two = lax.all_to_all(reply_two, BOTH, 0, 0, tiled=True)
    final, place, base, far_moved, weight, ready = call(
        functools.partial(between_kernel, members),
        (
            shape((rows, width), F32),
            shape((rows, rows), BF16),
            shape((size, width), BF16),
            shape((rows, size + 8), BF16),
            shape((width_in, width), BF16),
            shape((early, width), BF16),
        ),
        (self_weight1, neigh_weight1, self_weight2, neigh_weight2, pos, features, kept, mean),
        (near, far, asked),
        [
            pltpu.VMEM((width_in, width), BF16),
            pltpu.VMEM((width, width), BF16),
            pltpu.VMEM((width - early, width), BF16),
            pltpu.VMEM((rows, width_in), BF16),
            pltpu.VMEM((peers, CAP // 2, 2, width_in), BF16),
            pltpu.VMEM((rows, width_in), BF16),
            pltpu.VMEM((rows, width), F32),
            pltpu.VMEM((rows, rows), BF16),
            pltpu.VMEM((1, rows), I32),
            copies((11,)),
        ],
        2 * width * (rows * (2 * width_in + rows + 2 * width) + size * width_in),
        "between",
        limit=48 << 20,
        away=2,
    )
    finals = call(
        layer_two_kernel,
        tuple(shape((capacity, width), BF16) for _ in range(steps)),
        (neigh_weight2, final),
        (weight, ready, base, answer_two, far_moved),
        [pltpu.VMEM((width - early, width), BF16), pltpu.VMEM((rows, width), F32), copies((3,))],
        2 * width * (size * width_in + rows * (size + width)),
        "layer_two",
        limit=48 << 20,
    )
    arrived = [finals[0]]
    for q in range(1, steps):
        arrived.append(lax.ppermute(finals[q], "dev", [(i, (i + 2 * q) % members) for i in range(members)]))
    return call(
        scatter_kernel,
        shape((rows, width), BF16),
        (),
        (place, *arrived),
        [],
        2 * rows * rows * width,
        "scatter",
    )


def solution(mesh):
    return jax.shard_map(
        body,
        mesh=mesh,
        in_specs=(
            P(BOTH, None),
            P(BOTH, None),
            P(BOTH, None),
            P(BOTH),
            P(),
            P(),
            P(),
            P(),
        ),
        out_specs=P(BOTH, None),
        check_vma=False,
    )
```

```python
import functools

import jax
import jax.numpy as jnp
from jax import lax
from jax.experimental import pallas as pl
from jax.experimental.pallas import tpu as pltpu
from jax.sharding import PartitionSpec as P

CAP = 6
BOTH = ("grp", "dev")
F32 = jnp.float32
BF16 = jnp.bfloat16
I32 = jnp.int32


def divide(values, by):
    if by & (by - 1) == 0:
        return values >> (by.bit_length() - 1)
    return (values * (-(-(1 << 16) // by))) >> 16


def iota(shape, dim):
    return lax.broadcasted_iota(I32, shape, dim)


def bits(condition):
    return jnp.where(condition, 1.0, 0.0)


def earlier(count):
    return bits(iota((count, count), 0) < iota((count, count), 1)).astype(BF16)


def dot(left, right):
    return jnp.dot(left, right, preferred_element_type=F32)


def dot_lanes(left, right):
    return lax.dot_general(left, right, (((1,), (1,)), ((), ())), preferred_element_type=F32)


def near_by(n):
    return [pl.BlockSpec(memory_space=pltpu.VMEM)] * n


def far_off(n):
    return [pl.BlockSpec(memory_space=pltpu.HBM)] * n


def call(kernel, outs, remote, operands, scratch, flops, name, limit=24 << 20, away=0):
    single = not isinstance(outs, tuple)
    leaves = (outs,) if single else outs
    moved = sum(a.size * a.dtype.itemsize for a in (*remote, *operands, *leaves))
    return pl.pallas_call(
        kernel,
        out_shape=outs if single else (*(pltpu.HBM(a.shape, a.dtype) for a in leaves[:away]), *leaves[away:]),
        in_specs=far_off(len(remote)) + near_by(len(operands)),
        out_specs=near_by(1)[0] if single else far_off(away) + near_by(len(leaves) - away),
        scratch_shapes=scratch,
        compiler_params=pltpu.CompilerParams(vmem_limit_bytes=limit),
        cost_estimate=pl.CostEstimate(flops=flops, bytes_accessed=moved, transcendentals=0),
        name=name,
    )(*(pltpu.with_memory_space_constraint(a, pltpu.HBM) for a in remote), *operands)


def fetches(weight_ref, held, sems):
    pieces = sems.shape[0]
    depth = weight_ref.shape[0] // pieces
    return [
        pltpu.make_async_copy(
            weight_ref.at[pl.ds(i * depth, depth)], held.at[pl.ds(i * depth, depth)], sems.at[i]
        )
        for i in range(pieces)
    ]


def dot_fetched(left, held, copies):
    depth = held.shape[0] // len(copies)
    result = None
    for i, copy in enumerate(copies):
        copy.wait()
        part = dot(left[:, i * depth : (i + 1) * depth], held[i * depth : (i + 1) * depth])
        result = part if result is None else result + part
    return result


def seat():
    member = lax.axis_index("dev")
    return lax.axis_index("grp"), member >> 1, member & 1


def wrap(value, size):
    value = jnp.where(value < 0, value + size, value)
    return jnp.where(value >= size, value - size, value)


def device_at(index, groups, members):
    group, height, core = seat()
    step = divide(index, 2 * groups)
    mate = index - step * 2 * groups
    height = wrap(height + step, members // 2)
    return ((mate >> 1) ^ group) * members + 2 * height + ((mate & 1) ^ core), group * members + 2 * height + core


def apart(device, members):
    group, height, core = seat()
    its_group = divide(device, members)
    member = device - its_group * members
    return wrap((member >> 1) - height, members // 2), its_group ^ group, (member & 1) ^ core


def ask_kernel(groups, members, ids_hbm, mask_hbm, pos_hbm, key_ref, local_ref, span_ref, *refs):
    ask_refs, (ids, mask, pos_ref, sems) = refs[:-4], refs[-4:]
    peers = groups * members
    degree, rows = ids.shape
    copies = [
        pltpu.make_async_copy(ids_hbm, ids, sems.at[0]),
        pltpu.make_async_copy(mask_hbm, mask, sems.at[1]),
        pltpu.make_async_copy(pos_hbm, pos_ref, sems.at[2]),
    ]
    for copy in copies:
        copy.start()
    own = lax.axis_index("grp") * members + lax.axis_index("dev")
    peer, new_home = device_at(iota((peers, rows), 0), groups, members)
    prefix = earlier(rows)
    for copy in copies:
        copy.wait()
    slots = jnp.where(mask[...] > 0, ids[...], -1)
    owner = divide(jnp.maximum(slots, 0), rows)
    row = slots - owner * rows
    live = slots >= 0
    here = owner == own
    key = jnp.where(live & jnp.logical_not(here), owner, -1)
    half = CAP // 2
    width = (rows - 1).bit_length()
    top = width * (half - 1)
    low = jnp.zeros((peers, rows), I32)
    high = jnp.zeros((peers, rows), I32)
    total = jnp.zeros((peers, rows), I32)
    for s in range(degree):
        hit = key[s : s + 1] == peer
        high = jnp.where(hit, (high << width) | (low >> top), high)
        low = jnp.where(hit, ((low & ((1 << top) - 1)) << width) | row[s : s + 1], low)
        total += jnp.where(hit, 1, 0)
    before = dot(total.astype(F32).astype(BF16), prefix).astype(I32)
    packed = [jnp.where(before == 0, low, 0), jnp.where(before == 0, high, jnp.where(before == half, low, 0))]
    for k in range(1, half):
        shift, rest = width * k, width * (half - k)
        inside = before == k
        packed[0] = jnp.where(inside, (low & ((1 << rest) - 1)) << shift, packed[0])
        packed[1] = jnp.where(inside, (high << shift) | (low >> rest), packed[1])
        packed[1] = jnp.where(before == half + k, low << shift, packed[1])
    lane = iota((peers, rows), 1)
    wanted = jnp.zeros((peers, rows), I32)
    for w, word in enumerate(packed):
        word = jnp.broadcast_to(jnp.sum(word.astype(F32), axis=1, keepdims=True).astype(I32), (peers, rows))
        for k in range(half):
            wanted = jnp.where(lane == w * half + k, (word >> (width * k)) & ((1 << width) - 1), wanted)
    pos = pos_ref[...]
    place = jnp.where(divide(pos, rows) == new_home, pos - divide(pos, rows) * rows + 1, 0)
    asks = place + wanted * (2 * rows)
    for q, ref in enumerate(ask_refs):
        ref[...] = asks[q * 2 * groups : (q + 1) * 2 * groups]
    key_ref[...] = key
    local_ref[...] = jnp.where(live & here, row, -1)
    span_ref[0] = before
    span_ref[1] = total


def plan_kernel(
    peers, degree, features_hbm, key_ref, local_ref, span_ref, near_ref, far_ref, order_ref, features_ref, sems
):
    taken = pltpu.make_async_copy(features_hbm, features_ref, sems.at[0])
    taken.start()
    rows = features_ref.shape[0]
    local = local_ref[...]
    node = iota((rows, rows), 0)
    near = jnp.zeros((rows, rows), F32)
    for s in range(degree):
        near += bits(local[s : s + 1] == node)
    near = near.T.astype(BF16)
    near_ref[...] = near
    before, total = span_ref[0], span_ref[1]
    far = [bits((before <= k) & (k < before + total)).astype(BF16) for k in range(CAP)]
    far = jnp.concatenate(far, axis=0)
    size = peers * CAP
    line = iota((size, size), 0)
    peer = divide(line, CAP)
    order = bits(iota((size, size), 1) == (line - peer * CAP) * peers + peer).astype(BF16)
    order_ref[...] = order
    far_ref[:, :size] = dot(order, far).T.astype(BF16)
    live = bits((local >= 0) | (key_ref[...] >= 0))
    count = jnp.broadcast_to(jnp.sum(live, axis=0, keepdims=True), (rows, rows)).T.astype(BF16)
    far_ref[:, size:] = count[:, : far_ref.shape[1] - size]
    taken.wait()


def store_rows(reply_ref, rows):
    peers, pairs, two, width = reply_ref.shape
    reply_ref[...] = rows.reshape(peers, pairs, two, width)


def load_rows(answer_ref):
    peers, pairs, two, width = answer_ref.shape
    return answer_ref[...].reshape(peers * pairs * two, width)


def picks_of(wanted, order):
    lane = iota(wanted.shape, 1)
    picks = [bits(wanted[:, k : k + 1] == lane).astype(BF16) for k in range(CAP)]
    return dot(order, jnp.concatenate(picks, axis=0)).astype(BF16)


def sort_kernel(groups, *refs):
    steps = len(refs) - groups
    asked = jnp.concatenate([ref[...] for ref in refs[:steps]], axis=0)
    peers, rows = asked.shape
    wanted = divide(asked, 2 * rows)
    line = iota((peers, peers), 0)
    mate = divide(line, steps)
    pick = bits(iota((peers, peers), 1) == (line - mate * steps) * 2 * groups + mate).astype(BF16)
    sorted_rows = dot(pick, wanted.astype(F32).astype(BF16)).astype(I32)
    for m, ref in enumerate(refs[steps:]):
        ref[...] = sorted_rows[m * 2 * steps : (m + 1) * 2 * steps]


def serve_kernel(groups, steps, order_ref, *refs):
    asked_refs, refs = refs[:steps], refs[steps:]
    table_refs, reply_refs = refs[: 2 * groups], refs[2 * groups :]
    asked = jnp.concatenate([ref[...] for ref in asked_refs], axis=0)
    pick = picks_of(divide(asked, 2 * asked.shape[1]), order_ref[...])
    line = divide(iota(pick.shape, 0), CAP)
    mate = line - divide(line, 2 * groups) * 2 * groups
    rows = None
    for m in range(groups):
        left = [jnp.where(mate == 2 * m + side, pick, jnp.zeros_like(pick)) for side in range(2)]
        table = jnp.concatenate([table_refs[2 * m][...], table_refs[2 * m + 1][...]], axis=0)
        part = dot(jnp.concatenate(left, axis=1), table)
        rows = part if rows is None else rows + part
    rows = rows.astype(BF16)
    block = rows.shape[0] // steps
    for q, ref in enumerate(reply_refs):
        ref[...] = rows[q * block : (q + 1) * block]


def pick_kernel(members, kept_ref, passed_ref, pick_ref):
    kept = kept_ref[...]
    peers = kept.shape[0]
    steps = members // 2
    half = divide(iota(kept.shape, 0), steps)
    wanted = jnp.where((half & 1) == 0, kept, passed_ref[...])
    size = peers * CAP
    line = iota((size, size), 0)
    device = divide(line, CAP)
    step, group, core = apart(device, members)
    row = (2 * group + core) * steps + wrap(-step, steps)
    order = bits(iota((size, size), 1) == (line - device * CAP) * peers + row).astype(BF16)
    pick_ref[...] = picks_of(wanted, order)


def over_count(summed, far):
    size = far.shape[1] - 8
    return (summed / far[:, size : size + 1].astype(F32)).astype(BF16)


def layer_one_kernel(features_ref, near_ref, far_ref, pick_ref, *refs):
    answer_refs, (answer_hbm, mean_hbm, reply_ref, kept, mean_ref, sems) = refs[:-6], refs[-6:]
    answer = jnp.concatenate([ref[...] for ref in answer_refs], axis=0)
    kept[...] = answer
    saves = [
        pltpu.make_async_copy(kept, answer_hbm, sems.at[0]),
        pltpu.make_async_copy(mean_ref, mean_hbm, sems.at[1]),
    ]
    saves[0].start()
    far = far_ref[...]
    mean = over_count(dot(near_ref[...], features_ref[...]) + dot(far[:, : answer.shape[0]], answer), far)
    mean_ref[...] = mean
    saves[1].start()
    store_rows(reply_ref, dot(pick_ref[...], mean).astype(BF16))
    for save in saves:
        save.wait()


def between_kernel(
    groups, members, self_one_hbm, neigh_one_hbm, self_two_hbm, neigh_two_hbm, pos_hbm, features_hbm, answer_hbm, mean_hbm,
    near_ref, far_ref, *refs,
):
    asked_refs, refs = refs[: members // 2], refs[members // 2 :]
    between_body(
        groups, members, self_one_hbm, neigh_one_hbm, self_two_hbm, neigh_two_hbm, pos_hbm, features_hbm, answer_hbm, mean_hbm,
        near_ref, far_ref, asked_refs, *refs,
    )


def between_body(
    groups, members, self_one_hbm, neigh_one_hbm, self_two_hbm, neigh_two_hbm, pos_hbm, features_hbm, answer_hbm, mean_hbm,
    near_ref, far_ref, asked_refs,
    final_hbm, place_hbm, base_ref, far_moved_ref, neigh_one_ref, ready_ref,
    held_one, held_two, rest, features_ref, answer_ref, mean_ref, final_ref, place_ref, pos_ref, sems,
):
    ready = ready_ref.shape[0]
    copies = [
        pltpu.make_async_copy(pos_hbm, pos_ref, sems.at[0]),
        pltpu.make_async_copy(self_one_hbm, held_one, sems.at[1]),
        pltpu.make_async_copy(neigh_one_hbm, neigh_one_ref, sems.at[2]),
        pltpu.make_async_copy(self_two_hbm, held_two, sems.at[3]),
        pltpu.make_async_copy(neigh_two_hbm.at[pl.ds(0, ready)], ready_ref, sems.at[4]),
        pltpu.make_async_copy(neigh_two_hbm.at[pl.ds(ready, rest.shape[0])], rest, sems.at[5]),
    ]
    inputs = [
        pltpu.make_async_copy(features_hbm, features_ref, sems.at[6]),
        pltpu.make_async_copy(answer_hbm, answer_ref, sems.at[7]),
        pltpu.make_async_copy(mean_hbm, mean_ref, sems.at[8]),
    ]
    for copy in (*inputs, *copies):
        copy.start()
    rows = features_ref.shape[0]
    capacity = 2 * rows // members
    me = lax.axis_index("dev")
    first = lax.axis_index("grp") * members
    line = iota((rows, rows), 0)
    step = divide(line, capacity)
    rank = line - step * capacity
    target = me + 2 * step
    target = jnp.where(target >= members, target - members, target)
    prefix = earlier(rows)
    copies[0].wait()
    goes = target == divide(pos_ref[...], rows) - first
    before = dot(bits(goes).astype(BF16), prefix).astype(I32)
    move = bits(goes & (before == rank)).astype(BF16)
    near = dot(move, near_ref[...]).astype(BF16)
    size = base_ref.shape[0]
    slot = iota((size, size), 0)
    device = divide(slot, CAP)
    up, group, core = apart(device, members)
    came = ((up * groups + group) * 2 + core) * CAP + slot - device * CAP
    resort = bits(iota((size, size), 1) == came).astype(BF16)
    far = dot(move, far_ref[...]).astype(BF16)
    far_moved_ref[:, size:] = far[:, size:]
    far_moved_ref[:, :size] = dot_lanes(far[:, :size], resort).astype(BF16)
    place = jnp.zeros((rows, rows), F32)
    for q in range(members // 2):
        sent = asked_refs[q][0:1] & (2 * rows - 1)
        valid = jnp.broadcast_to(sent > 0, (rows, rows))
        before = dot(bits(valid).astype(BF16), prefix).astype(I32)
        lands = bits(sent - 1 == line).astype(BF16)
        comes = bits(valid & (step == q) & (before == rank)).astype(BF16)
        place += dot_lanes(lands, comes)
    place_ref[...] = place.astype(BF16)
    placed = pltpu.make_async_copy(place_ref, place_hbm, sems.at[9])
    placed.start()
    for copy in (*inputs, copies[1]):
        copy.wait()
    own = dot(features_ref[...], held_one[...])
    base_ref[...] = dot(dot(resort, answer_ref[...]).astype(BF16), held_one[...]).astype(BF16)
    copies[2].wait()
    hidden = jnp.maximum(own + dot(mean_ref[...], neigh_one_ref[...]), 0.0).astype(BF16)
    mean = over_count(dot(near, hidden), far)
    moved = dot(move, hidden).astype(BF16)
    copies[3].wait()
    final = dot(moved, held_two[...])
    copies[4].wait()
    final += dot(mean[:, :ready], ready_ref[...])
    copies[5].wait()
    final_ref[...] = final + dot(mean[:, ready:], rest[...])
    away = pltpu.make_async_copy(final_ref, final_hbm, sems.at[10])
    away.start()
    away.wait()
    placed.wait()


def layer_two_kernel(neigh_two_hbm, final_hbm, neigh_one_ref, ready_ref, base_ref, answer_ref, far_ref, *refs):
    outs, held, final_ref, sems = refs[:-3], refs[-3], refs[-2], refs[-1]
    ready = ready_ref.shape[0]
    pieces = sems.shape[0] - 1
    copies = fetches(neigh_two_hbm.at[pl.ds(ready, held.shape[0])], held, sems.at[pl.ds(0, pieces)])
    last = pltpu.make_async_copy(final_hbm, final_ref, sems.at[pieces])
    for copy in (*copies, last):
        copy.start()
    far = far_ref[...]
    other = jnp.maximum(base_ref[...].astype(F32) + dot(load_rows(answer_ref), neigh_one_ref[...]), 0.0).astype(BF16)
    mean = over_count(dot(far[:, : other.shape[0]], other), far)
    final = dot(mean[:, :ready], ready_ref[...]) + dot_fetched(mean[:, ready:], held, copies)
    last.wait()
    final = (final + final_ref[...]).astype(BF16)
    capacity = outs[0].shape[0]
    for q, ref in enumerate(outs):
        ref[...] = final[q * capacity : (q + 1) * capacity]


def scatter_kernel(place_ref, *refs):
    out_ref = refs[-1]
    arrived = jnp.concatenate([ref[...] for ref in refs[:-1]], axis=0)
    out_ref[...] = dot(place_ref[...], arrived).astype(BF16)


def body(features, neighbours, neighbour_mask, layer2_position, self_weight1, neigh_weight1, self_weight2, neigh_weight2):
    rows, degree = neighbours.shape
    members = lax.axis_size("dev")
    peers = lax.axis_size("grp") * members
    width_in, width = self_weight1.shape
    steps = members // 2
    capacity = rows // steps
    size = peers * CAP
    early = width // 2
    shape = jax.ShapeDtypeStruct
    copies = pltpu.SemaphoreType.DMA

    pos = layer2_position.reshape(1, rows)
    groups = peers // members
    mates = 2 * groups

    def shifts(by):
        return [(i, (i + by) % members) for i in range(members)]

    tables = [features] + [lax.ppermute(features, "grp", [(i, i ^ m) for i in range(groups)]) for m in range(1, groups)]
    others = [lax.ppermute(t, "dev", [(i, i ^ 1) for i in range(members)]) for t in tables]
    key, local, span, *asks = call(
        functools.partial(ask_kernel, groups, members),
        (
            shape((degree, rows), I32),
            shape((degree, rows), I32),
            shape((2, peers, rows), I32),
            *(shape((mates, rows), I32) for _ in range(steps)),
        ),
        (neighbours.T, neighbour_mask.T, pos),
        (),
        [pltpu.VMEM((degree, rows), I32), pltpu.VMEM((degree, rows), I32), pltpu.VMEM((1, rows), I32), copies((3,))],
        2 * peers * rows * rows,
        "ask",
    )
    asked = [asks[0]] + [lax.ppermute(asks[q], "dev", shifts(2 * q)) for q in range(1, steps)]
    near, far, order, table = call(
        functools.partial(plan_kernel, peers, degree),
        (
            shape((rows, rows), BF16),
            shape((rows, size + 8), BF16),
            shape((size, size), BF16),
            shape((rows, width_in), BF16),
        ),
        (features,),
        (key, local, span),
        [copies((1,))],
        2 * size * size * rows,
        "plan",
        limit=40 << 20,
    )
    by_mate = call(
        functools.partial(sort_kernel, groups),
        tuple(shape((2 * steps, rows), I32) for _ in range(groups)),
        (),
        asked,
        [],
        2 * peers * peers * rows,
        "sort",
    )
    kept_asks = jnp.concatenate(
        [by_mate[0]] + [lax.ppermute(by_mate[m], "grp", [(i, i ^ m) for i in range(groups)]) for m in range(1, groups)]
    )
    passed_asks = lax.ppermute(kept_asks, "dev", [(i, i ^ 1) for i in range(members)])
    replies = call(
        functools.partial(serve_kernel, groups, steps),
        tuple(shape((mates * CAP, width_in), BF16) for _ in range(steps)),
        (),
        (order, *asked, *(t for pair in zip([table, *tables[1:]], others) for t in pair)),
        [],
        2 * size * rows * mates * width_in,
        "serve",
    )
    answers = [replies[0]] + [lax.ppermute(replies[q], "dev", shifts(-2 * q)) for q in range(1, steps)]
    pick = call(
        functools.partial(pick_kernel, members),
        shape((size, rows), BF16),
        (),
        (kept_asks, passed_asks),
        [],
        2 * size * size * rows,
        "pick",
    )
    kept, mean, reply_two = call(
        layer_one_kernel,
        (
            shape((size, width_in), BF16),
            shape((rows, width_in), BF16),
            shape((peers, CAP // 2, 2, width_in), BF16),
        ),
        (),
        (table, near, far, pick, *answers),
        [pltpu.VMEM((size, width_in), BF16), pltpu.VMEM((rows, width_in), BF16), copies((2,))],
        2 * rows * width_in * (size + rows) + 2 * size * rows * width_in,
        "layer_one",
        away=2,
    )
    answer_two = lax.all_to_all(reply_two, BOTH, 0, 0, tiled=True)
    final, place, base, far_moved, weight, ready = call(
        functools.partial(between_kernel, groups, members),
        (
            shape((rows, width), F32),
            shape((rows, rows), BF16),
            shape((size, width), BF16),
            shape((rows, size + 8), BF16),
            shape((width_in, width), BF16),
            shape((early, width), BF16),
        ),
        (self_weight1, neigh_weight1, self_weight2, neigh_weight2, pos, features, kept, mean),
        (near, far, *asked),
        [
            pltpu.VMEM((width_in, width), BF16),
            pltpu.VMEM((width, width), BF16),
            pltpu.VMEM((width - early, width), BF16),
            pltpu.VMEM((rows, width_in), BF16),
            pltpu.VMEM((size, width_in), BF16),
            pltpu.VMEM((rows, width_in), BF16),
            pltpu.VMEM((rows, width), F32),
            pltpu.VMEM((rows, rows), BF16),
            pltpu.VMEM((1, rows), I32),
            copies((11,)),
        ],
        2 * width * (rows * (2 * width_in + rows + 2 * width) + size * width_in),
        "between",
        limit=48 << 20,
        away=2,
    )
    finals = call(
        layer_two_kernel,
        tuple(shape((capacity, width), BF16) for _ in range(steps)),
        (neigh_weight2, final),
        (weight, ready, base, answer_two, far_moved),
        [pltpu.VMEM((width - early, width), BF16), pltpu.VMEM((rows, width), F32), copies((3,))],
        2 * width * (size * width_in + rows * (size + width)),
        "layer_two",
        limit=48 << 20,
    )
    arrived = [finals[0]]
    for q in range(1, steps):
        arrived.append(lax.ppermute(finals[q], "dev", [(i, (i + 2 * q) % members) for i in range(members)]))
    return call(
        scatter_kernel,
        shape((rows, width), BF16),
        (),
        (place, *arrived),
        [],
        2 * rows * rows * width,
        "scatter",
    )


def solution(mesh):
    return jax.shard_map(
        body,
        mesh=mesh,
        in_specs=(
            P(BOTH, None),
            P(BOTH, None),
            P(BOTH, None),
            P(BOTH),
            P(),
            P(),
            P(),
            P(),
        ),
        out_specs=P(BOTH, None),
        check_vma=False,
    )
```

```python
import functools

import jax
import jax.numpy as jnp
from jax import lax
from jax.experimental import pallas as pl
from jax.experimental.pallas import tpu as pltpu
from jax.sharding import PartitionSpec as P


CAP = 6
BOTH = ("grp", "dev")
F32 = jnp.float32
BF16 = jnp.bfloat16
I32 = jnp.int32


def divide(values, by):
    if by & (by - 1) == 0:
        return values >> (by.bit_length() - 1)
    return (values * (-(-(1 << 16) // by))) >> 16


def iota(shape, dim):
    return lax.broadcasted_iota(I32, shape, dim)


def bits(condition):
    return jnp.where(condition, 1.0, 0.0)


def earlier(count):
    return bits(iota((count, count), 0) < iota((count, count), 1)).astype(BF16)


def dot(left, right):
    return jnp.dot(left, right, preferred_element_type=F32)


def dot_lanes(left, right):
    return lax.dot_general(left, right, (((1,), (1,)), ((), ())), preferred_element_type=F32)


def near_by(n):
    return [pl.BlockSpec(memory_space=pltpu.VMEM)] * n


def far_off(n):
    return [pl.BlockSpec(memory_space=pltpu.HBM)] * n


def call(kernel, outs, remote, operands, scratch, flops, limit=24 << 20, away=0):
    single = not isinstance(outs, tuple)
    leaves = (outs,) if single else outs
    moved = sum(a.size * a.dtype.itemsize for a in (*remote, *operands, *leaves))
    return pl.pallas_call(
        kernel,
        out_shape=outs if single else (*(pltpu.HBM(a.shape, a.dtype) for a in leaves[:away]), *leaves[away:]),
        in_specs=far_off(len(remote)) + near_by(len(operands)),
        out_specs=near_by(1)[0] if single else far_off(away) + near_by(len(leaves) - away),
        scratch_shapes=scratch,
        compiler_params=pltpu.CompilerParams(vmem_limit_bytes=limit),
        cost_estimate=pl.CostEstimate(flops=flops, bytes_accessed=moved, transcendentals=0),
    )(*(pltpu.with_memory_space_constraint(a, pltpu.HBM) for a in remote), *operands)


def fetches(weight_ref, held, sems):
    pieces = sems.shape[0]
    depth = weight_ref.shape[0] // pieces
    return [
        pltpu.make_async_copy(
            weight_ref.at[pl.ds(i * depth, depth)], held.at[pl.ds(i * depth, depth)], sems.at[i]
        )
        for i in range(pieces)
    ]


def dot_fetched(left, held, copies):
    depth = held.shape[0] // len(copies)
    result = None
    for i, copy in enumerate(copies):
        copy.wait()
        part = dot(left[:, i * depth : (i + 1) * depth], held[i * depth : (i + 1) * depth])
        result = part if result is None else result + part
    return result


def seat():
    member = lax.axis_index("dev")
    return lax.axis_index("grp"), member >> 1, member & 1


def wrap(value, size):
    value = jnp.where(value < 0, value + size, value)
    return jnp.where(value >= size, value - size, value)


def device_at(index, groups, members):
    group, height, core = seat()
    step = divide(index, 2 * groups)
    mate = index - step * 2 * groups
    height = wrap(height + step, members // 2)
    return ((mate >> 1) ^ group) * members + 2 * height + ((mate & 1) ^ core), group * members + 2 * height + core


def apart(device, members):
    group, height, core = seat()
    its_group = divide(device, members)
    member = device - its_group * members
    return wrap((member >> 1) - height, members // 2), its_group ^ group, (member & 1) ^ core


def ask_kernel(groups, members, ids_hbm, mask_hbm, pos_hbm, key_ref, local_ref, span_ref, *refs):
    ask_refs, (ids, mask, pos_ref, sems) = refs[:-4], refs[-4:]
    peers = groups * members
    degree, rows = ids.shape
    copies = [
        pltpu.make_async_copy(ids_hbm, ids, sems.at[0]),
        pltpu.make_async_copy(mask_hbm, mask, sems.at[1]),
        pltpu.make_async_copy(pos_hbm, pos_ref, sems.at[2]),
    ]
    for copy in copies:
        copy.start()
    own = lax.axis_index("grp") * members + lax.axis_index("dev")
    peer, new_home = device_at(iota((peers, rows), 0), groups, members)
    prefix = earlier(rows)
    for copy in copies:
        copy.wait()
    slots = jnp.where(mask[...] > 0, ids[...], -1)
    owner = divide(jnp.maximum(slots, 0), rows)
    row = slots - owner * rows
    live = slots >= 0
    here = owner == own
    key = jnp.where(live & jnp.logical_not(here), owner, -1)
    half = CAP // 2
    width = (rows - 1).bit_length()
    top = width * (half - 1)
    low = jnp.zeros((peers, rows), I32)
    high = jnp.zeros((peers, rows), I32)
    total = jnp.zeros((peers, rows), I32)
    for s in range(degree):
        hit = key[s : s + 1] == peer
        high = jnp.where(hit, (high << width) | (low >> top), high)
        low = jnp.where(hit, ((low & ((1 << top) - 1)) << width) | row[s : s + 1], low)
        total += jnp.where(hit, 1, 0)
    before = dot(total.astype(F32).astype(BF16), prefix).astype(I32)
    packed = [jnp.where(before == 0, low, 0), jnp.where(before == 0, high, jnp.where(before == half, low, 0))]
    for k in range(1, half):
        shift, rest = width * k, width * (half - k)
        inside = before == k
        packed[0] = jnp.where(inside, (low & ((1 << rest) - 1)) << shift, packed[0])
        packed[1] = jnp.where(inside, (high << shift) | (low >> rest), packed[1])
        packed[1] = jnp.where(before == half + k, low << shift, packed[1])
    lane = iota((peers, rows), 1)
    wanted = jnp.zeros((peers, rows), I32)
    for w, word in enumerate(packed):
        word = jnp.broadcast_to(jnp.sum(word.astype(F32), axis=1, keepdims=True).astype(I32), (peers, rows))
        for k in range(half):
            wanted = jnp.where(lane == w * half + k, (word >> (width * k)) & ((1 << width) - 1), wanted)
    pos = pos_ref[...]
    place = jnp.where(divide(pos, rows) == new_home, pos - divide(pos, rows) * rows + 1, 0)
    asks = place + wanted * (2 * rows)
    for q, ref in enumerate(ask_refs):
        ref[...] = asks[q * 2 * groups : (q + 1) * 2 * groups]
    key_ref[...] = key
    local_ref[...] = jnp.where(live & here, row, -1)
    span_ref[0] = before
    span_ref[1] = total


def plan_kernel(
    peers, degree, features_hbm, key_ref, local_ref, span_ref, near_ref, far_ref, order_ref, features_ref, sems
):
    taken = pltpu.make_async_copy(features_hbm, features_ref, sems.at[0])
    taken.start()
    rows = features_ref.shape[0]
    local = local_ref[...]
    node = iota((rows, rows), 0)
    near = jnp.zeros((rows, rows), F32)
    for s in range(degree):
        near += bits(local[s : s + 1] == node)
    near = near.T.astype(BF16)
    near_ref[...] = near
    before, total = span_ref[0], span_ref[1]
    far = [bits((before <= k) & (k < before + total)).astype(BF16) for k in range(CAP)]
    far = jnp.concatenate(far, axis=0)
    size = peers * CAP
    line = iota((size, size), 0)
    peer = divide(line, CAP)
    order = bits(iota((size, size), 1) == (line - peer * CAP) * peers + peer).astype(BF16)
    order_ref[...] = order
    far_ref[:, :size] = dot(order, far).T.astype(BF16)
    live = bits((local >= 0) | (key_ref[...] >= 0))
    count = jnp.broadcast_to(jnp.sum(live, axis=0, keepdims=True), (rows, rows)).T.astype(BF16)
    far_ref[:, size:] = count[:, : far_ref.shape[1] - size]
    taken.wait()


def store_rows(reply_ref, rows):
    peers, pairs, two, width = reply_ref.shape
    reply_ref[...] = rows.reshape(peers, pairs, two, width)


def load_rows(answer_ref):
    peers, pairs, two, width = answer_ref.shape
    return answer_ref[...].reshape(peers * pairs * two, width)


def picks_of(wanted, order):
    lane = iota(wanted.shape, 1)
    picks = [bits(wanted[:, k : k + 1] == lane).astype(BF16) for k in range(CAP)]
    return dot(order, jnp.concatenate(picks, axis=0)).astype(BF16)


def sort_kernel(groups, *refs):
    steps = len(refs) - groups
    asked = jnp.concatenate([ref[...] for ref in refs[:steps]], axis=0)
    peers, rows = asked.shape
    wanted = divide(asked, 2 * rows)
    line = iota((peers, peers), 0)
    mate = divide(line, steps)
    pick = bits(iota((peers, peers), 1) == (line - mate * steps) * 2 * groups + mate).astype(BF16)
    sorted_rows = dot(pick, wanted.astype(F32).astype(BF16)).astype(I32)
    for m, ref in enumerate(refs[steps:]):
        ref[...] = sorted_rows[m * 2 * steps : (m + 1) * 2 * steps]


def serve_kernel(groups, steps, order_ref, *refs):
    asked_refs, refs = refs[:steps], refs[steps:]
    table_refs, reply_refs = refs[: 2 * groups], refs[2 * groups :]
    asked = jnp.concatenate([ref[...] for ref in asked_refs], axis=0)
    pick = picks_of(divide(asked, 2 * asked.shape[1]), order_ref[...])
    line = divide(iota(pick.shape, 0), CAP)
    mate = line - divide(line, 2 * groups) * 2 * groups
    rows = None
    for m in range(groups):
        left = [jnp.where(mate == 2 * m + side, pick, jnp.zeros_like(pick)) for side in range(2)]
        table = jnp.concatenate([table_refs[2 * m][...], table_refs[2 * m + 1][...]], axis=0)
        part = dot(jnp.concatenate(left, axis=1), table)
        rows = part if rows is None else rows + part
    rows = rows.astype(BF16)
    block = rows.shape[0] // steps
    for q, ref in enumerate(reply_refs):
        ref[...] = rows[q * block : (q + 1) * block]


def pick_kernel(members, kept_ref, passed_ref, pick_ref):
    kept = kept_ref[...]
    peers = kept.shape[0]
    steps = members // 2
    half = divide(iota(kept.shape, 0), steps)
    wanted = jnp.where((half & 1) == 0, kept, passed_ref[...])
    size = peers * CAP
    line = iota((size, size), 0)
    device = divide(line, CAP)
    step, group, core = apart(device, members)
    row = (2 * group + core) * steps + wrap(-step, steps)
    order = bits(iota((size, size), 1) == (line - device * CAP) * peers + row).astype(BF16)
    pick_ref[...] = picks_of(wanted, order)


def over_count(summed, far):
    size = far.shape[1] - 8
    return (summed / far[:, size : size + 1].astype(F32)).astype(BF16)


def layer_one_kernel(features_ref, near_ref, far_ref, pick_ref, *refs):
    answer_refs, (answer_hbm, mean_hbm, reply_ref, kept, mean_ref, sems) = refs[:-6], refs[-6:]
    answer = jnp.concatenate([ref[...] for ref in answer_refs], axis=0)
    kept[...] = answer
    saves = [
        pltpu.make_async_copy(kept, answer_hbm, sems.at[0]),
        pltpu.make_async_copy(mean_ref, mean_hbm, sems.at[1]),
    ]
    saves[0].start()
    far = far_ref[...]
    mean = over_count(dot(near_ref[...], features_ref[...]) + dot(far[:, : answer.shape[0]], answer), far)
    mean_ref[...] = mean
    saves[1].start()
    store_rows(reply_ref, dot(pick_ref[...], mean).astype(BF16))
    for save in saves:
        save.wait()


def between_kernel(
    groups, members, self_one_hbm, neigh_one_hbm, self_two_hbm, neigh_two_hbm, pos_hbm, features_hbm, answer_hbm, mean_hbm,
    near_ref, far_ref, *refs,
):
    asked_refs, refs = refs[: members // 2], refs[members // 2 :]
    between_body(
        groups, members, self_one_hbm, neigh_one_hbm, self_two_hbm, neigh_two_hbm, pos_hbm, features_hbm, answer_hbm, mean_hbm,
        near_ref, far_ref, asked_refs, *refs,
    )


def between_body(
    groups, members, self_one_hbm, neigh_one_hbm, self_two_hbm, neigh_two_hbm, pos_hbm, features_hbm, answer_hbm, mean_hbm,
    near_ref, far_ref, asked_refs,
    final_hbm, place_hbm, base_ref, far_moved_ref, neigh_one_ref, ready_ref,
    held_one, held_two, rest, features_ref, answer_ref, mean_ref, final_ref, place_ref, pos_ref, sems,
):
    ready = ready_ref.shape[0]
    copies = [
        pltpu.make_async_copy(pos_hbm, pos_ref, sems.at[0]),
        pltpu.make_async_copy(self_one_hbm, held_one, sems.at[1]),
        pltpu.make_async_copy(neigh_one_hbm, neigh_one_ref, sems.at[2]),
        pltpu.make_async_copy(self_two_hbm, held_two, sems.at[3]),
        pltpu.make_async_copy(neigh_two_hbm.at[pl.ds(0, ready)], ready_ref, sems.at[4]),
        pltpu.make_async_copy(neigh_two_hbm.at[pl.ds(ready, rest.shape[0])], rest, sems.at[5]),
    ]
    inputs = [
        pltpu.make_async_copy(features_hbm, features_ref, sems.at[6]),
        pltpu.make_async_copy(answer_hbm, answer_ref, sems.at[7]),
        pltpu.make_async_copy(mean_hbm, mean_ref, sems.at[8]),
    ]
    for copy in (*inputs, *copies):
        copy.start()
    rows = features_ref.shape[0]
    capacity = 2 * rows // members
    me = lax.axis_index("dev")
    first = lax.axis_index("grp") * members
    line = iota((rows, rows), 0)
    step = divide(line, capacity)
    rank = line - step * capacity
    target = me + 2 * step
    target = jnp.where(target >= members, target - members, target)
    prefix = earlier(rows)
    copies[0].wait()
    goes = target == divide(pos_ref[...], rows) - first
    before = dot(bits(goes).astype(BF16), prefix).astype(I32)
    move = bits(goes & (before == rank)).astype(BF16)
    near = dot(move, near_ref[...]).astype(BF16)
    size = base_ref.shape[0]
    slot = iota((size, size), 0)
    device = divide(slot, CAP)
    up, group, core = apart(device, members)
    came = ((up * groups + group) * 2 + core) * CAP + slot - device * CAP
    resort = bits(iota((size, size), 1) == came).astype(BF16)
    far = dot(move, far_ref[...]).astype(BF16)
    far_moved_ref[:, size:] = far[:, size:]
    far_moved_ref[:, :size] = dot_lanes(far[:, :size], resort).astype(BF16)
    place = jnp.zeros((rows, rows), F32)
    for q in range(members // 2):
        sent = asked_refs[q][0:1] & (2 * rows - 1)
        valid = jnp.broadcast_to(sent > 0, (rows, rows))
        before = dot(bits(valid).astype(BF16), prefix).astype(I32)
        lands = bits(sent - 1 == line).astype(BF16)
        comes = bits(valid & (step == q) & (before == rank)).astype(BF16)
        place += dot_lanes(lands, comes)
    place_ref[...] = place.astype(BF16)
    placed = pltpu.make_async_copy(place_ref, place_hbm, sems.at[9])
    placed.start()
    for copy in (*inputs, copies[1]):
        copy.wait()
    own = dot(features_ref[...], held_one[...])
    base_ref[...] = dot(dot(resort, answer_ref[...]).astype(BF16), held_one[...]).astype(BF16)
    copies[2].wait()
    hidden = jnp.maximum(own + dot(mean_ref[...], neigh_one_ref[...]), 0.0).astype(BF16)
    mean = over_count(dot(near, hidden), far)
    moved = dot(move, hidden).astype(BF16)
    copies[3].wait()
    final = dot(moved, held_two[...])
    copies[4].wait()
    final += dot(mean[:, :ready], ready_ref[...])
    copies[5].wait()
    final_ref[...] = final + dot(mean[:, ready:], rest[...])
    away = pltpu.make_async_copy(final_ref, final_hbm, sems.at[10])
    away.start()
    away.wait()
    placed.wait()


def layer_two_kernel(neigh_two_hbm, final_hbm, neigh_one_ref, ready_ref, base_ref, answer_ref, far_ref, *refs):
    outs, held, final_ref, sems = refs[:-3], refs[-3], refs[-2], refs[-1]
    ready = ready_ref.shape[0]
    pieces = sems.shape[0] - 1
    copies = fetches(neigh_two_hbm.at[pl.ds(ready, held.shape[0])], held, sems.at[pl.ds(0, pieces)])
    last = pltpu.make_async_copy(final_hbm, final_ref, sems.at[pieces])
    for copy in (*copies, last):
        copy.start()
    far = far_ref[...]
    other = jnp.maximum(base_ref[...].astype(F32) + dot(load_rows(answer_ref), neigh_one_ref[...]), 0.0).astype(BF16)
    mean = over_count(dot(far[:, : other.shape[0]], other), far)
    final = dot(mean[:, :ready], ready_ref[...]) + dot_fetched(mean[:, ready:], held, copies)
    last.wait()
    final = (final + final_ref[...]).astype(BF16)
    capacity = outs[0].shape[0]
    for q, ref in enumerate(outs):
        ref[...] = final[q * capacity : (q + 1) * capacity]


def scatter_kernel(place_ref, *refs):
    out_ref = refs[-1]
    arrived = jnp.concatenate([ref[...] for ref in refs[:-1]], axis=0)
    out_ref[...] = dot(place_ref[...], arrived).astype(BF16)


def compute(features, neighbours, neighbour_mask, layer2_position, self_weight1, neigh_weight1, self_weight2, neigh_weight2):
    rows, degree = neighbours.shape
    members = lax.axis_size("dev")
    peers = lax.axis_size("grp") * members
    width_in, width = self_weight1.shape
    steps = members // 2
    capacity = rows // steps
    size = peers * CAP
    early = width // 2
    shape = jax.ShapeDtypeStruct
    copies = pltpu.SemaphoreType.DMA

    pos = layer2_position.reshape(1, rows)
    groups = peers // members
    mates = 2 * groups

    def shifts(by):
        return [(i, (i + by) % members) for i in range(members)]

    def across(by):
        return [(i, i ^ by) for i in range(groups)]

    pairs = [(i, i ^ 1) for i in range(members)]
    tables = [features] + [lax.ppermute(features, "grp", across(m)) for m in range(1, groups)]
    others = [lax.ppermute(t, "dev", pairs) for t in tables]
    key, local, span, *asks = call(
        functools.partial(ask_kernel, groups, members),
        (
            shape((degree, rows), I32),
            shape((degree, rows), I32),
            shape((2, peers, rows), I32),
            *(shape((mates, rows), I32) for _ in range(steps)),
        ),
        (neighbours.T, neighbour_mask.T, pos),
        (),
        [pltpu.VMEM((degree, rows), I32), pltpu.VMEM((degree, rows), I32), pltpu.VMEM((1, rows), I32), copies((3,))],
        2 * peers * rows * rows,
    )
    asked = [asks[0]] + [lax.ppermute(asks[q], "dev", shifts(2 * q)) for q in range(1, steps)]
    near, far, order, table = call(
        functools.partial(plan_kernel, peers, degree),
        (
            shape((rows, rows), BF16),
            shape((rows, size + 8), BF16),
            shape((size, size), BF16),
            shape((rows, width_in), BF16),
        ),
        (features,),
        (key, local, span),
        [copies((1,))],
        2 * size * size * rows,
        limit=40 << 20,
    )
    by_mate = call(
        functools.partial(sort_kernel, groups),
        tuple(shape((2 * steps, rows), I32) for _ in range(groups)),
        (),
        asked,
        [],
        2 * peers * peers * rows,
    )
    kept_asks = jnp.concatenate([by_mate[0]] + [lax.ppermute(by_mate[m], "grp", across(m)) for m in range(1, groups)])
    passed_asks = lax.ppermute(kept_asks, "dev", pairs)
    replies = call(
        functools.partial(serve_kernel, groups, steps),
        tuple(shape((mates * CAP, width_in), BF16) for _ in range(steps)),
        (),
        (order, *asked, *(t for pair in zip([table, *tables[1:]], others) for t in pair)),
        [],
        2 * size * rows * mates * width_in,
    )
    answers = [replies[0]] + [lax.ppermute(replies[q], "dev", shifts(-2 * q)) for q in range(1, steps)]
    pick = call(
        functools.partial(pick_kernel, members),
        shape((size, rows), BF16),
        (),
        (kept_asks, passed_asks),
        [],
        2 * size * size * rows,
    )
    kept, mean, reply_two = call(
        layer_one_kernel,
        (
            shape((size, width_in), BF16),
            shape((rows, width_in), BF16),
            shape((peers, CAP // 2, 2, width_in), BF16),
        ),
        (),
        (table, near, far, pick, *answers),
        [pltpu.VMEM((size, width_in), BF16), pltpu.VMEM((rows, width_in), BF16), copies((2,))],
        2 * rows * width_in * (size + rows) + 2 * size * rows * width_in,
        away=2,
    )
    answer_two = lax.all_to_all(reply_two, BOTH, 0, 0, tiled=True)
    final, place, base, far_moved, weight, ready = call(
        functools.partial(between_kernel, groups, members),
        (
            shape((rows, width), F32),
            shape((rows, rows), BF16),
            shape((size, width), BF16),
            shape((rows, size + 8), BF16),
            shape((width_in, width), BF16),
            shape((early, width), BF16),
        ),
        (self_weight1, neigh_weight1, self_weight2, neigh_weight2, pos, features, kept, mean),
        (near, far, *asked),
        [
            pltpu.VMEM((width_in, width), BF16),
            pltpu.VMEM((width, width), BF16),
            pltpu.VMEM((width - early, width), BF16),
            pltpu.VMEM((rows, width_in), BF16),
            pltpu.VMEM((size, width_in), BF16),
            pltpu.VMEM((rows, width_in), BF16),
            pltpu.VMEM((rows, width), F32),
            pltpu.VMEM((rows, rows), BF16),
            pltpu.VMEM((1, rows), I32),
            copies((11,)),
        ],
        2 * width * (rows * (2 * width_in + rows + 2 * width) + size * width_in),
        limit=48 << 20,
        away=2,
    )
    finals = call(
        layer_two_kernel,
        tuple(shape((capacity, width), BF16) for _ in range(steps)),
        (neigh_weight2, final),
        (weight, ready, base, answer_two, far_moved),
        [pltpu.VMEM((width - early, width), BF16), pltpu.VMEM((rows, width), F32), copies((3,))],
        2 * width * (size * width_in + rows * (size + width)),
        limit=48 << 20,
    )
    arrived = [finals[0]]
    for q in range(1, steps):
        arrived.append(lax.ppermute(finals[q], "dev", shifts(2 * q)))
    return call(scatter_kernel, shape((rows, width), BF16), (), (place, *arrived), [], 2 * rows * rows * width)


def solution(mesh):
    return jax.shard_map(
        compute,
        mesh=mesh,
        in_specs=(
            P(BOTH, None),
            P(BOTH, None),
            P(BOTH, None),
            P(BOTH),
            P(),
            P(),
            P(),
            P(),
        ),
        out_specs=P(BOTH, None),
        check_vma=False,
    )
```

```python
import functools

import jax
import jax.numpy as jnp
from jax import lax
from jax.experimental import pallas as pl
from jax.experimental.pallas import tpu as pltpu
from jax.sharding import PartitionSpec as P


CAP = 6
BOTH = ("grp", "dev")
F32 = jnp.float32
BF16 = jnp.bfloat16
I32 = jnp.int32


def divide(values, by):
    if by & (by - 1) == 0:
        return values >> (by.bit_length() - 1)
    return (values * (-(-(1 << 16) // by))) >> 16


def iota(shape, dim):
    return lax.broadcasted_iota(I32, shape, dim)


def bits(condition):
    return jnp.where(condition, 1.0, 0.0)


def earlier(count):
    return bits(iota((count, count), 0) < iota((count, count), 1)).astype(BF16)


def dot(left, right):
    return jnp.dot(left, right, preferred_element_type=F32)


def dot_lanes(left, right):
    return lax.dot_general(left, right, (((1,), (1,)), ((), ())), preferred_element_type=F32)


def near_by(n):
    return [pl.BlockSpec(memory_space=pltpu.VMEM)] * n


def far_off(n):
    return [pl.BlockSpec(memory_space=pltpu.HBM)] * n


def call(kernel, outs, remote, operands, scratch, flops, limit=24 << 20, away=0):
    single = not isinstance(outs, tuple)
    leaves = (outs,) if single else outs
    moved = sum(a.size * a.dtype.itemsize for a in (*remote, *operands, *leaves))
    return pl.pallas_call(
        kernel,
        out_shape=outs if single else (*(pltpu.HBM(a.shape, a.dtype) for a in leaves[:away]), *leaves[away:]),
        in_specs=far_off(len(remote)) + near_by(len(operands)),
        out_specs=near_by(1)[0] if single else far_off(away) + near_by(len(leaves) - away),
        scratch_shapes=scratch,
        compiler_params=pltpu.CompilerParams(vmem_limit_bytes=limit),
        cost_estimate=pl.CostEstimate(flops=flops, bytes_accessed=moved, transcendentals=0),
    )(*(pltpu.with_memory_space_constraint(a, pltpu.HBM) for a in remote), *operands)


def fetches(weight_ref, held, sems):
    pieces = sems.shape[0]
    depth = weight_ref.shape[0] // pieces
    return [
        pltpu.make_async_copy(
            weight_ref.at[pl.ds(i * depth, depth)], held.at[pl.ds(i * depth, depth)], sems.at[i]
        )
        for i in range(pieces)
    ]


def dot_fetched(left, held, copies):
    depth = held.shape[0] // len(copies)
    result = None
    for i, copy in enumerate(copies):
        copy.wait()
        part = dot(left[:, i * depth : (i + 1) * depth], held[i * depth : (i + 1) * depth])
        result = part if result is None else result + part
    return result


def seat():
    member = lax.axis_index("dev")
    return lax.axis_index("grp"), member >> 1, member & 1


def wrap(value, size):
    value = jnp.where(value < 0, value + size, value)
    return jnp.where(value >= size, value - size, value)


def device_at(index, groups, members):
    group, height, core = seat()
    step = divide(index, 2 * groups)
    mate = index - step * 2 * groups
    height = wrap(height + step, members // 2)
    return ((mate >> 1) ^ group) * members + 2 * height + ((mate & 1) ^ core), group * members + 2 * height + core


def apart(device, members):
    group, height, core = seat()
    its_group = divide(device, members)
    member = device - its_group * members
    return wrap((member >> 1) - height, members // 2), its_group ^ group, (member & 1) ^ core


def ask_kernel(groups, members, ids_hbm, mask_hbm, pos_hbm, key_ref, local_ref, span_ref, *refs):
    ask_refs, (ids, mask, pos_ref, sems) = refs[:-4], refs[-4:]
    peers = groups * members
    degree, rows = ids.shape
    copies = [
        pltpu.make_async_copy(ids_hbm, ids, sems.at[0]),
        pltpu.make_async_copy(mask_hbm, mask, sems.at[1]),
        pltpu.make_async_copy(pos_hbm, pos_ref, sems.at[2]),
    ]
    for copy in copies:
        copy.start()
    own = lax.axis_index("grp") * members + lax.axis_index("dev")
    peer, new_home = device_at(iota((peers, rows), 0), groups, members)
    prefix = earlier(rows)
    for copy in copies:
        copy.wait()
    slots = jnp.where(mask[...] > 0, ids[...], -1)
    owner = divide(jnp.maximum(slots, 0), rows)
    row = slots - owner * rows
    live = slots >= 0
    here = owner == own
    key = jnp.where(live & jnp.logical_not(here), owner, -1)
    half = CAP // 2
    width = (rows - 1).bit_length()
    top = width * (half - 1)
    low = jnp.zeros((peers, rows), I32)
    high = jnp.zeros((peers, rows), I32)
    total = jnp.zeros((peers, rows), I32)
    for s in range(degree):
        hit = key[s : s + 1] == peer
        high = jnp.where(hit, (high << width) | (low >> top), high)
        low = jnp.where(hit, ((low & ((1 << top) - 1)) << width) | row[s : s + 1], low)
        total += jnp.where(hit, 1, 0)
    before = dot(total.astype(F32).astype(BF16), prefix).astype(I32)
    packed = [jnp.where(before == 0, low, 0), jnp.where(before == 0, high, jnp.where(before == half, low, 0))]
    for k in range(1, half):
        shift, rest = width * k, width * (half - k)
        inside = before == k
        packed[0] = jnp.where(inside, (low & ((1 << rest) - 1)) << shift, packed[0])
        packed[1] = jnp.where(inside, (high << shift) | (low >> rest), packed[1])
        packed[1] = jnp.where(before == half + k, low << shift, packed[1])
    lane = iota((peers, rows), 1)
    wanted = jnp.zeros((peers, rows), I32)
    for w, word in enumerate(packed):
        word = jnp.broadcast_to(jnp.sum(word.astype(F32), axis=1, keepdims=True).astype(I32), (peers, rows))
        for k in range(half):
            wanted = jnp.where(lane == w * half + k, (word >> (width * k)) & ((1 << width) - 1), wanted)
    pos = pos_ref[...]
    place = jnp.where(divide(pos, rows) == new_home, pos - divide(pos, rows) * rows + 1, 0)
    asks = place + wanted * (2 * rows)
    for q, ref in enumerate(ask_refs):
        ref[...] = asks[q * 2 * groups : (q + 1) * 2 * groups]
    key_ref[...] = key
    local_ref[...] = jnp.where(live & here, row, -1)
    span_ref[0] = before
    span_ref[1] = total


def plan_kernel(
    peers, degree, features_hbm, key_ref, local_ref, span_ref, near_ref, far_ref, order_ref, features_ref, sems
):
    taken = pltpu.make_async_copy(features_hbm, features_ref, sems.at[0])
    taken.start()
    rows = features_ref.shape[0]
    local = local_ref[...]
    node = iota((rows, rows), 0)
    near = jnp.zeros((rows, rows), F32)
    for s in range(degree):
        near += bits(local[s : s + 1] == node)
    near = near.T.astype(BF16)
    near_ref[...] = near
    before, total = span_ref[0], span_ref[1]
    far = [bits((before <= k) & (k < before + total)).astype(BF16) for k in range(CAP)]
    far = jnp.concatenate(far, axis=0)
    size = peers * CAP
    line = iota((size, size), 0)
    peer = divide(line, CAP)
    order = bits(iota((size, size), 1) == (line - peer * CAP) * peers + peer).astype(BF16)
    order_ref[...] = order
    far_ref[:, :size] = dot(order, far).T.astype(BF16)
    live = bits((local >= 0) | (key_ref[...] >= 0))
    count = jnp.broadcast_to(jnp.sum(live, axis=0, keepdims=True), (rows, rows)).T.astype(BF16)
    far_ref[:, size:] = count[:, : far_ref.shape[1] - size]
    taken.wait()


def store_rows(reply_ref, rows):
    peers, pairs, two, width = reply_ref.shape
    reply_ref[...] = rows.reshape(peers, pairs, two, width)


def load_rows(answer_ref):
    peers, pairs, two, width = answer_ref.shape
    return answer_ref[...].reshape(peers * pairs * two, width)


def picks_of(wanted, order):
    lane = iota(wanted.shape, 1)
    picks = [bits(wanted[:, k : k + 1] == lane).astype(BF16) for k in range(CAP)]
    return dot(order, jnp.concatenate(picks, axis=0)).astype(BF16)


def sort_kernel(groups, *refs):
    steps = len(refs) - groups
    asked = jnp.concatenate([ref[...] for ref in refs[:steps]], axis=0)
    peers, rows = asked.shape
    wanted = divide(asked, 2 * rows)
    line = iota((peers, peers), 0)
    mate = divide(line, steps)
    pick = bits(iota((peers, peers), 1) == (line - mate * steps) * 2 * groups + mate).astype(BF16)
    sorted_rows = dot(pick, wanted.astype(F32).astype(BF16)).astype(I32)
    for m, ref in enumerate(refs[steps:]):
        ref[...] = sorted_rows[m * 2 * steps : (m + 1) * 2 * steps]


def serve_kernel(groups, steps, order_ref, *refs):
    asked_refs, refs = refs[:steps], refs[steps:]
    table_refs, reply_refs = refs[: 2 * groups], refs[2 * groups :]
    asked = jnp.concatenate([ref[...] for ref in asked_refs], axis=0)
    pick = picks_of(divide(asked, 2 * asked.shape[1]), order_ref[...])
    line = divide(iota(pick.shape, 0), CAP)
    mate = line - divide(line, 2 * groups) * 2 * groups
    rows = None
    for m in range(groups):
        left = [jnp.where(mate == 2 * m + side, pick, jnp.zeros_like(pick)) for side in range(2)]
        table = jnp.concatenate([table_refs[2 * m][...], table_refs[2 * m + 1][...]], axis=0)
        part = dot(jnp.concatenate(left, axis=1), table)
        rows = part if rows is None else rows + part
    rows = rows.astype(BF16)
    block = rows.shape[0] // steps
    for q, ref in enumerate(reply_refs):
        ref[...] = rows[q * block : (q + 1) * block]


def line_kernel(kept_ref, passed_ref, *refs):
    steps = len(refs)
    kept = kept_ref[...]
    peers = kept.shape[0]
    half = divide(iota(kept.shape, 0), steps)
    wanted = jnp.where((half & 1) == 0, kept, passed_ref[...])
    mates = peers // steps
    line = iota((peers, peers), 0)
    step = divide(line, mates)
    pick = bits(iota((peers, peers), 1) == (line - step * mates) * steps + step).astype(BF16)
    sorted_rows = dot(pick, wanted.astype(F32).astype(BF16)).astype(I32)
    for q, ref in enumerate(refs):
        ref[...] = sorted_rows[q * mates : (q + 1) * mates]


def pick_kernel(members, *refs):
    wanted_refs, pick_ref = refs[:-1], refs[-1]
    wanted = jnp.concatenate([ref[...] for ref in wanted_refs], axis=0)
    peers = wanted.shape[0]
    steps = members // 2
    size = peers * CAP
    line = iota((size, size), 0)
    device = divide(line, CAP)
    step, group, core = apart(device, members)
    row = wrap(-step, steps) * (peers // steps) + 2 * group + core
    order = bits(iota((size, size), 1) == (line - device * CAP) * peers + row).astype(BF16)
    pick_ref[...] = picks_of(wanted, order)


def over_count(summed, far):
    size = far.shape[1] - 8
    return (summed / far[:, size : size + 1].astype(F32)).astype(BF16)


def layer_one_kernel(features_ref, near_ref, far_ref, pick_ref, *refs):
    answer_refs, (answer_hbm, mean_hbm, reply_ref, kept, mean_ref, sems) = refs[:-6], refs[-6:]
    answer = jnp.concatenate([ref[...] for ref in answer_refs], axis=0)
    kept[...] = answer
    saves = [
        pltpu.make_async_copy(kept, answer_hbm, sems.at[0]),
        pltpu.make_async_copy(mean_ref, mean_hbm, sems.at[1]),
    ]
    saves[0].start()
    far = far_ref[...]
    mean = over_count(dot(near_ref[...], features_ref[...]) + dot(far[:, : answer.shape[0]], answer), far)
    mean_ref[...] = mean
    saves[1].start()
    store_rows(reply_ref, dot(pick_ref[...], mean).astype(BF16))
    for save in saves:
        save.wait()


def between_kernel(
    groups, members, self_one_hbm, neigh_one_hbm, self_two_hbm, neigh_two_hbm, pos_hbm, features_hbm, answer_hbm, mean_hbm,
    near_ref, far_ref, *refs,
):
    asked_refs, refs = refs[: members // 2], refs[members // 2 :]
    between_body(
        groups, members, self_one_hbm, neigh_one_hbm, self_two_hbm, neigh_two_hbm, pos_hbm, features_hbm, answer_hbm, mean_hbm,
        near_ref, far_ref, asked_refs, *refs,
    )


def between_body(
    groups, members, self_one_hbm, neigh_one_hbm, self_two_hbm, neigh_two_hbm, pos_hbm, features_hbm, answer_hbm, mean_hbm,
    near_ref, far_ref, asked_refs,
    final_hbm, place_hbm, base_ref, far_moved_ref, neigh_one_ref, ready_ref,
    held_one, held_two, rest, features_ref, answer_ref, mean_ref, final_ref, place_ref, pos_ref, sems,
):
    ready = ready_ref.shape[0]
    copies = [
        pltpu.make_async_copy(pos_hbm, pos_ref, sems.at[0]),
        pltpu.make_async_copy(self_one_hbm, held_one, sems.at[1]),
        pltpu.make_async_copy(neigh_one_hbm, neigh_one_ref, sems.at[2]),
        pltpu.make_async_copy(self_two_hbm, held_two, sems.at[3]),
        pltpu.make_async_copy(neigh_two_hbm.at[pl.ds(0, ready)], ready_ref, sems.at[4]),
        pltpu.make_async_copy(neigh_two_hbm.at[pl.ds(ready, rest.shape[0])], rest, sems.at[5]),
    ]
    inputs = [
        pltpu.make_async_copy(features_hbm, features_ref, sems.at[6]),
        pltpu.make_async_copy(answer_hbm, answer_ref, sems.at[7]),
        pltpu.make_async_copy(mean_hbm, mean_ref, sems.at[8]),
    ]
    for copy in (*inputs, *copies):
        copy.start()
    rows = features_ref.shape[0]
    capacity = 2 * rows // members
    me = lax.axis_index("dev")
    first = lax.axis_index("grp") * members
    line = iota((rows, rows), 0)
    step = divide(line, capacity)
    rank = line - step * capacity
    target = me + 2 * step
    target = jnp.where(target >= members, target - members, target)
    prefix = earlier(rows)
    copies[0].wait()
    goes = target == divide(pos_ref[...], rows) - first
    before = dot(bits(goes).astype(BF16), prefix).astype(I32)
    move = bits(goes & (before == rank)).astype(BF16)
    near = dot(move, near_ref[...]).astype(BF16)
    size = base_ref.shape[0]
    slot = iota((size, size), 0)
    device = divide(slot, CAP)
    up, group, core = apart(device, members)
    came = ((up * groups + group) * 2 + core) * CAP + slot - device * CAP
    resort = bits(iota((size, size), 1) == came).astype(BF16)
    far = dot(move, far_ref[...]).astype(BF16)
    far_moved_ref[:, size:] = far[:, size:]
    far_moved_ref[:, :size] = dot_lanes(far[:, :size], resort).astype(BF16)
    place = jnp.zeros((rows, rows), F32)
    for q in range(members // 2):
        sent = asked_refs[q][0:1] & (2 * rows - 1)
        valid = jnp.broadcast_to(sent > 0, (rows, rows))
        before = dot(bits(valid).astype(BF16), prefix).astype(I32)
        lands = bits(sent - 1 == line).astype(BF16)
        comes = bits(valid & (step == q) & (before == rank)).astype(BF16)
        place += dot_lanes(lands, comes)
    place_ref[...] = place.astype(BF16)
    placed = pltpu.make_async_copy(place_ref, place_hbm, sems.at[9])
    placed.start()
    for copy in (*inputs, copies[1]):
        copy.wait()
    own = dot(features_ref[...], held_one[...])
    base_ref[...] = dot(dot(resort, answer_ref[...]).astype(BF16), held_one[...]).astype(BF16)
    copies[2].wait()
    hidden = jnp.maximum(own + dot(mean_ref[...], neigh_one_ref[...]), 0.0).astype(BF16)
    mean = over_count(dot(near, hidden), far)
    moved = dot(move, hidden).astype(BF16)
    copies[3].wait()
    final = dot(moved, held_two[...])
    copies[4].wait()
    final += dot(mean[:, :ready], ready_ref[...])
    copies[5].wait()
    final_ref[...] = final + dot(mean[:, ready:], rest[...])
    away = pltpu.make_async_copy(final_ref, final_hbm, sems.at[10])
    away.start()
    away.wait()
    placed.wait()


def layer_two_kernel(neigh_two_hbm, final_hbm, neigh_one_ref, ready_ref, base_ref, answer_ref, far_ref, *refs):
    outs, held, final_ref, sems = refs[:-3], refs[-3], refs[-2], refs[-1]
    ready = ready_ref.shape[0]
    pieces = sems.shape[0] - 1
    copies = fetches(neigh_two_hbm.at[pl.ds(ready, held.shape[0])], held, sems.at[pl.ds(0, pieces)])
    last = pltpu.make_async_copy(final_hbm, final_ref, sems.at[pieces])
    for copy in (*copies, last):
        copy.start()
    far = far_ref[...]
    other = jnp.maximum(base_ref[...].astype(F32) + dot(load_rows(answer_ref), neigh_one_ref[...]), 0.0).astype(BF16)
    mean = over_count(dot(far[:, : other.shape[0]], other), far)
    final = dot(mean[:, :ready], ready_ref[...]) + dot_fetched(mean[:, ready:], held, copies)
    last.wait()
    final = (final + final_ref[...]).astype(BF16)
    capacity = outs[0].shape[0]
    for q, ref in enumerate(outs):
        ref[...] = final[q * capacity : (q + 1) * capacity]


def scatter_kernel(place_ref, *refs):
    out_ref = refs[-1]
    arrived = jnp.concatenate([ref[...] for ref in refs[:-1]], axis=0)
    out_ref[...] = dot(place_ref[...], arrived).astype(BF16)


def compute(features, neighbours, neighbour_mask, layer2_position, self_weight1, neigh_weight1, self_weight2, neigh_weight2):
    rows, degree = neighbours.shape
    members = lax.axis_size("dev")
    peers = lax.axis_size("grp") * members
    width_in, width = self_weight1.shape
    steps = members // 2
    capacity = rows // steps
    size = peers * CAP
    early = width // 2
    shape = jax.ShapeDtypeStruct
    copies = pltpu.SemaphoreType.DMA

    pos = layer2_position.reshape(1, rows)
    groups = peers // members
    mates = 2 * groups

    def shifts(by):
        return [(i, (i + by) % members) for i in range(members)]

    def across(by):
        return [(i, i ^ by) for i in range(groups)]

    pairs = [(i, i ^ 1) for i in range(members)]
    tables = [features] + [lax.ppermute(features, "grp", across(m)) for m in range(1, groups)]
    others = [lax.ppermute(t, "dev", pairs) for t in tables]
    key, local, span, *asks = call(
        functools.partial(ask_kernel, groups, members),
        (
            shape((degree, rows), I32),
            shape((degree, rows), I32),
            shape((2, peers, rows), I32),
            *(shape((mates, rows), I32) for _ in range(steps)),
        ),
        (neighbours.T, neighbour_mask.T, pos),
        (),
        [pltpu.VMEM((degree, rows), I32), pltpu.VMEM((degree, rows), I32), pltpu.VMEM((1, rows), I32), copies((3,))],
        2 * peers * rows * rows,
    )
    asked = [asks[0]] + [lax.ppermute(asks[q], "dev", shifts(2 * q)) for q in range(1, steps)]
    near, far, order, table = call(
        functools.partial(plan_kernel, peers, degree),
        (
            shape((rows, rows), BF16),
            shape((rows, size + 8), BF16),
            shape((size, size), BF16),
            shape((rows, width_in), BF16),
        ),
        (features,),
        (key, local, span),
        [copies((1,))],
        2 * size * size * rows,
        limit=40 << 20,
    )
    by_mate = call(
        functools.partial(sort_kernel, groups),
        tuple(shape((2 * steps, rows), I32) for _ in range(groups)),
        (),
        asks,
        [],
        2 * peers * peers * rows,
    )
    kept_asks = jnp.concatenate([by_mate[0]] + [lax.ppermute(by_mate[m], "grp", across(m)) for m in range(1, groups)])
    passed_asks = lax.ppermute(kept_asks, "dev", pairs)
    replies = call(
        functools.partial(serve_kernel, groups, steps),
        tuple(shape((mates * CAP, width_in), BF16) for _ in range(steps)),
        (),
        (order, *asked, *(t for pair in zip([table, *tables[1:]], others) for t in pair)),
        [],
        2 * size * rows * mates * width_in,
    )
    answers = [replies[0]] + [lax.ppermute(replies[q], "dev", shifts(-2 * q)) for q in range(1, steps)]
    lines = call(
        line_kernel,
        tuple(shape((mates, rows), I32) for _ in range(steps)),
        (),
        (kept_asks, passed_asks),
        [],
        2 * peers * peers * rows,
    )
    wanted = [lines[0]] + [lax.ppermute(lines[q], "dev", shifts(2 * q)) for q in range(1, steps)]
    pick = call(
        functools.partial(pick_kernel, members), shape((size, rows), BF16), (), wanted, [], 2 * size * size * rows
    )
    kept, mean, reply_two = call(
        layer_one_kernel,
        (
            shape((size, width_in), BF16),
            shape((rows, width_in), BF16),
            shape((peers, CAP // 2, 2, width_in), BF16),
        ),
        (),
        (table, near, far, pick, *answers),
        [pltpu.VMEM((size, width_in), BF16), pltpu.VMEM((rows, width_in), BF16), copies((2,))],
        2 * rows * width_in * (size + rows) + 2 * size * rows * width_in,
        away=2,
    )
    answer_two = lax.all_to_all(reply_two, BOTH, 0, 0, tiled=True)
    final, place, base, far_moved, weight, ready = call(
        functools.partial(between_kernel, groups, members),
        (
            shape((rows, width), F32),
            shape((rows, rows), BF16),
            shape((size, width), BF16),
            shape((rows, size + 8), BF16),
            shape((width_in, width), BF16),
            shape((early, width), BF16),
        ),
        (self_weight1, neigh_weight1, self_weight2, neigh_weight2, pos, features, kept, mean),
        (near, far, *asked),
        [
            pltpu.VMEM((width_in, width), BF16),
            pltpu.VMEM((width, width), BF16),
            pltpu.VMEM((width - early, width), BF16),
            pltpu.VMEM((rows, width_in), BF16),
            pltpu.VMEM((size, width_in), BF16),
            pltpu.VMEM((rows, width_in), BF16),
            pltpu.VMEM((rows, width), F32),
            pltpu.VMEM((rows, rows), BF16),
            pltpu.VMEM((1, rows), I32),
            copies((11,)),
        ],
        2 * width * (rows * (2 * width_in + rows + 2 * width) + size * width_in),
        limit=48 << 20,
        away=2,
    )
    finals = call(
        layer_two_kernel,
        tuple(shape((capacity, width), BF16) for _ in range(steps)),
        (neigh_weight2, final),
        (weight, ready, base, answer_two, far_moved),
        [pltpu.VMEM((width - early, width), BF16), pltpu.VMEM((rows, width), F32), copies((3,))],
        2 * width * (size * width_in + rows * (size + width)),
        limit=48 << 20,
    )
    arrived = [finals[0]]
    for q in range(1, steps):
        arrived.append(lax.ppermute(finals[q], "dev", shifts(2 * q)))
    return call(scatter_kernel, shape((rows, width), BF16), (), (place, *arrived), [], 2 * rows * rows * width)


def solution(mesh):
    return jax.shard_map(
        compute,
        mesh=mesh,
        in_specs=(
            P(BOTH, None),
            P(BOTH, None),
            P(BOTH, None),
            P(BOTH),
            P(),
            P(),
            P(),
            P(),
        ),
        out_specs=P(BOTH, None),
        check_vma=False,
    )
```

```python
import functools

import jax
import jax.numpy as jnp
from jax import lax
from jax.experimental import pallas as pl
from jax.experimental.pallas import tpu as pltpu
from jax.sharding import PartitionSpec as P

CAP = 6
BOTH = ("grp", "dev")
F32 = jnp.float32
BF16 = jnp.bfloat16
I32 = jnp.int32


def divide(values, by):
    if by & (by - 1) == 0:
        return values >> (by.bit_length() - 1)
    return (values * (-(-(1 << 16) // by))) >> 16


def iota(shape, dim):
    return lax.broadcasted_iota(I32, shape, dim)


def bits(condition):
    return jnp.where(condition, 1.0, 0.0)


def earlier(count):
    return bits(iota((count, count), 0) < iota((count, count), 1)).astype(BF16)


def dot(left, right):
    return jnp.dot(left, right, preferred_element_type=F32)


def dot_lanes(left, right):
    return lax.dot_general(left, right, (((1,), (1,)), ((), ())), preferred_element_type=F32)


def near_by(n):
    return [pl.BlockSpec(memory_space=pltpu.VMEM)] * n


def far_off(n):
    return [pl.BlockSpec(memory_space=pltpu.HBM)] * n


def call(kernel, outs, remote, operands, scratch, flops, name, limit=24 << 20, away=0):
    single = not isinstance(outs, tuple)
    leaves = (outs,) if single else outs
    moved = sum(a.size * a.dtype.itemsize for a in (*remote, *operands, *leaves))
    return pl.pallas_call(
        kernel,
        out_shape=outs if single else (*(pltpu.HBM(a.shape, a.dtype) for a in leaves[:away]), *leaves[away:]),
        in_specs=far_off(len(remote)) + near_by(len(operands)),
        out_specs=near_by(1)[0] if single else far_off(away) + near_by(len(leaves) - away),
        scratch_shapes=scratch,
        compiler_params=pltpu.CompilerParams(vmem_limit_bytes=limit),
        cost_estimate=pl.CostEstimate(flops=flops, bytes_accessed=moved, transcendentals=0),
        name=name,
    )(*(pltpu.with_memory_space_constraint(a, pltpu.HBM) for a in remote), *operands)


def fetches(weight_ref, held, sems):
    pieces = sems.shape[0]
    depth = weight_ref.shape[0] // pieces
    return [
        pltpu.make_async_copy(
            weight_ref.at[pl.ds(i * depth, depth)], held.at[pl.ds(i * depth, depth)], sems.at[i]
        )
        for i in range(pieces)
    ]


def dot_fetched(left, held, copies):
    depth = held.shape[0] // len(copies)
    result = None
    for i, copy in enumerate(copies):
        copy.wait()
        part = dot(left[:, i * depth : (i + 1) * depth], held[i * depth : (i + 1) * depth])
        result = part if result is None else result + part
    return result


def ask_kernel(
    members, peers, ids_hbm, mask_hbm, pos_hbm, features_hbm, ask_ref, near_ref, far_ref, order_ref, features_ref, ids, mask, pos_ref, sems
):
    degree, rows = ids.shape
    copies = [
        pltpu.make_async_copy(ids_hbm, ids, sems.at[0]),
        pltpu.make_async_copy(mask_hbm, mask, sems.at[1]),
        pltpu.make_async_copy(pos_hbm, pos_ref, sems.at[2]),
    ]
    table = pltpu.make_async_copy(features_hbm, features_ref, sems.at[3])
    for copy in (*copies, table):
        copy.start()
    own = lax.axis_index("grp") * members + lax.axis_index("dev")
    peer = iota((peers, rows), 0)
    prefix = earlier(rows)
    for copy in copies:
        copy.wait()
    slots = jnp.where(mask[...] > 0, ids[...], -1)
    owner = divide(jnp.maximum(slots, 0), rows)
    row = slots - owner * rows
    live = slots >= 0
    here = owner == own
    key = jnp.where(live & jnp.logical_not(here), owner, -1)
    half = CAP // 2
    width = (rows - 1).bit_length()
    top = width * (half - 1)
    low = jnp.zeros((peers, rows), I32)
    high = jnp.zeros((peers, rows), I32)
    total = jnp.zeros((peers, rows), I32)
    for s in range(degree):
        hit = key[s : s + 1] == peer
        high = jnp.where(hit, (high << width) | (low >> top), high)
        low = jnp.where(hit, ((low & ((1 << top) - 1)) << width) | row[s : s + 1], low)
        total += jnp.where(hit, 1, 0)
    before = dot(total.astype(F32).astype(BF16), prefix).astype(I32)
    packed = [jnp.where(before == 0, low, 0), jnp.where(before == 0, high, jnp.where(before == half, low, 0))]
    for k in range(1, half):
        shift, rest = width * k, width * (half - k)
        inside = before == k
        packed[0] = jnp.where(inside, (low & ((1 << rest) - 1)) << shift, packed[0])
        packed[1] = jnp.where(inside, (high << shift) | (low >> rest), packed[1])
        packed[1] = jnp.where(before == half + k, low << shift, packed[1])
    lane = iota((peers, rows), 1)
    wanted = jnp.zeros((peers, rows), I32)
    for w, word in enumerate(packed):
        word = jnp.broadcast_to(jnp.sum(word.astype(F32), axis=1, keepdims=True).astype(I32), (peers, rows))
        for k in range(half):
            wanted = jnp.where(lane == w * half + k, (word >> (width * k)) & ((1 << width) - 1), wanted)
    pos = pos_ref[...]
    place = jnp.where(divide(pos, rows) == peer, pos - divide(pos, rows) * rows + 1, 0)
    ask_ref[...] = (place + wanted * (2 * rows)).reshape(peers, 1, rows)
    local = jnp.where(live & here, row, -1)
    node = iota((rows, rows), 0)
    near = jnp.zeros((rows, rows), F32)
    for s in range(degree):
        near += bits(local[s : s + 1] == node)
    near_ref[...] = near.T.astype(BF16)
    far = [bits((before <= k) & (k < before + total)).astype(BF16) for k in range(CAP)]
    far = jnp.concatenate(far, axis=0)
    size = peers * CAP
    line = iota((size, size), 0)
    device = divide(line, CAP)
    order = bits(iota((size, size), 1) == (line - device * CAP) * peers + device).astype(BF16)
    order_ref[...] = order
    far_ref[:, :size] = dot(order, far).T.astype(BF16)
    count = jnp.broadcast_to(jnp.sum(bits(live), axis=0, keepdims=True), (rows, rows)).T.astype(BF16)
    far_ref[:, size:] = count[:, : far_ref.shape[1] - size]
    table.wait()


def store_rows(reply_ref, rows):
    peers, pairs, two, width = reply_ref.shape
    reply_ref[...] = rows.reshape(peers, pairs, two, width)


def load_rows(answer_ref):
    peers, pairs, two, width = answer_ref.shape
    return answer_ref[...].reshape(peers * pairs * two, width)


def serve_kernel(asked_ref, order_ref, source_ref, reply_ref, pick_ref):
    peers, _, rows = asked_ref.shape
    asked = asked_ref[...].reshape(peers, rows)
    wanted = divide(asked, 2 * rows)
    lane = iota((peers, rows), 1)
    picks = [bits(wanted[:, k : k + 1] == lane).astype(BF16) for k in range(CAP)]
    pick = dot(order_ref[...], jnp.concatenate(picks, axis=0)).astype(BF16)
    pick_ref[...] = pick
    store_rows(reply_ref, dot(pick, source_ref[...]).astype(BF16))


def over_count(summed, far):
    size = far.shape[1] - 8
    return (summed / far[:, size : size + 1].astype(F32)).astype(BF16)


def layer_one_kernel(
    features_ref, near_ref, answer_ref, far_ref, pick_ref, answer_hbm, mean_hbm, reply_ref, mean_ref, sems
):
    kept = pltpu.make_async_copy(answer_ref, answer_hbm, sems.at[0])
    kept.start()
    answer = load_rows(answer_ref)
    far = far_ref[...]
    mean = over_count(dot(near_ref[...], features_ref[...]) + dot(far[:, : answer.shape[0]], answer), far)
    mean_ref[...] = mean
    saved = pltpu.make_async_copy(mean_ref, mean_hbm, sems.at[1])
    saved.start()
    store_rows(reply_ref, dot(pick_ref[...], mean).astype(BF16))
    kept.wait()
    saved.wait()


def between_kernel(
    members, self_one_hbm, neigh_one_hbm, self_two_hbm, neigh_two_hbm, pos_hbm, features_hbm, answer_hbm, mean_hbm,
    near_ref, far_ref, asked_ref,
    final_hbm, place_hbm, base_ref, far_moved_ref, neigh_one_ref, ready_ref,
    held_one, held_two, rest, features_ref, answer_ref, mean_ref, final_ref, place_ref, pos_ref, sems,
):
    ready = ready_ref.shape[0]
    copies = [
        pltpu.make_async_copy(pos_hbm, pos_ref, sems.at[0]),
        pltpu.make_async_copy(self_one_hbm, held_one, sems.at[1]),
        pltpu.make_async_copy(neigh_one_hbm, neigh_one_ref, sems.at[2]),
        pltpu.make_async_copy(self_two_hbm, held_two, sems.at[3]),
        pltpu.make_async_copy(neigh_two_hbm.at[pl.ds(0, ready)], ready_ref, sems.at[4]),
        pltpu.make_async_copy(neigh_two_hbm.at[pl.ds(ready, rest.shape[0])], rest, sems.at[5]),
    ]
    inputs = [
        pltpu.make_async_copy(features_hbm, features_ref, sems.at[6]),
        pltpu.make_async_copy(answer_hbm, answer_ref, sems.at[7]),
        pltpu.make_async_copy(mean_hbm, mean_ref, sems.at[8]),
    ]
    for copy in (*inputs, *copies):
        copy.start()
    rows = features_ref.shape[0]
    capacity = 2 * rows // members
    me = lax.axis_index("dev")
    first = lax.axis_index("grp") * members
    line = iota((rows, rows), 0)
    step = divide(line, capacity)
    rank = line - step * capacity
    target = me + 2 * step
    target = jnp.where(target >= members, target - members, target)
    prefix = earlier(rows)
    copies[0].wait()
    goes = target == divide(pos_ref[...], rows) - first
    before = dot(bits(goes).astype(BF16), prefix).astype(I32)
    move = bits(goes & (before == rank)).astype(BF16)
    near = dot(move, near_ref[...]).astype(BF16)
    far = dot(move, far_ref[...]).astype(BF16)
    far_moved_ref[...] = far
    place = jnp.zeros((rows, rows), F32)
    for q in range(members // 2):
        source = me - 2 * q
        source = first + jnp.where(source < 0, source + members, source)
        sent = asked_ref[source] & (2 * rows - 1)
        valid = jnp.broadcast_to(sent > 0, (rows, rows))
        before = dot(bits(valid).astype(BF16), prefix).astype(I32)
        lands = bits(sent - 1 == line).astype(BF16)
        comes = bits(valid & (step == q) & (before == rank)).astype(BF16)
        place += dot_lanes(lands, comes)
    place_ref[...] = place.astype(BF16)
    placed = pltpu.make_async_copy(place_ref, place_hbm, sems.at[9])
    placed.start()
    for copy in (*inputs, copies[1]):
        copy.wait()
    own = dot(features_ref[...], held_one[...])
    base_ref[...] = dot(load_rows(answer_ref), held_one[...]).astype(BF16)
    copies[2].wait()
    hidden = jnp.maximum(own + dot(mean_ref[...], neigh_one_ref[...]), 0.0).astype(BF16)
    mean = over_count(dot(near, hidden), far)
    moved = dot(move, hidden).astype(BF16)
    copies[3].wait()
    final = dot(moved, held_two[...])
    copies[4].wait()
    final += dot(mean[:, :ready], ready_ref[...])
    copies[5].wait()
    final_ref[...] = final + dot(mean[:, ready:], rest[...])
    away = pltpu.make_async_copy(final_ref, final_hbm, sems.at[10])
    away.start()
    away.wait()
    placed.wait()


def layer_two_kernel(neigh_two_hbm, final_hbm, neigh_one_ref, ready_ref, base_ref, answer_ref, far_ref, *refs):
    outs, held, final_ref, sems = refs[:-3], refs[-3], refs[-2], refs[-1]
    ready = ready_ref.shape[0]
    pieces = sems.shape[0] - 1
    copies = fetches(neigh_two_hbm.at[pl.ds(ready, held.shape[0])], held, sems.at[pl.ds(0, pieces)])
    last = pltpu.make_async_copy(final_hbm, final_ref, sems.at[pieces])
    for copy in (*copies, last):
        copy.start()
    far = far_ref[...]
    other = jnp.maximum(base_ref[...].astype(F32) + dot(load_rows(answer_ref), neigh_one_ref[...]), 0.0).astype(BF16)
    mean = over_count(dot(far[:, : other.shape[0]], other), far)
    final = dot(mean[:, :ready], ready_ref[...]) + dot_fetched(mean[:, ready:], held, copies)
    last.wait()
    final = (final + final_ref[...]).astype(BF16)
    capacity = outs[0].shape[0]
    for q, ref in enumerate(outs):
        ref[...] = final[q * capacity : (q + 1) * capacity]


def scatter_kernel(place_ref, *refs):
    out_ref = refs[-1]
    arrived = jnp.concatenate([ref[...] for ref in refs[:-1]], axis=0)
    out_ref[...] = dot(place_ref[...], arrived).astype(BF16)


def body(features, neighbours, neighbour_mask, layer2_position, self_weight1, neigh_weight1, self_weight2, neigh_weight2):
    rows, degree = neighbours.shape
    members = lax.axis_size("dev")
    peers = lax.axis_size("grp") * members
    width_in, width = self_weight1.shape
    steps = members // 2
    capacity = rows // steps
    size = peers * CAP
    early = width // 2
    shape = jax.ShapeDtypeStruct
    copies = pltpu.SemaphoreType.DMA

    pos = layer2_position.reshape(1, rows)
    ask, near, far, order, table = call(
        functools.partial(ask_kernel, members, peers),
        (
            shape((peers, 1, rows), I32),
            shape((rows, rows), BF16),
            shape((rows, size + 8), BF16),
            shape((size, size), BF16),
            shape((rows, width_in), BF16),
        ),
        (neighbours.T, neighbour_mask.T, pos, features),
        (),
        [pltpu.VMEM((degree, rows), I32), pltpu.VMEM((degree, rows), I32), pltpu.VMEM((1, rows), I32), copies((4,))],
        2 * size * size * rows,
        "ask",
        limit=40 << 20,
    )
    asked = lax.all_to_all(ask, BOTH, 0, 0, tiled=True)
    reply, pick = call(
        serve_kernel,
        (shape((peers, CAP // 2, 2, width_in), BF16), shape((size, rows), BF16)),
        (),
        (asked, order, table),
        [],
        2 * size * rows * width_in,
        "serve",
    )
    answer = lax.all_to_all(reply, BOTH, 0, 0, tiled=True)
    kept, mean, reply_two = call(
        layer_one_kernel,
        (
            shape((peers, CAP // 2, 2, width_in), BF16),
            shape((rows, width_in), BF16),
            shape((peers, CAP // 2, 2, width_in), BF16),
        ),
        (),
        (table, near, answer, far, pick),
        [pltpu.VMEM((rows, width_in), BF16), copies((2,))],
        2 * rows * width_in * (size + rows) + 2 * size * rows * width_in,
        "layer_one",
        away=2,
    )
    answer_two = lax.all_to_all(reply_two, BOTH, 0, 0, tiled=True)
    final, place, base, far_moved, weight, ready = call(
        functools.partial(between_kernel, members),
        (
            shape((rows, width), F32),
            shape((rows, rows), BF16),
            shape((size, width), BF16),
            shape((rows, size + 8), BF16),
            shape((width_in, width), BF16),
            shape((early, width), BF16),
        ),
        (self_weight1, neigh_weight1, self_weight2, neigh_weight2, pos, features, kept, mean),
        (near, far, asked),
        [
            pltpu.VMEM((width_in, width), BF16),
            pltpu.VMEM((width, width), BF16),
            pltpu.VMEM((width - early, width), BF16),
            pltpu.VMEM((rows, width_in), BF16),
            pltpu.VMEM((peers, CAP // 2, 2, width_in), BF16),
            pltpu.VMEM((rows, width_in), BF16),
            pltpu.VMEM((rows, width), F32),
            pltpu.VMEM((rows, rows), BF16),
            pltpu.VMEM((1, rows), I32),
            copies((11,)),
        ],
        2 * width * (rows * (2 * width_in + rows + 2 * width) + size * width_in),
        "between",
        limit=48 << 20,
        away=2,
    )
    finals = call(
        layer_two_kernel,
        tuple(shape((capacity, width), BF16) for _ in range(steps)),
        (neigh_weight2, final),
        (weight, ready, base, answer_two, far_moved),
        [pltpu.VMEM((width - early, width), BF16), pltpu.VMEM((rows, width), F32), copies((3,))],
        2 * width * (size * width_in + rows * (size + width)),
        "layer_two",
        limit=48 << 20,
    )
    arrived = [finals[0]]
    for q in range(1, steps):
        arrived.append(lax.ppermute(finals[q], "dev", [(i, (i + 2 * q) % members) for i in range(members)]))
    return call(
        scatter_kernel,
        shape((rows, width), BF16),
        (),
        (place, *arrived),
        [],
        2 * rows * rows * width,
        "scatter",
    )


def solution(mesh):
    return jax.shard_map(
        body,
        mesh=mesh,
        in_specs=(
            P(BOTH, None),
            P(BOTH, None),
            P(BOTH, None),
            P(BOTH),
            P(),
            P(),
            P(),
            P(),
        ),
        out_specs=P(BOTH, None),
        check_vma=False,
    )
```

```python
import functools

import jax
import jax.numpy as jnp
from jax import lax
from jax.experimental import pallas as pl
from jax.experimental.pallas import tpu as pltpu
from jax.sharding import PartitionSpec as P

CAP = 6
BOTH = ("grp", "dev")
F32 = jnp.float32
BF16 = jnp.bfloat16
I32 = jnp.int32


def divide(values, by):
    if by & (by - 1) == 0:
        return values >> (by.bit_length() - 1)
    return (values * (-(-(1 << 16) // by))) >> 16


def iota(shape, dim):
    return lax.broadcasted_iota(I32, shape, dim)


def bits(condition):
    return jnp.where(condition, 1.0, 0.0)


def earlier(count):
    return bits(iota((count, count), 0) < iota((count, count), 1)).astype(BF16)


def dot(left, right):
    return jnp.dot(left, right, preferred_element_type=F32)


def dot_lanes(left, right):
    return lax.dot_general(left, right, (((1,), (1,)), ((), ())), preferred_element_type=F32)


def near_by(n):
    return [pl.BlockSpec(memory_space=pltpu.VMEM)] * n


def far_off(n):
    return [pl.BlockSpec(memory_space=pltpu.HBM)] * n


def call(kernel, outs, remote, operands, scratch, flops, name, limit=24 << 20, away=0):
    single = not isinstance(outs, tuple)
    leaves = (outs,) if single else outs
    moved = sum(a.size * a.dtype.itemsize for a in (*remote, *operands, *leaves))
    return pl.pallas_call(
        kernel,
        out_shape=outs if single else (*(pltpu.HBM(a.shape, a.dtype) for a in leaves[:away]), *leaves[away:]),
        in_specs=far_off(len(remote)) + near_by(len(operands)),
        out_specs=near_by(1)[0] if single else far_off(away) + near_by(len(leaves) - away),
        scratch_shapes=scratch,
        compiler_params=pltpu.CompilerParams(vmem_limit_bytes=limit),
        cost_estimate=pl.CostEstimate(flops=flops, bytes_accessed=moved, transcendentals=0),
        name=name,
    )(*(pltpu.with_memory_space_constraint(a, pltpu.HBM) for a in remote), *operands)


def fetches(weight_ref, held, sems):
    pieces = sems.shape[0]
    depth = weight_ref.shape[0] // pieces
    return [
        pltpu.make_async_copy(
            weight_ref.at[pl.ds(i * depth, depth)], held.at[pl.ds(i * depth, depth)], sems.at[i]
        )
        for i in range(pieces)
    ]


def dot_fetched(left, held, copies):
    depth = held.shape[0] // len(copies)
    result = None
    for i, copy in enumerate(copies):
        copy.wait()
        part = dot(left[:, i * depth : (i + 1) * depth], held[i * depth : (i + 1) * depth])
        result = part if result is None else result + part
    return result


def ask_kernel(
    members, peers, ids_hbm, mask_hbm, pos_hbm, features_hbm, ask_ref, near_ref, far_ref, order_ref, features_ref, ids, mask, pos_ref, sems
):
    degree, rows = ids.shape
    copies = [
        pltpu.make_async_copy(ids_hbm, ids, sems.at[0]),
        pltpu.make_async_copy(mask_hbm, mask, sems.at[1]),
        pltpu.make_async_copy(pos_hbm, pos_ref, sems.at[2]),
    ]
    table = pltpu.make_async_copy(features_hbm, features_ref, sems.at[3])
    for copy in (*copies, table):
        copy.start()
    own = lax.axis_index("grp") * members + lax.axis_index("dev")
    peer = iota((peers, rows), 0)
    prefix = earlier(rows)
    for copy in copies:
        copy.wait()
    slots = jnp.where(mask[...] > 0, ids[...], -1)
    owner = divide(jnp.maximum(slots, 0), rows)
    row = slots - owner * rows
    live = slots >= 0
    here = owner == own
    key = jnp.where(live & jnp.logical_not(here), owner, -1)
    half = CAP // 2
    width = (rows - 1).bit_length()
    top = width * (half - 1)
    low = jnp.zeros((peers, rows), I32)
    high = jnp.zeros((peers, rows), I32)
    total = jnp.zeros((peers, rows), I32)
    for s in range(degree):
        hit = key[s : s + 1] == peer
        high = jnp.where(hit, (high << width) | (low >> top), high)
        low = jnp.where(hit, ((low & ((1 << top) - 1)) << width) | row[s : s + 1], low)
        total += jnp.where(hit, 1, 0)
    before = dot(total.astype(F32).astype(BF16), prefix).astype(I32)
    packed = [jnp.where(before == 0, low, 0), jnp.where(before == 0, high, jnp.where(before == half, low, 0))]
    for k in range(1, half):
        shift, rest = width * k, width * (half - k)
        inside = before == k
        packed[0] = jnp.where(inside, (low & ((1 << rest) - 1)) << shift, packed[0])
        packed[1] = jnp.where(inside, (high << shift) | (low >> rest), packed[1])
        packed[1] = jnp.where(before == half + k, low << shift, packed[1])
    lane = iota((peers, rows), 1)
    wanted = jnp.zeros((peers, rows), I32)
    for w, word in enumerate(packed):
        word = jnp.broadcast_to(jnp.sum(word.astype(F32), axis=1, keepdims=True).astype(I32), (peers, rows))
        for k in range(half):
            wanted = jnp.where(lane == w * half + k, (word >> (width * k)) & ((1 << width) - 1), wanted)
    pos = pos_ref[...]
    place = jnp.where(divide(pos, rows) == peer, pos - divide(pos, rows) * rows + 1, 0)
    ask_ref[...] = (place + wanted * (2 * rows)).reshape(peers, 1, rows)
    local = jnp.where(live & here, row, -1)
    node = iota((rows, rows), 0)
    near = jnp.zeros((rows, rows), F32)
    for s in range(degree):
        near += bits(local[s : s + 1] == node)
    near_ref[...] = near.T.astype(BF16)
    far = [bits((before <= k) & (k < before + total)).astype(BF16) for k in range(CAP)]
    far = jnp.concatenate(far, axis=0)
    size = peers * CAP
    line = iota((size, size), 0)
    device = divide(line, CAP)
    order = bits(iota((size, size), 1) == (line - device * CAP) * peers + device).astype(BF16)
    order_ref[...] = order
    far_ref[:, :size] = dot(order, far).T.astype(BF16)
    count = jnp.broadcast_to(jnp.sum(bits(live), axis=0, keepdims=True), (rows, rows)).T.astype(BF16)
    far_ref[:, size:] = count[:, : far_ref.shape[1] - size]
    table.wait()


def store_rows(reply_ref, rows):
    peers, pairs, two, width = reply_ref.shape
    reply_ref[...] = rows.reshape(peers, pairs, two, width)


def load_rows(answer_ref):
    peers, pairs, two, width = answer_ref.shape
    return answer_ref[...].reshape(peers * pairs * two, width)


def serve_kernel(asked_ref, order_ref, source_ref, reply_ref, pick_ref):
    peers, _, rows = asked_ref.shape
    asked = asked_ref[...].reshape(peers, rows)
    wanted = divide(asked, 2 * rows)
    lane = iota((peers, rows), 1)
    picks = [bits(wanted[:, k : k + 1] == lane).astype(BF16) for k in range(CAP)]
    pick = dot(order_ref[...], jnp.concatenate(picks, axis=0)).astype(BF16)
    pick_ref[...] = pick
    store_rows(reply_ref, dot(pick, source_ref[...]).astype(BF16))


def over_count(summed, far):
    size = far.shape[1] - 8
    return (summed / far[:, size : size + 1].astype(F32)).astype(BF16)


def layer_one_kernel(
    features_ref, near_ref, answer_ref, far_ref, pick_ref, answer_hbm, mean_hbm, reply_ref, mean_ref, sems
):
    kept = pltpu.make_async_copy(answer_ref, answer_hbm, sems.at[0])
    kept.start()
    answer = load_rows(answer_ref)
    far = far_ref[...]
    mean = over_count(dot(near_ref[...], features_ref[...]) + dot(far[:, : answer.shape[0]], answer), far)
    mean_ref[...] = mean
    saved = pltpu.make_async_copy(mean_ref, mean_hbm, sems.at[1])
    saved.start()
    store_rows(reply_ref, dot(pick_ref[...], mean).astype(BF16))
    kept.wait()
    saved.wait()


def between_kernel(
    members, self_one_hbm, neigh_one_hbm, self_two_hbm, neigh_two_hbm, pos_hbm, features_hbm, answer_hbm, mean_hbm,
    near_ref, far_ref, asked_ref,
    final_hbm, place_hbm, base_ref, far_moved_ref, dense_ref, neigh_one_ref, ready_ref,
    held_one, held_two, rest, features_ref, answer_ref, mean_ref, final_ref, place_ref, pos_ref, sems,
):
    ready = ready_ref.shape[0]
    copies = [
        pltpu.make_async_copy(pos_hbm, pos_ref, sems.at[0]),
        pltpu.make_async_copy(self_one_hbm, held_one, sems.at[1]),
        pltpu.make_async_copy(neigh_one_hbm, neigh_one_ref, sems.at[2]),
        pltpu.make_async_copy(self_two_hbm, held_two, sems.at[3]),
        pltpu.make_async_copy(neigh_two_hbm.at[pl.ds(0, ready)], ready_ref, sems.at[4]),
        pltpu.make_async_copy(neigh_two_hbm.at[pl.ds(ready, rest.shape[0])], rest, sems.at[5]),
    ]
    inputs = [
        pltpu.make_async_copy(features_hbm, features_ref, sems.at[6]),
        pltpu.make_async_copy(answer_hbm, answer_ref, sems.at[7]),
        pltpu.make_async_copy(mean_hbm, mean_ref, sems.at[8]),
    ]
    for copy in (*inputs, *copies):
        copy.start()
    rows = features_ref.shape[0]
    capacity = 2 * rows // members
    me = lax.axis_index("dev")
    first = lax.axis_index("grp") * members
    line = iota((rows, rows), 0)
    step = divide(line, capacity)
    rank = line - step * capacity
    target = me + 2 * step
    target = jnp.where(target >= members, target - members, target)
    prefix = earlier(rows)
    copies[0].wait()
    goes = target == divide(pos_ref[...], rows) - first
    before = dot(bits(goes).astype(BF16), prefix).astype(I32)
    move = bits(goes & (before == rank)).astype(BF16)
    near = dot(move, near_ref[...]).astype(BF16)
    far = dot(move, far_ref[...]).astype(BF16)
    size = far.shape[1] - 8
    used = jnp.sum(far_ref[:, :size].astype(F32), axis=0, keepdims=True) > 0.0
    used = jnp.broadcast_to(used, dense_ref.shape)
    seats = dot(bits(used).astype(BF16), earlier(size)).astype(I32)
    dense = bits(used & (seats == iota(used.shape, 0))).astype(BF16)
    dense_ref[...] = dense
    held = dense.shape[0]
    far_moved_ref[:, :held] = dot_lanes(far[:, :size], dense).astype(BF16)
    far_moved_ref[:, held:] = far[:, size:]
    place = jnp.zeros((rows, rows), F32)
    for q in range(members // 2):
        source = me - 2 * q
        source = first + jnp.where(source < 0, source + members, source)
        sent = asked_ref[source] & (2 * rows - 1)
        valid = jnp.broadcast_to(sent > 0, (rows, rows))
        before = dot(bits(valid).astype(BF16), prefix).astype(I32)
        lands = bits(sent - 1 == line).astype(BF16)
        comes = bits(valid & (step == q) & (before == rank)).astype(BF16)
        place += dot_lanes(lands, comes)
    place_ref[...] = place.astype(BF16)
    placed = pltpu.make_async_copy(place_ref, place_hbm, sems.at[9])
    placed.start()
    for copy in (*inputs, copies[1]):
        copy.wait()
    own = dot(features_ref[...], held_one[...])
    base_ref[...] = dot(dot(dense, load_rows(answer_ref)).astype(BF16), held_one[...]).astype(BF16)
    copies[2].wait()
    hidden = jnp.maximum(own + dot(mean_ref[...], neigh_one_ref[...]), 0.0).astype(BF16)
    mean = over_count(dot(near, hidden), far)
    moved = dot(move, hidden).astype(BF16)
    copies[3].wait()
    final = dot(moved, held_two[...])
    copies[4].wait()
    final += dot(mean[:, :ready], ready_ref[...])
    copies[5].wait()
    final_ref[...] = (final + dot(mean[:, ready:], rest[...])).astype(BF16)
    away = pltpu.make_async_copy(final_ref, final_hbm, sems.at[10])
    away.start()
    away.wait()
    placed.wait()


def layer_two_kernel(neigh_two_hbm, final_hbm, neigh_one_ref, ready_ref, base_ref, answer_ref, far_ref, dense_ref, *refs):
    outs, held, final_ref, sems = refs[:-3], refs[-3], refs[-2], refs[-1]
    ready = ready_ref.shape[0]
    pieces = sems.shape[0] - 1
    copies = fetches(neigh_two_hbm.at[pl.ds(ready, held.shape[0])], held, sems.at[pl.ds(0, pieces)])
    last = pltpu.make_async_copy(final_hbm, final_ref, sems.at[pieces])
    for copy in (*copies, last):
        copy.start()
    far = far_ref[...]
    answer = dot(dense_ref[...], load_rows(answer_ref)).astype(BF16)
    other = jnp.maximum(base_ref[...].astype(F32) + dot(answer, neigh_one_ref[...]), 0.0).astype(BF16)
    mean = over_count(dot(far[:, : other.shape[0]], other), far)
    final = dot(mean[:, :ready], ready_ref[...]) + dot_fetched(mean[:, ready:], held, copies)
    last.wait()
    final = (final + final_ref[...].astype(F32)).astype(BF16)
    capacity = outs[0].shape[0]
    for q, ref in enumerate(outs):
        ref[...] = final[q * capacity : (q + 1) * capacity]


def scatter_kernel(place_ref, *refs):
    out_ref = refs[-1]
    arrived = jnp.concatenate([ref[...] for ref in refs[:-1]], axis=0)
    out_ref[...] = dot(place_ref[...], arrived).astype(BF16)


def body(features, neighbours, neighbour_mask, layer2_position, self_weight1, neigh_weight1, self_weight2, neigh_weight2):
    rows, degree = neighbours.shape
    members = lax.axis_size("dev")
    peers = lax.axis_size("grp") * members
    width_in, width = self_weight1.shape
    steps = members // 2
    capacity = rows // steps
    size = peers * CAP
    early = width * 9 // 16
    held = -(-((peers - 1) * CAP // 2) // 16) * 16
    shape = jax.ShapeDtypeStruct
    copies = pltpu.SemaphoreType.DMA

    pos = layer2_position.reshape(1, rows)
    ask, near, far, order, table = call(
        functools.partial(ask_kernel, members, peers),
        (
            shape((peers, 1, rows), I32),
            shape((rows, rows), BF16),
            shape((rows, size + 8), BF16),
            shape((size, size), BF16),
            shape((rows, width_in), BF16),
        ),
        (neighbours.T, neighbour_mask.T, pos, features),
        (),
        [pltpu.VMEM((degree, rows), I32), pltpu.VMEM((degree, rows), I32), pltpu.VMEM((1, rows), I32), copies((4,))],
        2 * size * size * rows,
        "ask",
        limit=40 << 20,
    )
    asked = lax.all_to_all(ask, BOTH, 0, 0, tiled=True)
    reply, pick = call(
        serve_kernel,
        (shape((peers, CAP // 2, 2, width_in), BF16), shape((size, rows), BF16)),
        (),
        (asked, order, table),
        [],
        2 * size * rows * width_in,
        "serve",
    )
    answer = lax.all_to_all(reply, BOTH, 0, 0, tiled=True)
    kept, mean, reply_two = call(
        layer_one_kernel,
        (
            shape((peers, CAP // 2, 2, width_in), BF16),
            shape((rows, width_in), BF16),
            shape((peers, CAP // 2, 2, width_in), BF16),
        ),
        (),
        (table, near, answer, far, pick),
        [pltpu.VMEM((rows, width_in), BF16), copies((2,))],
        2 * rows * width_in * (size + rows) + 2 * size * rows * width_in,
        "layer_one",
        away=2,
    )
    answer_two = lax.all_to_all(reply_two, BOTH, 0, 0, tiled=True)
    final, place, base, far_moved, dense, weight, ready = call(
        functools.partial(between_kernel, members),
        (
            shape((rows, width), BF16),
            shape((rows, rows), BF16),
            shape((held, width), BF16),
            shape((rows, held + 8), BF16),
            shape((held, size), BF16),
            shape((width_in, width), BF16),
            shape((early, width), BF16),
        ),
        (self_weight1, neigh_weight1, self_weight2, neigh_weight2, pos, features, kept, mean),
        (near, far, asked),
        [
            pltpu.VMEM((width_in, width), BF16),
            pltpu.VMEM((width, width), BF16),
            pltpu.VMEM((width - early, width), BF16),
            pltpu.VMEM((rows, width_in), BF16),
            pltpu.VMEM((peers, CAP // 2, 2, width_in), BF16),
            pltpu.VMEM((rows, width_in), BF16),
            pltpu.VMEM((rows, width), BF16),
            pltpu.VMEM((rows, rows), BF16),
            pltpu.VMEM((1, rows), I32),
            copies((11,)),
        ],
        2 * width * (rows * (2 * width_in + rows + 2 * width) + size * width_in),
        "between",
        limit=48 << 20,
        away=2,
    )
    finals = call(
        layer_two_kernel,
        tuple(shape((capacity, width), BF16) for _ in range(steps)),
        (neigh_weight2, final),
        (weight, ready, base, answer_two, far_moved, dense),
        [pltpu.VMEM((width - early, width), BF16), pltpu.VMEM((rows, width), BF16), copies((3,))],
        2 * width * (size * width_in + rows * (size + width)),
        "layer_two",
        limit=48 << 20,
    )
    arrived = [finals[0]]
    for q in range(1, steps):
        arrived.append(lax.ppermute(finals[q], "dev", [(i, (i + 2 * q) % members) for i in range(members)]))
    return call(
        scatter_kernel,
        shape((rows, width), BF16),
        (),
        (place, *arrived),
        [],
        2 * rows * rows * width,
        "scatter",
    )


def solution(mesh):
    return jax.shard_map(
        body,
        mesh=mesh,
        in_specs=(
            P(BOTH, None),
            P(BOTH, None),
            P(BOTH, None),
            P(BOTH),
            P(),
            P(),
            P(),
            P(),
        ),
        out_specs=P(BOTH, None),
        check_vma=False,
    )
```

```python
import functools

import jax
import jax.numpy as jnp
from jax import lax
from jax.experimental import pallas as pl
from jax.experimental.pallas import tpu as pltpu
from jax.sharding import PartitionSpec as P

CAP = 6
BOTH = ("grp", "dev")
F32 = jnp.float32
BF16 = jnp.bfloat16
I32 = jnp.int32


def divide(values, by):
    if by & (by - 1) == 0:
        return values >> (by.bit_length() - 1)
    return (values * (-(-(1 << 16) // by))) >> 16


def iota(shape, dim):
    return lax.broadcasted_iota(I32, shape, dim)


def bits(condition):
    return jnp.where(condition, 1.0, 0.0)


def earlier(count):
    return bits(iota((count, count), 0) < iota((count, count), 1)).astype(BF16)


def dot(left, right):
    return jnp.dot(left, right, preferred_element_type=F32)


def dot_lanes(left, right):
    return lax.dot_general(left, right, (((1,), (1,)), ((), ())), preferred_element_type=F32)


def near_by(n):
    return [pl.BlockSpec(memory_space=pltpu.VMEM)] * n


def far_off(n):
    return [pl.BlockSpec(memory_space=pltpu.HBM)] * n


def call(kernel, outs, remote, operands, scratch, flops, name, limit=24 << 20, away=0):
    single = not isinstance(outs, tuple)
    leaves = (outs,) if single else outs
    moved = sum(a.size * a.dtype.itemsize for a in (*remote, *operands, *leaves))
    return pl.pallas_call(
        kernel,
        out_shape=outs if single else (*(pltpu.HBM(a.shape, a.dtype) for a in leaves[:away]), *leaves[away:]),
        in_specs=far_off(len(remote)) + near_by(len(operands)),
        out_specs=near_by(1)[0] if single else far_off(away) + near_by(len(leaves) - away),
        scratch_shapes=scratch,
        compiler_params=pltpu.CompilerParams(vmem_limit_bytes=limit),
        cost_estimate=pl.CostEstimate(flops=flops, bytes_accessed=moved, transcendentals=0),
        name=name,
    )(*(pltpu.with_memory_space_constraint(a, pltpu.HBM) for a in remote), *operands)


def fetches(weight_ref, held, sems):
    pieces = sems.shape[0]
    depth = weight_ref.shape[0] // pieces
    return [
        pltpu.make_async_copy(
            weight_ref.at[pl.ds(i * depth, depth)], held.at[pl.ds(i * depth, depth)], sems.at[i]
        )
        for i in range(pieces)
    ]


def dot_fetched(left, held, copies):
    depth = held.shape[0] // len(copies)
    result = None
    for i, copy in enumerate(copies):
        copy.wait()
        part = dot(left[:, i * depth : (i + 1) * depth], held[i * depth : (i + 1) * depth])
        result = part if result is None else result + part
    return result


def ask_kernel(
    members, peers, ids_hbm, mask_hbm, pos_hbm, features_hbm, ask_ref, near_ref, far_ref, order_ref, features_ref, ids, mask, pos_ref, sems
):
    degree, rows = ids.shape
    copies = [
        pltpu.make_async_copy(ids_hbm, ids, sems.at[0]),
        pltpu.make_async_copy(mask_hbm, mask, sems.at[1]),
        pltpu.make_async_copy(pos_hbm, pos_ref, sems.at[2]),
    ]
    table = pltpu.make_async_copy(features_hbm, features_ref, sems.at[3])
    for copy in (*copies, table):
        copy.start()
    own = lax.axis_index("grp") * members + lax.axis_index("dev")
    peer = iota((peers, rows), 0)
    prefix = earlier(rows)
    for copy in copies:
        copy.wait()
    slots = jnp.where(mask[...] > 0, ids[...], -1)
    owner = divide(jnp.maximum(slots, 0), rows)
    row = slots - owner * rows
    live = slots >= 0
    here = owner == own
    key = jnp.where(live & jnp.logical_not(here), owner, -1)
    half = CAP // 2
    width = (rows - 1).bit_length()
    top = width * (half - 1)
    low = jnp.zeros((peers, rows), I32)
    high = jnp.zeros((peers, rows), I32)
    total = jnp.zeros((peers, rows), I32)
    for s in range(degree):
        hit = key[s : s + 1] == peer
        high = jnp.where(hit, (high << width) | (low >> top), high)
        low = jnp.where(hit, ((low & ((1 << top) - 1)) << width) | row[s : s + 1], low)
        total += jnp.where(hit, 1, 0)
    before = dot(total.astype(F32).astype(BF16), prefix).astype(I32)
    packed = [jnp.where(before == 0, low, 0), jnp.where(before == 0, high, jnp.where(before == half, low, 0))]
    for k in range(1, half):
        shift, rest = width * k, width * (half - k)
        inside = before == k
        packed[0] = jnp.where(inside, (low & ((1 << rest) - 1)) << shift, packed[0])
        packed[1] = jnp.where(inside, (high << shift) | (low >> rest), packed[1])
        packed[1] = jnp.where(before == half + k, low << shift, packed[1])
    lane = iota((peers, rows), 1)
    wanted = jnp.zeros((peers, rows), I32)
    for w, word in enumerate(packed):
        word = jnp.broadcast_to(jnp.sum(word.astype(F32), axis=1, keepdims=True).astype(I32), (peers, rows))
        for k in range(half):
            wanted = jnp.where(lane == w * half + k, (word >> (width * k)) & ((1 << width) - 1), wanted)
    pos = pos_ref[...]
    place = jnp.where(divide(pos, rows) == peer, pos - divide(pos, rows) * rows + 1, 0)
    ask_ref[...] = (place + wanted * (2 * rows)).reshape(peers, 1, rows)
    local = jnp.where(live & here, row, -1)
    node = iota((rows, rows), 0)
    near = jnp.zeros((rows, rows), F32)
    for s in range(degree):
        near += bits(local[s : s + 1] == node)
    near_ref[...] = near.T.astype(BF16)
    far = [bits((before <= k) & (k < before + total)).astype(BF16) for k in range(CAP)]
    far = jnp.concatenate(far, axis=0)
    size = peers * CAP
    line = iota((size, size), 0)
    device = divide(line, CAP)
    order = bits(iota((size, size), 1) == (line - device * CAP) * peers + device).astype(BF16)
    order_ref[...] = order
    far_ref[:, :size] = dot(order, far).T.astype(BF16)
    count = jnp.broadcast_to(jnp.sum(bits(live), axis=0, keepdims=True), (rows, rows)).T.astype(BF16)
    far_ref[:, size:] = count[:, : far_ref.shape[1] - size]
    table.wait()


def store_rows(reply_ref, rows):
    peers, pairs, two, width = reply_ref.shape
    reply_ref[...] = rows.reshape(peers, pairs, two, width)


def load_rows(answer_ref):
    peers, pairs, two, width = answer_ref.shape
    return answer_ref[...].reshape(peers * pairs * two, width)


def serve_kernel(asked_ref, order_ref, source_ref, reply_ref, pick_ref):
    peers, _, rows = asked_ref.shape
    asked = asked_ref[...].reshape(peers, rows)
    wanted = divide(asked, 2 * rows)
    lane = iota((peers, rows), 1)
    picks = [bits(wanted[:, k : k + 1] == lane).astype(BF16) for k in range(CAP)]
    pick = dot(order_ref[...], jnp.concatenate(picks, axis=0)).astype(BF16)
    pick_ref[...] = pick
    store_rows(reply_ref, dot(pick, source_ref[...]).astype(BF16))


def over_count(summed, far):
    size = far.shape[1] - 8
    return (summed / far[:, size : size + 1].astype(F32)).astype(BF16)


def layer_one_kernel(
    features_ref, near_ref, answer_ref, far_ref, pick_ref, answer_hbm, mean_hbm, reply_hbm, mean_ref, reply_ref, sems
):
    kept = pltpu.make_async_copy(answer_ref, answer_hbm, sems.at[0])
    kept.start()
    answer = load_rows(answer_ref)
    far = far_ref[...]
    mean = over_count(dot(near_ref[...], features_ref[...]) + dot(far[:, : answer.shape[0]], answer), far)
    mean_ref[...] = mean
    saved = pltpu.make_async_copy(mean_ref, mean_hbm, sems.at[1])
    saved.start()
    store_rows(reply_ref, dot(pick_ref[...], mean).astype(BF16))
    sent = pltpu.make_async_copy(reply_ref, reply_hbm, sems.at[2])
    sent.start()
    kept.wait()
    saved.wait()
    sent.wait()


def between_kernel(
    members, self_one_hbm, neigh_one_hbm, self_two_hbm, neigh_two_hbm, pos_hbm, features_hbm, answer_hbm, mean_hbm,
    near_ref, far_ref, asked_ref,
    final_hbm, place_hbm, base_ref, far_moved_ref, dense_ref, neigh_one_ref, ready_ref,
    held_one, held_two, rest, features_ref, answer_ref, mean_ref, final_ref, place_ref, pos_ref, sems,
):
    ready = ready_ref.shape[0]
    copies = [
        pltpu.make_async_copy(pos_hbm, pos_ref, sems.at[0]),
        pltpu.make_async_copy(self_one_hbm, held_one, sems.at[1]),
        pltpu.make_async_copy(neigh_one_hbm, neigh_one_ref, sems.at[2]),
        pltpu.make_async_copy(self_two_hbm, held_two, sems.at[3]),
        pltpu.make_async_copy(neigh_two_hbm.at[pl.ds(0, ready)], ready_ref, sems.at[4]),
        pltpu.make_async_copy(neigh_two_hbm.at[pl.ds(ready, rest.shape[0])], rest, sems.at[5]),
    ]
    inputs = [
        pltpu.make_async_copy(features_hbm, features_ref, sems.at[6]),
        pltpu.make_async_copy(answer_hbm, answer_ref, sems.at[7]),
        pltpu.make_async_copy(mean_hbm, mean_ref, sems.at[8]),
    ]
    for copy in (*inputs, *copies):
        copy.start()
    rows = features_ref.shape[0]
    capacity = 2 * rows // members
    me = lax.axis_index("dev")
    first = lax.axis_index("grp") * members
    line = iota((rows, rows), 0)
    step = divide(line, capacity)
    rank = line - step * capacity
    target = me + 2 * step
    target = jnp.where(target >= members, target - members, target)
    prefix = earlier(rows)
    copies[0].wait()
    goes = target == divide(pos_ref[...], rows) - first
    before = dot(bits(goes).astype(BF16), prefix).astype(I32)
    move = bits(goes & (before == rank)).astype(BF16)
    near = dot(move, near_ref[...]).astype(BF16)
    far = dot(move, far_ref[...]).astype(BF16)
    size = far.shape[1] - 8
    used = jnp.sum(far_ref[:, :size].astype(F32), axis=0, keepdims=True) > 0.0
    used = jnp.broadcast_to(used, dense_ref.shape)
    seats = dot(bits(used).astype(BF16), earlier(size)).astype(I32)
    dense = bits(used & (seats == iota(used.shape, 0))).astype(BF16)
    dense_ref[...] = dense
    held = dense.shape[0]
    far_moved_ref[:, :held] = dot_lanes(far[:, :size], dense).astype(BF16)
    far_moved_ref[:, held:] = far[:, size:]
    place = jnp.zeros((rows, rows), F32)
    for q in range(members // 2):
        source = me - 2 * q
        source = first + jnp.where(source < 0, source + members, source)
        sent = asked_ref[source] & (2 * rows - 1)
        valid = jnp.broadcast_to(sent > 0, (rows, rows))
        before = dot(bits(valid).astype(BF16), prefix).astype(I32)
        lands = bits(sent - 1 == line).astype(BF16)
        comes = bits(valid & (step == q) & (before == rank)).astype(BF16)
        place += dot_lanes(lands, comes)
    place_ref[...] = place.astype(BF16)
    placed = pltpu.make_async_copy(place_ref, place_hbm, sems.at[9])
    placed.start()
    for copy in (*inputs, copies[1]):
        copy.wait()
    own = dot(features_ref[...], held_one[...])
    base_ref[...] = dot(dot(dense, load_rows(answer_ref)).astype(BF16), held_one[...]).astype(BF16)
    copies[2].wait()
    hidden = jnp.maximum(own + dot(mean_ref[...], neigh_one_ref[...]), 0.0).astype(BF16)
    mean = over_count(dot(near, hidden), far)
    moved = dot(move, hidden).astype(BF16)
    copies[3].wait()
    final = dot(moved, held_two[...])
    copies[4].wait()
    final += dot(mean[:, :ready], ready_ref[...])
    copies[5].wait()
    final_ref[...] = (final + dot(mean[:, ready:], rest[...])).astype(BF16)
    away = pltpu.make_async_copy(final_ref, final_hbm, sems.at[10])
    away.start()
    away.wait()
    placed.wait()


def layer_two_kernel(neigh_two_hbm, final_hbm, neigh_one_ref, ready_ref, base_ref, answer_ref, far_ref, dense_ref, *refs):
    outs, held, final_ref, sems = refs[:-3], refs[-3], refs[-2], refs[-1]
    ready = ready_ref.shape[0]
    pieces = sems.shape[0] - 1
    copies = fetches(neigh_two_hbm.at[pl.ds(ready, held.shape[0])], held, sems.at[pl.ds(0, pieces)])
    last = pltpu.make_async_copy(final_hbm, final_ref, sems.at[pieces])

    depth = held.shape[0] // pieces

    @pl.loop(0, pieces)
    def _(i):
        piece = pl.ds(pl.multiple_of(i * depth, 16), depth)
        pltpu.make_async_copy(neigh_two_hbm.at[pl.ds(ready, held.shape[0])].at[piece], held.at[piece], sems.at[i]).start()

        @pl.when(i == pieces - 1)
        def _():
            last.start()

    far = far_ref[...]
    answer = dot(dense_ref[...], load_rows(answer_ref)).astype(BF16)
    other = jnp.maximum(base_ref[...].astype(F32) + dot(answer, neigh_one_ref[...]), 0.0).astype(BF16)
    mean = over_count(dot(far[:, : other.shape[0]], other), far)
    final = dot(mean[:, :ready], ready_ref[...]) + dot_fetched(mean[:, ready:], held, copies)
    last.wait()
    final = (final + final_ref[...].astype(F32)).astype(BF16)
    capacity = outs[0].shape[0]
    for q, ref in enumerate(outs):
        ref[...] = final[q * capacity : (q + 1) * capacity]


def scatter_kernel(place_ref, *refs):
    out_ref = refs[-1]
    arrived = jnp.concatenate([ref[...] for ref in refs[:-1]], axis=0)
    out_ref[...] = dot(place_ref[...], arrived).astype(BF16)


def body(features, neighbours, neighbour_mask, layer2_position, self_weight1, neigh_weight1, self_weight2, neigh_weight2):
    rows, degree = neighbours.shape
    members = lax.axis_size("dev")
    peers = lax.axis_size("grp") * members
    width_in, width = self_weight1.shape
    steps = members // 2
    capacity = rows // steps
    size = peers * CAP
    early = width * 9 // 16
    held = -(-((peers - 1) * CAP // 2) // 16) * 16
    shape = jax.ShapeDtypeStruct
    copies = pltpu.SemaphoreType.DMA

    pos = layer2_position.reshape(1, rows)
    ask, near, far, order, table = call(
        functools.partial(ask_kernel, members, peers),
        (
            shape((peers, 1, rows), I32),
            shape((rows, rows), BF16),
            shape((rows, size + 8), BF16),
            shape((size, size), BF16),
            shape((rows, width_in), BF16),
        ),
        (neighbours.T, neighbour_mask.T, pos, features),
        (),
        [pltpu.VMEM((degree, rows), I32), pltpu.VMEM((degree, rows), I32), pltpu.VMEM((1, rows), I32), copies((4,))],
        2 * size * size * rows,
        "ask",
        limit=40 << 20,
    )
    asked = lax.all_to_all(ask, BOTH, 0, 0, tiled=True)
    reply, pick = call(
        serve_kernel,
        (shape((peers, CAP // 2, 2, width_in), BF16), shape((size, rows), BF16)),
        (),
        (asked, order, table),
        [],
        2 * size * rows * width_in,
        "serve",
    )
    answer = lax.all_to_all(reply, BOTH, 0, 0, tiled=True)
    kept, mean, reply_two = call(
        layer_one_kernel,
        (
            shape((peers, CAP // 2, 2, width_in), BF16),
            shape((rows, width_in), BF16),
            shape((peers, CAP // 2, 2, width_in), BF16),
        ),
        (),
        (table, near, answer, far, pick),
        [pltpu.VMEM((rows, width_in), BF16), pltpu.VMEM((peers, CAP // 2, 2, width_in), BF16), copies((3,))],
        2 * rows * width_in * (size + rows) + 2 * size * rows * width_in,
        "layer_one",
        away=3,
    )
    answer_two = lax.all_to_all(reply_two, BOTH, 0, 0, tiled=True)
    final, place, base, far_moved, dense, weight, ready = call(
        functools.partial(between_kernel, members),
        (
            shape((rows, width), BF16),
            shape((rows, rows), BF16),
            shape((held, width), BF16),
            shape((rows, held + 8), BF16),
            shape((held, size), BF16),
            shape((width_in, width), BF16),
            shape((early, width), BF16),
        ),
        (self_weight1, neigh_weight1, self_weight2, neigh_weight2, pos, features, kept, mean),
        (near, far, asked),
        [
            pltpu.VMEM((width_in, width), BF16),
            pltpu.VMEM((width, width), BF16),
            pltpu.VMEM((width - early, width), BF16),
            pltpu.VMEM((rows, width_in), BF16),
            pltpu.VMEM((peers, CAP // 2, 2, width_in), BF16),
            pltpu.VMEM((rows, width_in), BF16),
            pltpu.VMEM((rows, width), BF16),
            pltpu.VMEM((rows, rows), BF16),
            pltpu.VMEM((1, rows), I32),
            copies((11,)),
        ],
        2 * width * (rows * (2 * width_in + rows + 2 * width) + size * width_in),
        "between",
        limit=48 << 20,
        away=2,
    )
    finals = call(
        layer_two_kernel,
        tuple(shape((capacity, width), BF16) for _ in range(steps)),
        (neigh_weight2, final),
        (weight, ready, base, answer_two, far_moved, dense),
        [pltpu.VMEM((width - early, width), BF16), pltpu.VMEM((rows, width), BF16), copies((3,))],
        2 * width * (size * width_in + rows * (size + width)),
        "layer_two",
        limit=48 << 20,
    )
    arrived = [finals[0]]
    for q in range(1, steps):
        arrived.append(lax.ppermute(finals[q], "dev", [(i, (i + 2 * q) % members) for i in range(members)]))
    return call(
        scatter_kernel,
        shape((rows, width), BF16),
        (),
        (place, *arrived),
        [],
        2 * rows * rows * width,
        "scatter",
    )


def solution(mesh):
    return jax.shard_map(
        body,
        mesh=mesh,
        in_specs=(
            P(BOTH, None),
            P(BOTH, None),
            P(BOTH, None),
            P(BOTH),
            P(),
            P(),
            P(),
            P(),
        ),
        out_specs=P(BOTH, None),
        check_vma=False,
    )
```

```python
import functools

import jax
import jax.numpy as jnp
from jax import lax
from jax.experimental import pallas as pl
from jax.experimental.pallas import tpu as pltpu
from jax.sharding import PartitionSpec as P

CAP = 6
BOTH = ("grp", "dev")
F32 = jnp.float32
BF16 = jnp.bfloat16
I32 = jnp.int32


def divide(values, by):
    if by & (by - 1) == 0:
        return values >> (by.bit_length() - 1)
    return (values * (-(-(1 << 16) // by))) >> 16


def iota(shape, dim):
    return lax.broadcasted_iota(I32, shape, dim)


def bits(condition):
    return jnp.where(condition, 1.0, 0.0)


def earlier(count):
    return bits(iota((count, count), 0) < iota((count, count), 1)).astype(BF16)


def dot(left, right):
    return jnp.dot(left, right, preferred_element_type=F32)


def dot_lanes(left, right):
    return lax.dot_general(left, right, (((1,), (1,)), ((), ())), preferred_element_type=F32)


def near_by(n):
    return [pl.BlockSpec(memory_space=pltpu.VMEM)] * n


def far_off(n):
    return [pl.BlockSpec(memory_space=pltpu.HBM)] * n


def call(kernel, outs, remote, operands, scratch, flops, name, limit=24 << 20, away=0):
    single = not isinstance(outs, tuple)
    leaves = (outs,) if single else outs
    moved = sum(a.size * a.dtype.itemsize for a in (*remote, *operands, *leaves))
    return pl.pallas_call(
        kernel,
        out_shape=outs if single else (*(pltpu.HBM(a.shape, a.dtype) for a in leaves[:away]), *leaves[away:]),
        in_specs=far_off(len(remote)) + near_by(len(operands)),
        out_specs=near_by(1)[0] if single else far_off(away) + near_by(len(leaves) - away),
        scratch_shapes=scratch,
        compiler_params=pltpu.CompilerParams(vmem_limit_bytes=limit),
        cost_estimate=pl.CostEstimate(flops=flops, bytes_accessed=moved, transcendentals=0),
        name=name,
    )(*(pltpu.with_memory_space_constraint(a, pltpu.HBM) for a in remote), *operands)


def fetches(weight_ref, held, sems):
    pieces = sems.shape[0]
    depth = weight_ref.shape[0] // pieces
    return [
        pltpu.make_async_copy(
            weight_ref.at[pl.ds(i * depth, depth)], held.at[pl.ds(i * depth, depth)], sems.at[i]
        )
        for i in range(pieces)
    ]


def dot_fetched(left, held, copies):
    depth = held.shape[0] // len(copies)
    result = None
    for i, copy in enumerate(copies):
        copy.wait()
        part = dot(left[:, i * depth : (i + 1) * depth], held[i * depth : (i + 1) * depth])
        result = part if result is None else result + part
    return result


def ask_kernel(
    members, peers, ids_hbm, mask_hbm, pos_hbm, features_hbm, ask_ref, near_ref, far_ref, order_ref, features_ref, ids, mask, pos_ref, sems
):
    degree, rows = ids.shape
    copies = [
        pltpu.make_async_copy(ids_hbm, ids, sems.at[0]),
        pltpu.make_async_copy(mask_hbm, mask, sems.at[1]),
        pltpu.make_async_copy(pos_hbm, pos_ref, sems.at[2]),
    ]
    table = pltpu.make_async_copy(features_hbm, features_ref, sems.at[3])
    for copy in (*copies, table):
        copy.start()
    own = lax.axis_index("grp") * members + lax.axis_index("dev")
    peer = iota((peers, rows), 0)
    prefix = earlier(rows)
    for copy in copies:
        copy.wait()
    slots = jnp.where(mask[...] > 0, ids[...], -1)
    owner = divide(jnp.maximum(slots, 0), rows)
    row = slots - owner * rows
    live = slots >= 0
    here = owner == own
    key = jnp.where(live & jnp.logical_not(here), owner, -1)
    half = CAP // 2
    width = (rows - 1).bit_length()
    top = width * (half - 1)
    low = jnp.zeros((peers, rows), I32)
    high = jnp.zeros((peers, rows), I32)
    total = jnp.zeros((peers, rows), I32)
    for s in range(degree):
        hit = key[s : s + 1] == peer
        high = jnp.where(hit, (high << width) | (low >> top), high)
        low = jnp.where(hit, ((low & ((1 << top) - 1)) << width) | row[s : s + 1], low)
        total += jnp.where(hit, 1, 0)
    before = dot(total.astype(F32).astype(BF16), prefix).astype(I32)
    packed = [jnp.where(before == 0, low, 0), jnp.where(before == 0, high, jnp.where(before == half, low, 0))]
    for k in range(1, half):
        shift, rest = width * k, width * (half - k)
        inside = before == k
        packed[0] = jnp.where(inside, (low & ((1 << rest) - 1)) << shift, packed[0])
        packed[1] = jnp.where(inside, (high << shift) | (low >> rest), packed[1])
        packed[1] = jnp.where(before == half + k, low << shift, packed[1])
    lane = iota((peers, rows), 1)
    wanted = jnp.zeros((peers, rows), I32)
    for w, word in enumerate(packed):
        word = jnp.broadcast_to(jnp.sum(word.astype(F32), axis=1, keepdims=True).astype(I32), (peers, rows))
        for k in range(half):
            wanted = jnp.where(lane == w * half + k, (word >> (width * k)) & ((1 << width) - 1), wanted)
    pos = pos_ref[...]
    place = jnp.where(divide(pos, rows) == peer, pos - divide(pos, rows) * rows + 1, 0)
    ask_ref[...] = (place + wanted * (2 * rows)).reshape(peers, 1, rows)
    local = jnp.where(live & here, row, -1)
    node = iota((rows, rows), 0).astype(F32).astype(BF16)
    local = local.astype(F32).astype(BF16)
    one, none = jnp.ones((rows, rows), BF16), jnp.zeros((rows, rows), BF16)
    near = none
    for s in range(degree):
        near += jnp.where(local[s : s + 1] == node, one, none)
    near_ref[...] = near.astype(F32).T.astype(BF16)
    far = [bits((before <= k) & (k < before + total)).astype(BF16) for k in range(CAP)]
    far = jnp.concatenate(far, axis=0)
    size = peers * CAP
    line = iota((size, size), 0)
    device = divide(line, CAP)
    order = bits(iota((size, size), 1) == (line - device * CAP) * peers + device).astype(BF16)
    order_ref[...] = order
    far_ref[:, :size] = dot(order, far).T.astype(BF16)
    count = jnp.broadcast_to(jnp.sum(bits(live), axis=0, keepdims=True), (rows, rows)).T.astype(BF16)
    far_ref[:, size:] = count[:, : far_ref.shape[1] - size]
    table.wait()


def store_rows(reply_ref, rows):
    peers, pairs, two, width = reply_ref.shape
    reply_ref[...] = rows.reshape(peers, pairs, two, width)


def load_rows(answer_ref):
    peers, pairs, two, width = answer_ref.shape
    return answer_ref[...].reshape(peers * pairs * two, width)


def serve_kernel(asked_ref, order_ref, source_ref, reply_ref, pick_ref):
    peers, _, rows = asked_ref.shape
    asked = asked_ref[...].reshape(peers, rows)
    wanted = divide(asked, 2 * rows)
    lane = iota((peers, rows), 1)
    picks = [bits(wanted[:, k : k + 1] == lane).astype(BF16) for k in range(CAP)]
    pick = dot(order_ref[...], jnp.concatenate(picks, axis=0)).astype(BF16)
    pick_ref[...] = pick
    store_rows(reply_ref, dot(pick, source_ref[...]).astype(BF16))


def over_count(summed, far):
    size = far.shape[1] - 8
    return (summed / far[:, size : size + 1].astype(F32)).astype(BF16)


def layer_one_kernel(
    features_ref, near_ref, answer_ref, far_ref, pick_ref, answer_hbm, mean_hbm, reply_hbm, mean_ref, reply_ref, sems
):
    kept = pltpu.make_async_copy(answer_ref, answer_hbm, sems.at[0])
    kept.start()
    answer = load_rows(answer_ref)
    far = far_ref[...]
    mean = over_count(dot(near_ref[...], features_ref[...]) + dot(far[:, : answer.shape[0]], answer), far)
    mean_ref[...] = mean
    saved = pltpu.make_async_copy(mean_ref, mean_hbm, sems.at[1])
    saved.start()
    store_rows(reply_ref, dot(pick_ref[...], mean).astype(BF16))
    sent = pltpu.make_async_copy(reply_ref, reply_hbm, sems.at[2])
    sent.start()
    kept.wait()
    saved.wait()
    sent.wait()


def between_kernel(
    members, self_one_hbm, neigh_one_hbm, self_two_hbm, neigh_two_hbm, pos_hbm, features_hbm, answer_hbm, mean_hbm,
    near_ref, far_ref, asked_ref,
    final_hbm, place_hbm, base_ref, far_moved_ref, dense_ref, neigh_one_ref, ready_ref,
    held_one, held_two, rest, features_ref, answer_ref, mean_ref, final_ref, place_ref, pos_ref, sems,
):
    ready = ready_ref.shape[0]
    copies = [
        pltpu.make_async_copy(pos_hbm, pos_ref, sems.at[0]),
        pltpu.make_async_copy(self_one_hbm, held_one, sems.at[1]),
        pltpu.make_async_copy(neigh_one_hbm, neigh_one_ref, sems.at[2]),
        pltpu.make_async_copy(self_two_hbm, held_two, sems.at[3]),
        pltpu.make_async_copy(neigh_two_hbm.at[pl.ds(0, ready)], ready_ref, sems.at[4]),
        pltpu.make_async_copy(neigh_two_hbm.at[pl.ds(ready, rest.shape[0])], rest, sems.at[5]),
    ]
    inputs = [
        pltpu.make_async_copy(features_hbm, features_ref, sems.at[6]),
        pltpu.make_async_copy(answer_hbm, answer_ref, sems.at[7]),
        pltpu.make_async_copy(mean_hbm, mean_ref, sems.at[8]),
    ]
    for copy in (*inputs, *copies):
        copy.start()
    rows = features_ref.shape[0]
    capacity = 2 * rows // members
    me = lax.axis_index("dev")
    first = lax.axis_index("grp") * members
    line = iota((rows, rows), 0)
    step = divide(line, capacity)
    rank = line - step * capacity
    target = me + 2 * step
    target = jnp.where(target >= members, target - members, target)
    prefix = earlier(rows)
    copies[0].wait()
    goes = target == divide(pos_ref[...], rows) - first
    before = dot(bits(goes).astype(BF16), prefix).astype(I32)
    move = bits(goes & (before == rank)).astype(BF16)
    near = dot(move, near_ref[...]).astype(BF16)
    far = dot(move, far_ref[...]).astype(BF16)
    size = far.shape[1] - 8
    used = jnp.sum(far_ref[:, :size].astype(F32), axis=0, keepdims=True) > 0.0
    used = jnp.broadcast_to(used, dense_ref.shape)
    seats = dot(bits(used).astype(BF16), earlier(size)).astype(I32)
    dense = bits(used & (seats == iota(used.shape, 0))).astype(BF16)
    dense_ref[...] = dense
    held = dense.shape[0]
    far_moved_ref[:, :held] = dot_lanes(far[:, :size], dense).astype(BF16)
    far_moved_ref[:, held:] = far[:, size:]
    place = jnp.zeros((rows, rows), F32)
    for q in range(members // 2):
        source = me - 2 * q
        source = first + jnp.where(source < 0, source + members, source)
        sent = asked_ref[source] & (2 * rows - 1)
        valid = jnp.broadcast_to(sent > 0, (rows, rows))
        before = dot(bits(valid).astype(BF16), prefix).astype(I32)
        lands = bits(sent - 1 == line).astype(BF16)
        comes = bits(valid & (step == q) & (before == rank)).astype(BF16)
        place += dot_lanes(lands, comes)
    place_ref[...] = place.astype(BF16)
    placed = pltpu.make_async_copy(place_ref, place_hbm, sems.at[9])
    placed.start()
    for copy in (*inputs, copies[1]):
        copy.wait()
    own = dot(features_ref[...], held_one[...])
    base_ref[...] = dot(dot(dense, load_rows(answer_ref)).astype(BF16), held_one[...]).astype(BF16)
    copies[2].wait()
    hidden = jnp.maximum(own + dot(mean_ref[...], neigh_one_ref[...]), 0.0).astype(BF16)
    mean = over_count(dot(near, hidden), far)
    moved = dot(move, hidden).astype(BF16)
    copies[3].wait()
    final = dot(moved, held_two[...])
    copies[4].wait()
    final += dot(mean[:, :ready], ready_ref[...])
    copies[5].wait()
    final_ref[...] = (final + dot(mean[:, ready:], rest[...])).astype(BF16)
    away = pltpu.make_async_copy(final_ref, final_hbm, sems.at[10])
    away.start()
    away.wait()
    placed.wait()


def layer_two_kernel(neigh_two_hbm, final_hbm, neigh_one_ref, ready_ref, base_ref, answer_ref, far_ref, dense_ref, *refs):
    outs, (held, final_ref, mean_ref, sum_ref, sems) = refs[:-5], refs[-5:]
    ready = ready_ref.shape[0]
    pieces = sems.shape[0] - 1
    last = pltpu.make_async_copy(final_hbm, final_ref, sems.at[pieces])
    depth = held.shape[0] // pieces

    def fetch(i):
        piece = pl.ds(pl.multiple_of(i * depth, 16), depth)
        return pltpu.make_async_copy(neigh_two_hbm.at[pl.ds(ready, held.shape[0])].at[piece], held.at[piece], sems.at[i])

    @pl.loop(0, pieces)
    def _(i):
        fetch(i).start()

        @pl.when(i == pieces - 1)
        def _():
            last.start()

    far = far_ref[...]
    answer = dot(dense_ref[...], load_rows(answer_ref)).astype(BF16)
    other = jnp.maximum(base_ref[...].astype(F32) + dot(answer, neigh_one_ref[...]), 0.0).astype(BF16)
    mean = over_count(dot(far[:, : other.shape[0]], other), far)
    mean_ref[...] = mean[:, ready:]
    sum_ref[...] = dot(mean[:, :ready], ready_ref[...])

    @pl.loop(0, pieces)
    def _(i):
        fetch(i).wait()

    final = sum_ref[...] + dot(mean_ref[...], held[...])
    last.wait()
    final = (final + final_ref[...].astype(F32)).astype(BF16)
    capacity = outs[0].shape[0]
    for q, ref in enumerate(outs):
        ref[...] = final[q * capacity : (q + 1) * capacity]


def scatter_kernel(place_ref, *refs):
    out_ref = refs[-1]
    arrived = jnp.concatenate([ref[...] for ref in refs[:-1]], axis=0)
    out_ref[...] = dot(place_ref[...], arrived).astype(BF16)


def body(features, neighbours, neighbour_mask, layer2_position, self_weight1, neigh_weight1, self_weight2, neigh_weight2):
    rows, degree = neighbours.shape
    members = lax.axis_size("dev")
    peers = lax.axis_size("grp") * members
    width_in, width = self_weight1.shape
    steps = members // 2
    capacity = rows // steps
    size = peers * CAP
    early = width * 9 // 16
    held = -(-((peers - 1) * CAP // 2) // 16) * 16
    shape = jax.ShapeDtypeStruct
    copies = pltpu.SemaphoreType.DMA

    pos = layer2_position.reshape(1, rows)
    ask, near, far, order, table = call(
        functools.partial(ask_kernel, members, peers),
        (
            shape((peers, 1, rows), I32),
            shape((rows, rows), BF16),
            shape((rows, size + 8), BF16),
            shape((size, size), BF16),
            shape((rows, width_in), BF16),
        ),
        (neighbours.T, neighbour_mask.T, pos, features),
        (),
        [pltpu.VMEM((degree, rows), I32), pltpu.VMEM((degree, rows), I32), pltpu.VMEM((1, rows), I32), copies((4,))],
        2 * size * size * rows,
        "ask",
        limit=40 << 20,
    )
    asked = lax.all_to_all(ask, BOTH, 0, 0, tiled=True)
    reply, pick = call(
        serve_kernel,
        (shape((peers, CAP // 2, 2, width_in), BF16), shape((size, rows), BF16)),
        (),
        (asked, order, table),
        [],
        2 * size * rows * width_in,
        "serve",
    )
    answer = lax.all_to_all(reply, BOTH, 0, 0, tiled=True)
    kept, mean, reply_two = call(
        layer_one_kernel,
        (
            shape((peers, CAP // 2, 2, width_in), BF16),
            shape((rows, width_in), BF16),
            shape((peers, CAP // 2, 2, width_in), BF16),
        ),
        (),
        (table, near, answer, far, pick),
        [pltpu.VMEM((rows, width_in), BF16), pltpu.VMEM((peers, CAP // 2, 2, width_in), BF16), copies((3,))],
        2 * rows * width_in * (size + rows) + 2 * size * rows * width_in,
        "layer_one",
        away=3,
    )
    answer_two = lax.all_to_all(reply_two, BOTH, 0, 0, tiled=True)
    final, place, base, far_moved, dense, weight, ready = call(
        functools.partial(between_kernel, members),
        (
            shape((rows, width), BF16),
            shape((rows, rows), BF16),
            shape((held, width), BF16),
            shape((rows, held + 8), BF16),
            shape((held, size), BF16),
            shape((width_in, width), BF16),
            shape((early, width), BF16),
        ),
        (self_weight1, neigh_weight1, self_weight2, neigh_weight2, pos, features, kept, mean),
        (near, far, asked),
        [
            pltpu.VMEM((width_in, width), BF16),
            pltpu.VMEM((width, width), BF16),
            pltpu.VMEM((width - early, width), BF16),
            pltpu.VMEM((rows, width_in), BF16),
            pltpu.VMEM((peers, CAP // 2, 2, width_in), BF16),
            pltpu.VMEM((rows, width_in), BF16),
            pltpu.VMEM((rows, width), BF16),
            pltpu.VMEM((rows, rows), BF16),
            pltpu.VMEM((1, rows), I32),
            copies((11,)),
        ],
        2 * width * (rows * (2 * width_in + rows + 2 * width) + size * width_in),
        "between",
        limit=48 << 20,
        away=2,
    )
    finals = call(
        layer_two_kernel,
        tuple(shape((capacity, width), BF16) for _ in range(steps)),
        (neigh_weight2, final),
        (weight, ready, base, answer_two, far_moved, dense),
        [
            pltpu.VMEM((width - early, width), BF16),
            pltpu.VMEM((rows, width), BF16),
            pltpu.VMEM((rows, width - early), BF16),
            pltpu.VMEM((rows, width), F32),
            copies((3,)),
        ],
        2 * width * (size * width_in + rows * (size + width)),
        "layer_two",
        limit=48 << 20,
    )
    arrived = [finals[0]]
    for q in range(1, steps):
        arrived.append(lax.ppermute(finals[q], "dev", [(i, (i + 2 * q) % members) for i in range(members)]))
    return call(
        scatter_kernel,
        shape((rows, width), BF16),
        (),
        (place, *arrived),
        [],
        2 * rows * rows * width,
        "scatter",
    )


def solution(mesh):
    return jax.shard_map(
        body,
        mesh=mesh,
        in_specs=(
            P(BOTH, None),
            P(BOTH, None),
            P(BOTH, None),
            P(BOTH),
            P(),
            P(),
            P(),
            P(),
        ),
        out_specs=P(BOTH, None),
        check_vma=False,
    )
```

```python
import functools

import jax
import jax.numpy as jnp
from jax import lax
from jax.experimental import pallas as pl
from jax.experimental.pallas import tpu as pltpu
from jax.sharding import PartitionSpec as P

CAP = 6
BOTH = ("grp", "dev")
F32 = jnp.float32
BF16 = jnp.bfloat16
I32 = jnp.int32


def divide(values, by):
    if by & (by - 1) == 0:
        return values >> (by.bit_length() - 1)
    return (values * (-(-(1 << 16) // by))) >> 16


def iota(shape, dim):
    return lax.broadcasted_iota(I32, shape, dim)


def bits(condition):
    return jnp.where(condition, 1.0, 0.0)


def earlier(count):
    return bits(iota((count, count), 0) < iota((count, count), 1)).astype(BF16)


def dot(left, right):
    return jnp.dot(left, right, preferred_element_type=F32)


def dot_lanes(left, right):
    return lax.dot_general(left, right, (((1,), (1,)), ((), ())), preferred_element_type=F32)


def near_by(n):
    return [pl.BlockSpec(memory_space=pltpu.VMEM)] * n


def far_off(n):
    return [pl.BlockSpec(memory_space=pltpu.HBM)] * n


def call(kernel, outs, remote, operands, scratch, flops, name, limit=24 << 20, away=0):
    single = not isinstance(outs, tuple)
    leaves = (outs,) if single else outs
    moved = sum(a.size * a.dtype.itemsize for a in (*remote, *operands, *leaves))
    return pl.pallas_call(
        kernel,
        out_shape=outs if single else (*(pltpu.HBM(a.shape, a.dtype) for a in leaves[:away]), *leaves[away:]),
        in_specs=far_off(len(remote)) + near_by(len(operands)),
        out_specs=near_by(1)[0] if single else far_off(away) + near_by(len(leaves) - away),
        scratch_shapes=scratch,
        compiler_params=pltpu.CompilerParams(vmem_limit_bytes=limit),
        cost_estimate=pl.CostEstimate(flops=flops, bytes_accessed=moved, transcendentals=0),
        name=name,
    )(*(pltpu.with_memory_space_constraint(a, pltpu.HBM) for a in remote), *operands)


def fetches(weight_ref, held, sems):
    pieces = sems.shape[0]
    depth = weight_ref.shape[0] // pieces
    return [
        pltpu.make_async_copy(
            weight_ref.at[pl.ds(i * depth, depth)], held.at[pl.ds(i * depth, depth)], sems.at[i]
        )
        for i in range(pieces)
    ]


def dot_fetched(left, held, copies):
    depth = held.shape[0] // len(copies)
    result = None
    for i, copy in enumerate(copies):
        copy.wait()
        part = dot(left[:, i * depth : (i + 1) * depth], held[i * depth : (i + 1) * depth])
        result = part if result is None else result + part
    return result


def ask_kernel(
    members, peers, ids_hbm, mask_hbm, pos_hbm, features_hbm, ask_ref, near_ref, far_ref, order_ref, features_ref, ids, mask, pos_ref, sems
):
    degree, rows = ids.shape
    copies = [
        pltpu.make_async_copy(ids_hbm, ids, sems.at[0]),
        pltpu.make_async_copy(mask_hbm, mask, sems.at[1]),
        pltpu.make_async_copy(pos_hbm, pos_ref, sems.at[2]),
    ]
    table = pltpu.make_async_copy(features_hbm, features_ref, sems.at[3])
    for copy in (*copies, table):
        copy.start()
    own = lax.axis_index("grp") * members + lax.axis_index("dev")
    peer = iota((peers, rows), 0)
    prefix = earlier(rows)
    for copy in copies:
        copy.wait()
    slots = jnp.where(mask[...] > 0, ids[...], -1)
    owner = divide(jnp.maximum(slots, 0), rows)
    row = slots - owner * rows
    live = slots >= 0
    here = owner == own
    key = jnp.where(live & jnp.logical_not(here), owner, -1)
    half = CAP // 2
    width = (rows - 1).bit_length()
    top = width * (half - 1)
    low = jnp.zeros((peers, rows), I32)
    high = jnp.zeros((peers, rows), I32)
    total = jnp.zeros((peers, rows), I32)
    for s in range(degree):
        hit = key[s : s + 1] == peer
        high = jnp.where(hit, (high << width) | (low >> top), high)
        low = jnp.where(hit, ((low & ((1 << top) - 1)) << width) | row[s : s + 1], low)
        total += jnp.where(hit, 1, 0)
    before = dot(total.astype(F32).astype(BF16), prefix).astype(I32)
    packed = [jnp.where(before == 0, low, 0), jnp.where(before == 0, high, jnp.where(before == half, low, 0))]
    for k in range(1, half):
        shift, rest = width * k, width * (half - k)
        inside = before == k
        packed[0] = jnp.where(inside, (low & ((1 << rest) - 1)) << shift, packed[0])
        packed[1] = jnp.where(inside, (high << shift) | (low >> rest), packed[1])
        packed[1] = jnp.where(before == half + k, low << shift, packed[1])
    lane = iota((peers, rows), 1)
    wanted = jnp.zeros((peers, rows), I32)
    for w, word in enumerate(packed):
        word = jnp.broadcast_to(jnp.sum(word.astype(F32), axis=1, keepdims=True).astype(I32), (peers, rows))
        for k in range(half):
            wanted = jnp.where(lane == w * half + k, (word >> (width * k)) & ((1 << width) - 1), wanted)
    pos = pos_ref[...]
    place = jnp.where(divide(pos, rows) == peer, pos - divide(pos, rows) * rows + 1, 0)
    ask_ref[...] = (place + wanted * (2 * rows)).reshape(peers, 1, rows)
    local = jnp.where(live & here, row, -1)
    node = iota((rows, rows), 0).astype(F32).astype(BF16)
    local = local.astype(F32).astype(BF16)
    one, none = jnp.ones((rows, rows), BF16), jnp.zeros((rows, rows), BF16)
    near = none
    for s in range(degree):
        near += jnp.where(local[s : s + 1] == node, one, none)
    near_ref[...] = near.astype(F32).T.astype(BF16)
    far = [bits((before <= k) & (k < before + total)).astype(BF16) for k in range(CAP)]
    far = jnp.concatenate(far, axis=0)
    size = peers * CAP
    line = iota((size, size), 0)
    device = divide(line, CAP)
    order = bits(iota((size, size), 1) == (line - device * CAP) * peers + device).astype(BF16)
    order_ref[...] = order
    far_ref[:, :size] = dot(order, far).T.astype(BF16)
    count = jnp.broadcast_to(jnp.sum(bits(live), axis=0, keepdims=True), (rows, rows)).T.astype(BF16)
    far_ref[:, size:] = count[:, : far_ref.shape[1] - size]
    table.wait()


def store_rows(reply_ref, rows):
    peers, pairs, two, width = reply_ref.shape
    reply_ref[...] = rows.reshape(peers, pairs, two, width)


def load_rows(answer_ref):
    peers, pairs, two, width = answer_ref.shape
    return answer_ref[...].reshape(peers * pairs * two, width)


def serve_kernel(asked_ref, order_ref, source_ref, reply_ref, pick_ref):
    peers, _, rows = asked_ref.shape
    asked = asked_ref[...].reshape(peers, rows)
    wanted = divide(asked, 2 * rows)
    lane = iota((peers, rows), 1)
    picks = [bits(wanted[:, k : k + 1] == lane).astype(BF16) for k in range(CAP)]
    pick = dot(order_ref[...], jnp.concatenate(picks, axis=0)).astype(BF16)
    pick_ref[...] = pick
    store_rows(reply_ref, dot(pick, source_ref[...]).astype(BF16))


def over_count(summed, far):
    size = far.shape[1] - 8
    return (summed / far[:, size : size + 1].astype(F32)).astype(BF16)


def layer_one_kernel(
    features_ref, near_ref, answer_ref, far_ref, pick_ref, answer_hbm, mean_hbm, reply_hbm, mean_ref, reply_ref, sems
):
    kept = pltpu.make_async_copy(answer_ref, answer_hbm, sems.at[0])
    kept.start()
    answer = load_rows(answer_ref)
    far = far_ref[...]
    mean = over_count(dot(near_ref[...], features_ref[...]) + dot(far[:, : answer.shape[0]], answer), far)
    mean_ref[...] = mean
    saved = pltpu.make_async_copy(mean_ref, mean_hbm, sems.at[1])
    saved.start()
    store_rows(reply_ref, dot(pick_ref[...], mean).astype(BF16))
    sent = pltpu.make_async_copy(reply_ref, reply_hbm, sems.at[2])
    sent.start()
    kept.wait()
    saved.wait()
    sent.wait()


def wrap(value, size):
    value = jnp.where(value < 0, value + size, value)
    return jnp.where(value >= size, value - size, value)


def between_kernel(
    members, self_one_hbm, neigh_one_hbm, self_two_hbm, neigh_two_hbm, pos_hbm, features_hbm, answer_hbm, mean_hbm,
    near_ref, far_ref, asked_ref,
    final_hbm, place_hbm, base_ref, far_moved_ref, dense_ref, neigh_one_ref, ready_ref,
    held_one, held_two, rest, features_ref, answer_ref, mean_ref, final_ref, place_ref, pos_ref, sems,
):
    ready = ready_ref.shape[0]
    copies = [
        pltpu.make_async_copy(pos_hbm, pos_ref, sems.at[0]),
        pltpu.make_async_copy(self_one_hbm, held_one, sems.at[1]),
        pltpu.make_async_copy(neigh_one_hbm, neigh_one_ref, sems.at[2]),
        pltpu.make_async_copy(self_two_hbm, held_two, sems.at[3]),
        pltpu.make_async_copy(neigh_two_hbm.at[pl.ds(0, ready)], ready_ref, sems.at[4]),
        pltpu.make_async_copy(neigh_two_hbm.at[pl.ds(ready, rest.shape[0])], rest, sems.at[5]),
    ]
    inputs = [
        pltpu.make_async_copy(features_hbm, features_ref, sems.at[6]),
        pltpu.make_async_copy(answer_hbm, answer_ref, sems.at[7]),
        pltpu.make_async_copy(mean_hbm, mean_ref, sems.at[8]),
    ]
    for copy in (*inputs, *copies):
        copy.start()
    rows = features_ref.shape[0]
    capacity = 2 * rows // members
    me = lax.axis_index("dev")
    first = lax.axis_index("grp") * members
    line = iota((rows, rows), 0)
    step = divide(line, capacity)
    rank = line - step * capacity
    sense = 2 - 4 * (me & 1)
    target = wrap(me + sense * step, members)
    prefix = earlier(rows)
    copies[0].wait()
    goes = target == divide(pos_ref[...], rows) - first
    before = dot(bits(goes).astype(BF16), prefix).astype(I32)
    move = bits(goes & (before == rank)).astype(BF16)
    near = dot(move, near_ref[...]).astype(BF16)
    far = dot(move, far_ref[...]).astype(BF16)
    size = far.shape[1] - 8
    used = jnp.sum(far_ref[:, :size].astype(F32), axis=0, keepdims=True) > 0.0
    used = jnp.broadcast_to(used, dense_ref.shape)
    seats = dot(bits(used).astype(BF16), earlier(size)).astype(I32)
    dense = bits(used & (seats == iota(used.shape, 0))).astype(BF16)
    dense_ref[...] = dense
    held = dense.shape[0]
    far_moved_ref[:, :held] = dot_lanes(far[:, :size], dense).astype(BF16)
    far_moved_ref[:, held:] = far[:, size:]
    place = jnp.zeros((rows, rows), F32)
    for q in range(members // 2):
        source = first + wrap(me - sense * q, members)
        sent = asked_ref[source] & (2 * rows - 1)
        valid = jnp.broadcast_to(sent > 0, (rows, rows))
        before = dot(bits(valid).astype(BF16), prefix).astype(I32)
        lands = bits(sent - 1 == line).astype(BF16)
        comes = bits(valid & (step == q) & (before == rank)).astype(BF16)
        place += dot_lanes(lands, comes)
    place_ref[...] = place.astype(BF16)
    placed = pltpu.make_async_copy(place_ref, place_hbm, sems.at[9])
    placed.start()
    for copy in (*inputs, copies[1]):
        copy.wait()
    own = dot(features_ref[...], held_one[...])
    base_ref[...] = dot(dot(dense, load_rows(answer_ref)).astype(BF16), held_one[...]).astype(BF16)
    copies[2].wait()
    hidden = jnp.maximum(own + dot(mean_ref[...], neigh_one_ref[...]), 0.0).astype(BF16)
    mean = over_count(dot(near, hidden), far)
    moved = dot(move, hidden).astype(BF16)
    copies[3].wait()
    final = dot(moved, held_two[...])
    copies[4].wait()
    final += dot(mean[:, :ready], ready_ref[...])
    copies[5].wait()
    final_ref[...] = (final + dot(mean[:, ready:], rest[...])).astype(BF16)
    away = pltpu.make_async_copy(final_ref, final_hbm, sems.at[10])
    away.start()
    away.wait()
    placed.wait()


def layer_two_kernel(neigh_two_hbm, final_hbm, neigh_one_ref, ready_ref, base_ref, answer_ref, far_ref, dense_ref, *refs):
    outs, (held, final_ref, mean_ref, sum_ref, sems) = refs[:-5], refs[-5:]
    ready = ready_ref.shape[0]
    pieces = sems.shape[0] - 1
    last = pltpu.make_async_copy(final_hbm, final_ref, sems.at[pieces])
    depth = held.shape[0] // pieces

    def fetch(i):
        piece = pl.ds(pl.multiple_of(i * depth, 16), depth)
        return pltpu.make_async_copy(neigh_two_hbm.at[pl.ds(ready, held.shape[0])].at[piece], held.at[piece], sems.at[i])

    @pl.loop(0, pieces)
    def _(i):
        fetch(i).start()

        @pl.when(i == pieces - 1)
        def _():
            last.start()

    far = far_ref[...]
    answer = dot(dense_ref[...], load_rows(answer_ref)).astype(BF16)
    other = jnp.maximum(base_ref[...].astype(F32) + dot(answer, neigh_one_ref[...]), 0.0).astype(BF16)
    mean = over_count(dot(far[:, : other.shape[0]], other), far)
    mean_ref[...] = mean[:, ready:]
    sum_ref[...] = dot(mean[:, :ready], ready_ref[...])

    @pl.loop(0, pieces)
    def _(i):
        fetch(i).wait()

    final = sum_ref[...] + dot(mean_ref[...], held[...])
    last.wait()
    final = (final + final_ref[...].astype(F32)).astype(BF16)
    capacity = outs[0].shape[0]
    for q, ref in enumerate(outs):
        ref[...] = final[q * capacity : (q + 1) * capacity]


def scatter_kernel(place_ref, *refs):
    out_ref = refs[-1]
    arrived = jnp.concatenate([ref[...] for ref in refs[:-1]], axis=0)
    out_ref[...] = dot(place_ref[...], arrived).astype(BF16)


def body(features, neighbours, neighbour_mask, layer2_position, self_weight1, neigh_weight1, self_weight2, neigh_weight2):
    rows, degree = neighbours.shape
    members = lax.axis_size("dev")
    peers = lax.axis_size("grp") * members
    width_in, width = self_weight1.shape
    steps = members // 2
    capacity = rows // steps
    size = peers * CAP
    early = width * 9 // 16
    held = -(-((peers - 1) * CAP // 2) // 16) * 16
    shape = jax.ShapeDtypeStruct
    copies = pltpu.SemaphoreType.DMA

    pos = layer2_position.reshape(1, rows)
    ask, near, far, order, table = call(
        functools.partial(ask_kernel, members, peers),
        (
            shape((peers, 1, rows), I32),
            shape((rows, rows), BF16),
            shape((rows, size + 8), BF16),
            shape((size, size), BF16),
            shape((rows, width_in), BF16),
        ),
        (neighbours.T, neighbour_mask.T, pos, features),
        (),
        [pltpu.VMEM((degree, rows), I32), pltpu.VMEM((degree, rows), I32), pltpu.VMEM((1, rows), I32), copies((4,))],
        2 * size * size * rows,
        "ask",
        limit=40 << 20,
    )
    asked = lax.all_to_all(ask, BOTH, 0, 0, tiled=True)
    reply, pick = call(
        serve_kernel,
        (shape((peers, CAP // 2, 2, width_in), BF16), shape((size, rows), BF16)),
        (),
        (asked, order, table),
        [],
        2 * size * rows * width_in,
        "serve",
    )
    answer = lax.all_to_all(reply, BOTH, 0, 0, tiled=True)
    kept, mean, reply_two = call(
        layer_one_kernel,
        (
            shape((peers, CAP // 2, 2, width_in), BF16),
            shape((rows, width_in), BF16),
            shape((peers, CAP // 2, 2, width_in), BF16),
        ),
        (),
        (table, near, answer, far, pick),
        [pltpu.VMEM((rows, width_in), BF16), pltpu.VMEM((peers, CAP // 2, 2, width_in), BF16), copies((3,))],
        2 * rows * width_in * (size + rows) + 2 * size * rows * width_in,
        "layer_one",
        away=3,
    )
    answer_two = lax.all_to_all(reply_two, BOTH, 0, 0, tiled=True)
    final, place, base, far_moved, dense, weight, ready = call(
        functools.partial(between_kernel, members),
        (
            shape((rows, width), BF16),
            shape((rows, rows), BF16),
            shape((held, width), BF16),
            shape((rows, held + 8), BF16),
            shape((held, size), BF16),
            shape((width_in, width), BF16),
            shape((early, width), BF16),
        ),
        (self_weight1, neigh_weight1, self_weight2, neigh_weight2, pos, features, kept, mean),
        (near, far, asked),
        [
            pltpu.VMEM((width_in, width), BF16),
            pltpu.VMEM((width, width), BF16),
            pltpu.VMEM((width - early, width), BF16),
            pltpu.VMEM((rows, width_in), BF16),
            pltpu.VMEM((peers, CAP // 2, 2, width_in), BF16),
            pltpu.VMEM((rows, width_in), BF16),
            pltpu.VMEM((rows, width), BF16),
            pltpu.VMEM((rows, rows), BF16),
            pltpu.VMEM((1, rows), I32),
            copies((11,)),
        ],
        2 * width * (rows * (2 * width_in + rows + 2 * width) + size * width_in),
        "between",
        limit=48 << 20,
        away=2,
    )
    finals = call(
        layer_two_kernel,
        tuple(shape((capacity, width), BF16) for _ in range(steps)),
        (neigh_weight2, final),
        (weight, ready, base, answer_two, far_moved, dense),
        [
            pltpu.VMEM((width - early, width), BF16),
            pltpu.VMEM((rows, width), BF16),
            pltpu.VMEM((rows, width - early), BF16),
            pltpu.VMEM((rows, width), F32),
            copies((3,)),
        ],
        2 * width * (size * width_in + rows * (size + width)),
        "layer_two",
        limit=48 << 20,
    )
    arrived = [finals[0]]
    for q in range(1, steps):
        arrived.append(lax.ppermute(finals[q], "dev", [(i, (i + (2 - 4 * (i & 1)) * q) % members) for i in range(members)]))
    return call(
        scatter_kernel,
        shape((rows, width), BF16),
        (),
        (place, *arrived),
        [],
        2 * rows * rows * width,
        "scatter",
    )


def solution(mesh):
    return jax.shard_map(
        body,
        mesh=mesh,
        in_specs=(
            P(BOTH, None),
            P(BOTH, None),
            P(BOTH, None),
            P(BOTH),
            P(),
            P(),
            P(),
            P(),
        ),
        out_specs=P(BOTH, None),
        check_vma=False,
    )
```

```python
import functools

import jax
import jax.numpy as jnp
from jax import lax
from jax.experimental import pallas as pl
from jax.experimental.pallas import tpu as pltpu
from jax.sharding import PartitionSpec as P

CAP = 6
BOTH = ("grp", "dev")
F32 = jnp.float32
BF16 = jnp.bfloat16
I32 = jnp.int32


def divide(values, by):
    if by & (by - 1) == 0:
        return values >> (by.bit_length() - 1)
    return (values * (-(-(1 << 16) // by))) >> 16


def iota(shape, dim):
    return lax.broadcasted_iota(I32, shape, dim)


def bits(condition):
    return jnp.where(condition, 1.0, 0.0)


def earlier(count):
    return bits(iota((count, count), 0) < iota((count, count), 1)).astype(BF16)


def dot(left, right):
    return jnp.dot(left, right, preferred_element_type=F32)


def dot_lanes(left, right):
    return lax.dot_general(left, right, (((1,), (1,)), ((), ())), preferred_element_type=F32)


def near_by(n):
    return [pl.BlockSpec(memory_space=pltpu.VMEM)] * n


def far_off(n):
    return [pl.BlockSpec(memory_space=pltpu.HBM)] * n


def call(kernel, outs, remote, operands, scratch, flops, name, limit=24 << 20, away=0):
    single = not isinstance(outs, tuple)
    leaves = (outs,) if single else outs
    moved = sum(a.size * a.dtype.itemsize for a in (*remote, *operands, *leaves))
    return pl.pallas_call(
        kernel,
        out_shape=outs if single else (*(pltpu.HBM(a.shape, a.dtype) for a in leaves[:away]), *leaves[away:]),
        in_specs=far_off(len(remote)) + near_by(len(operands)),
        out_specs=near_by(1)[0] if single else far_off(away) + near_by(len(leaves) - away),
        scratch_shapes=scratch,
        compiler_params=pltpu.CompilerParams(vmem_limit_bytes=limit),
        cost_estimate=pl.CostEstimate(flops=flops, bytes_accessed=moved, transcendentals=0),
        name=name,
    )(*(pltpu.with_memory_space_constraint(a, pltpu.HBM) for a in remote), *operands)


def fetches(weight_ref, held, sems):
    pieces = sems.shape[0]
    depth = weight_ref.shape[0] // pieces
    return [
        pltpu.make_async_copy(
            weight_ref.at[pl.ds(i * depth, depth)], held.at[pl.ds(i * depth, depth)], sems.at[i]
        )
        for i in range(pieces)
    ]


def dot_fetched(left, held, copies):
    depth = held.shape[0] // len(copies)
    result = None
    for i, copy in enumerate(copies):
        copy.wait()
        part = dot(left[:, i * depth : (i + 1) * depth], held[i * depth : (i + 1) * depth])
        result = part if result is None else result + part
    return result


def ask_kernel(
    members, peers, ids_hbm, mask_hbm, pos_hbm, features_hbm, ask_ref, near_ref, far_ref, order_ref, features_ref, ids, mask, pos_ref, sems
):
    degree, rows = ids.shape
    copies = [
        pltpu.make_async_copy(ids_hbm, ids, sems.at[0]),
        pltpu.make_async_copy(mask_hbm, mask, sems.at[1]),
        pltpu.make_async_copy(pos_hbm, pos_ref, sems.at[2]),
    ]
    table = pltpu.make_async_copy(features_hbm, features_ref, sems.at[3])
    for copy in (*copies, table):
        copy.start()
    own = lax.axis_index("grp") * members + lax.axis_index("dev")
    peer = iota((peers, rows), 0)
    size = peers * CAP
    line = iota((size, size), 0)
    device = divide(line, CAP)
    order_ref[...] = bits(iota((size, size), 1) == (line - device * CAP) * peers + device).astype(BF16)

    @pl.loop(0, 2)
    def _(i):
        @pl.when(i == 0)
        def _():
            copies[0].wait()
            copies[1].wait()

        @pl.when(i == 1)
        def _():
            copies[2].wait()

    prefix = earlier(rows)
    slots = jnp.where(mask[...] > 0, ids[...], -1)
    owner = divide(jnp.maximum(slots, 0), rows)
    row = slots - owner * rows
    live = slots >= 0
    here = owner == own
    key = jnp.where(live & jnp.logical_not(here), owner, -1)
    half = CAP // 2
    width = (rows - 1).bit_length()
    top = width * (half - 1)
    low = jnp.zeros((peers, rows), I32)
    high = jnp.zeros((peers, rows), I32)
    total = jnp.zeros((peers, rows), I32)
    for s in range(degree):
        hit = key[s : s + 1] == peer
        high = jnp.where(hit, (high << width) | (low >> top), high)
        low = jnp.where(hit, ((low & ((1 << top) - 1)) << width) | row[s : s + 1], low)
        total += jnp.where(hit, 1, 0)
    before = dot(total.astype(F32).astype(BF16), prefix).astype(I32)
    packed = [jnp.where(before == 0, low, 0), jnp.where(before == 0, high, jnp.where(before == half, low, 0))]
    for k in range(1, half):
        shift, rest = width * k, width * (half - k)
        inside = before == k
        packed[0] = jnp.where(inside, (low & ((1 << rest) - 1)) << shift, packed[0])
        packed[1] = jnp.where(inside, (high << shift) | (low >> rest), packed[1])
        packed[1] = jnp.where(before == half + k, low << shift, packed[1])
    lane = iota((peers, rows), 1)
    wanted = jnp.zeros((peers, rows), I32)
    for w, word in enumerate(packed):
        word = jnp.broadcast_to(jnp.sum(word.astype(F32), axis=1, keepdims=True).astype(I32), (peers, rows))
        for k in range(half):
            wanted = jnp.where(lane == w * half + k, (word >> (width * k)) & ((1 << width) - 1), wanted)
    pos = pos_ref[...]
    place = jnp.where(divide(pos, rows) == peer, pos - divide(pos, rows) * rows + 1, 0)
    ask_ref[...] = (place + wanted * (2 * rows)).reshape(peers, 1, rows)
    local = jnp.where(live & here, row, -1)
    node = iota((rows, rows), 0).astype(F32).astype(BF16)
    local = local.astype(F32).astype(BF16)
    one, none = jnp.ones((rows, rows), BF16), jnp.zeros((rows, rows), BF16)
    near = none
    for s in range(degree):
        near += jnp.where(local[s : s + 1] == node, one, none)
    near_ref[...] = near.astype(F32).T.astype(BF16)
    far = [bits((before <= k) & (k < before + total)).astype(BF16) for k in range(CAP)]
    far = jnp.concatenate(far, axis=0)
    far_ref[:, :size] = dot(order_ref[...], far).T.astype(BF16)
    count = jnp.broadcast_to(jnp.sum(bits(live), axis=0, keepdims=True), (rows, rows)).T.astype(BF16)
    far_ref[:, size:] = count[:, : far_ref.shape[1] - size]
    table.wait()


def store_rows(reply_ref, rows):
    peers, pairs, two, width = reply_ref.shape
    reply_ref[...] = rows.reshape(peers, pairs, two, width)


def load_rows(answer_ref):
    peers, pairs, two, width = answer_ref.shape
    return answer_ref[...].reshape(peers * pairs * two, width)


def serve_kernel(asked_ref, order_ref, source_ref, reply_ref, pick_ref):
    peers, _, rows = asked_ref.shape
    asked = asked_ref[...].reshape(peers, rows)
    wanted = divide(asked, 2 * rows)
    lane = iota((peers, rows), 1)
    picks = [bits(wanted[:, k : k + 1] == lane).astype(BF16) for k in range(CAP)]
    pick = dot(order_ref[...], jnp.concatenate(picks, axis=0)).astype(BF16)
    pick_ref[...] = pick
    store_rows(reply_ref, dot(pick, source_ref[...]).astype(BF16))


def over_count(summed, far):
    size = far.shape[1] - 8
    return (summed / far[:, size : size + 1].astype(F32)).astype(BF16)


def layer_one_kernel(
    features_ref, near_ref, answer_ref, far_ref, pick_ref, answer_hbm, mean_hbm, reply_hbm, mean_ref, reply_ref, sems
):
    kept = pltpu.make_async_copy(answer_ref, answer_hbm, sems.at[0])
    kept.start()
    answer = load_rows(answer_ref)
    far = far_ref[...]
    mean = over_count(dot(near_ref[...], features_ref[...]) + dot(far[:, : answer.shape[0]], answer), far)
    mean_ref[...] = mean
    saved = pltpu.make_async_copy(mean_ref, mean_hbm, sems.at[1])
    saved.start()
    store_rows(reply_ref, dot(pick_ref[...], mean).astype(BF16))
    sent = pltpu.make_async_copy(reply_ref, reply_hbm, sems.at[2])
    sent.start()
    kept.wait()
    saved.wait()
    sent.wait()


def between_kernel(
    members, self_one_hbm, self_two_hbm, neigh_two_hbm, pos_hbm, features_hbm, answer_hbm, mean_hbm,
    neigh_one_ref, near_ref, far_ref, asked_ref,
    final_hbm, place_hbm, base_ref, far_moved_ref, dense_ref, ready_ref,
    held_one, held_two, rest, features_ref, answer_ref, mean_ref, final_ref, place_ref, pos_ref, sems,
):
    ready = ready_ref.shape[0]
    copies = [
        pltpu.make_async_copy(pos_hbm, pos_ref, sems.at[0]),
        pltpu.make_async_copy(self_one_hbm, held_one, sems.at[1]),
        pltpu.make_async_copy(self_two_hbm, held_two, sems.at[2]),
        pltpu.make_async_copy(neigh_two_hbm.at[pl.ds(0, ready)], ready_ref, sems.at[3]),
        pltpu.make_async_copy(neigh_two_hbm.at[pl.ds(ready, rest.shape[0])], rest, sems.at[4]),
    ]
    inputs = [
        pltpu.make_async_copy(features_hbm, features_ref, sems.at[6]),
        pltpu.make_async_copy(answer_hbm, answer_ref, sems.at[7]),
        pltpu.make_async_copy(mean_hbm, mean_ref, sems.at[8]),
    ]
    for copy in (*inputs, *copies):
        copy.start()
    rows = features_ref.shape[0]
    capacity = 2 * rows // members
    me = lax.axis_index("dev")
    first = lax.axis_index("grp") * members
    line = iota((rows, rows), 0)
    step = divide(line, capacity)
    rank = line - step * capacity
    target = me + 2 * step
    target = jnp.where(target >= members, target - members, target)
    prefix = earlier(rows)
    copies[0].wait()
    goes = target == divide(pos_ref[...], rows) - first
    before = dot(bits(goes).astype(BF16), prefix).astype(I32)
    move = bits(goes & (before == rank)).astype(BF16)
    near = dot(move, near_ref[...]).astype(BF16)
    far = dot(move, far_ref[...]).astype(BF16)
    size = far.shape[1] - 8
    used = jnp.sum(far_ref[:, :size].astype(F32), axis=0, keepdims=True) > 0.0
    used = jnp.broadcast_to(used, dense_ref.shape)
    seats = dot(bits(used).astype(BF16), earlier(size)).astype(I32)
    dense = bits(used & (seats == iota(used.shape, 0))).astype(BF16)
    dense_ref[...] = dense
    held = dense.shape[0]
    far_moved_ref[:, :held] = dot_lanes(far[:, :size], dense).astype(BF16)
    far_moved_ref[:, held:] = far[:, size:]
    place = jnp.zeros((rows, rows), F32)
    for q in range(members // 2):
        source = me - 2 * q
        source = first + jnp.where(source < 0, source + members, source)
        sent = asked_ref[source] & (2 * rows - 1)
        valid = jnp.broadcast_to(sent > 0, (rows, rows))
        before = dot(bits(valid).astype(BF16), prefix).astype(I32)
        lands = bits(sent - 1 == line).astype(BF16)
        comes = bits(valid & (step == q) & (before == rank)).astype(BF16)
        place += dot_lanes(lands, comes)
    place_ref[...] = place.astype(BF16)
    placed = pltpu.make_async_copy(place_ref, place_hbm, sems.at[9])
    placed.start()
    for copy in (*inputs, copies[1]):
        copy.wait()
    own = dot(features_ref[...], held_one[...])
    base_ref[...] = dot(dot(dense, load_rows(answer_ref)).astype(BF16), held_one[...]).astype(BF16)
    hidden = jnp.maximum(own + dot(mean_ref[...], neigh_one_ref[...]), 0.0).astype(BF16)
    mean = over_count(dot(near, hidden), far)
    moved = dot(move, hidden).astype(BF16)
    copies[2].wait()
    final = dot(moved, held_two[...])
    copies[3].wait()
    final += dot(mean[:, :ready], ready_ref[...])
    copies[4].wait()
    final_ref[...] = (final + dot(mean[:, ready:], rest[...])).astype(BF16)
    away = pltpu.make_async_copy(final_ref, final_hbm, sems.at[10])
    away.start()
    away.wait()
    placed.wait()


def layer_two_kernel(neigh_two_hbm, final_hbm, neigh_one_ref, ready_ref, base_ref, answer_ref, far_ref, dense_ref, *refs):
    outs, (held, final_ref, mean_ref, sum_ref, sems) = refs[:-5], refs[-5:]
    ready = ready_ref.shape[0]
    pieces = sems.shape[0] - 1
    last = pltpu.make_async_copy(final_hbm, final_ref, sems.at[pieces])
    depth = held.shape[0] // pieces

    def fetch(i):
        piece = pl.ds(pl.multiple_of(i * depth, 16), depth)
        return pltpu.make_async_copy(neigh_two_hbm.at[pl.ds(ready, held.shape[0])].at[piece], held.at[piece], sems.at[i])

    @pl.loop(0, pieces)
    def _(i):
        fetch(i).start()

        @pl.when(i == pieces - 1)
        def _():
            last.start()

    far = far_ref[...]
    answer = dot(dense_ref[...], load_rows(answer_ref)).astype(BF16)
    other = jnp.maximum(base_ref[...].astype(F32) + dot(answer, neigh_one_ref[...]), 0.0).astype(BF16)
    mean = over_count(dot(far[:, : other.shape[0]], other), far)
    mean_ref[...] = mean[:, ready:]
    sum_ref[...] = dot(mean[:, :ready], ready_ref[...])

    @pl.loop(0, pieces)
    def _(i):
        fetch(i).wait()

    final = sum_ref[...] + dot(mean_ref[...], held[...])
    last.wait()
    final = (final + final_ref[...].astype(F32)).astype(BF16)
    capacity = outs[0].shape[0]
    for q, ref in enumerate(outs):
        ref[...] = final[q * capacity : (q + 1) * capacity]


def scatter_kernel(place_ref, *refs):
    out_ref = refs[-1]
    arrived = jnp.concatenate([ref[...] for ref in refs[:-1]], axis=0)
    out_ref[...] = dot(place_ref[...], arrived).astype(BF16)


def body(features, neighbours, neighbour_mask, layer2_position, self_weight1, neigh_weight1, self_weight2, neigh_weight2):
    rows, degree = neighbours.shape
    members = lax.axis_size("dev")
    peers = lax.axis_size("grp") * members
    width_in, width = self_weight1.shape
    steps = members // 2
    capacity = rows // steps
    size = peers * CAP
    early = width * 9 // 16
    held = -(-((peers - 1) * CAP // 2) // 16) * 16
    shape = jax.ShapeDtypeStruct
    copies = pltpu.SemaphoreType.DMA

    pos = layer2_position.reshape(1, rows)
    ask, near, far, order, table = call(
        functools.partial(ask_kernel, members, peers),
        (
            shape((peers, 1, rows), I32),
            shape((rows, rows), BF16),
            shape((rows, size + 8), BF16),
            shape((size, size), BF16),
            shape((rows, width_in), BF16),
        ),
        (neighbours.T, neighbour_mask.T, pos, features),
        (),
        [pltpu.VMEM((degree, rows), I32), pltpu.VMEM((degree, rows), I32), pltpu.VMEM((1, rows), I32), copies((4,))],
        2 * size * size * rows,
        "ask",
        limit=40 << 20,
    )
    asked = lax.all_to_all(ask, BOTH, 0, 0, tiled=True)
    reply, pick = call(
        serve_kernel,
        (shape((peers, CAP // 2, 2, width_in), BF16), shape((size, rows), BF16)),
        (),
        (asked, order, table),
        [],
        2 * size * rows * width_in,
        "serve",
    )
    answer = lax.all_to_all(reply, BOTH, 0, 0, tiled=True)
    kept, mean, reply_two = call(
        layer_one_kernel,
        (
            shape((peers, CAP // 2, 2, width_in), BF16),
            shape((rows, width_in), BF16),
            shape((peers, CAP // 2, 2, width_in), BF16),
        ),
        (),
        (table, near, answer, far, pick),
        [pltpu.VMEM((rows, width_in), BF16), pltpu.VMEM((peers, CAP // 2, 2, width_in), BF16), copies((3,))],
        2 * rows * width_in * (size + rows) + 2 * size * rows * width_in,
        "layer_one",
        away=3,
    )
    answer_two = lax.all_to_all(reply_two, BOTH, 0, 0, tiled=True)
    final, place, base, far_moved, dense, ready = call(
        functools.partial(between_kernel, members),
        (
            shape((rows, width), BF16),
            shape((rows, rows), BF16),
            shape((held, width), BF16),
            shape((rows, held + 8), BF16),
            shape((held, size), BF16),
            shape((early, width), BF16),
        ),
        (self_weight1, self_weight2, neigh_weight2, pos, features, kept, mean),
        (neigh_weight1, near, far, asked),
        [
            pltpu.VMEM((width_in, width), BF16),
            pltpu.VMEM((width, width), BF16),
            pltpu.VMEM((width - early, width), BF16),
            pltpu.VMEM((rows, width_in), BF16),
            pltpu.VMEM((peers, CAP // 2, 2, width_in), BF16),
            pltpu.VMEM((rows, width_in), BF16),
            pltpu.VMEM((rows, width), BF16),
            pltpu.VMEM((rows, rows), BF16),
            pltpu.VMEM((1, rows), I32),
            copies((11,)),
        ],
        2 * width * (rows * (2 * width_in + rows + 2 * width) + size * width_in),
        "between",
        limit=48 << 20,
        away=2,
    )
    finals = call(
        layer_two_kernel,
        tuple(shape((capacity, width), BF16) for _ in range(steps)),
        (neigh_weight2, final),
        (neigh_weight1, ready, base, answer_two, far_moved, dense),
        [
            pltpu.VMEM((width - early, width), BF16),
            pltpu.VMEM((rows, width), BF16),
            pltpu.VMEM((rows, width - early), BF16),
            pltpu.VMEM((rows, width), F32),
            copies((3,)),
        ],
        2 * width * (size * width_in + rows * (size + width)),
        "layer_two",
        limit=48 << 20,
    )
    arrived = [finals[0]]
    for q in range(1, steps):
        arrived.append(lax.ppermute(finals[q], "dev", [(i, (i + 2 * q) % members) for i in range(members)]))
    return call(
        scatter_kernel,
        shape((rows, width), BF16),
        (),
        (place, *arrived),
        [],
        2 * rows * rows * width,
        "scatter",
    )


def solution(mesh):
    return jax.shard_map(
        body,
        mesh=mesh,
        in_specs=(
            P(BOTH, None),
            P(BOTH, None),
            P(BOTH, None),
            P(BOTH),
            P(),
            P(),
            P(),
            P(),
        ),
        out_specs=P(BOTH, None),
        check_vma=False,
    )
```

```python
import functools

import jax
import jax.numpy as jnp
from jax import lax
from jax.experimental import pallas as pl
from jax.experimental.pallas import tpu as pltpu
from jax.sharding import PartitionSpec as P


CAP = 6
BOTH = ("grp", "dev")
F32 = jnp.float32
BF16 = jnp.bfloat16
I32 = jnp.int32


def divide(values, by):
    if by & (by - 1) == 0:
        return values >> (by.bit_length() - 1)
    return (values * (-(-(1 << 16) // by))) >> 16


def iota(shape, dim):
    return lax.broadcasted_iota(I32, shape, dim)


def bits(condition):
    return jnp.where(condition, 1.0, 0.0)


def earlier(count):
    return bits(iota((count, count), 0) < iota((count, count), 1)).astype(BF16)


def dot(left, right):
    return jnp.dot(left, right, preferred_element_type=F32)


def dot_lanes(left, right):
    return lax.dot_general(left, right, (((1,), (1,)), ((), ())), preferred_element_type=F32)


def near_by(n):
    return [pl.BlockSpec(memory_space=pltpu.VMEM)] * n


def far_off(n):
    return [pl.BlockSpec(memory_space=pltpu.HBM)] * n


def call(kernel, outs, remote, operands, scratch, flops, limit=24 << 20, away=0):
    single = not isinstance(outs, tuple)
    leaves = (outs,) if single else outs
    moved = sum(a.size * a.dtype.itemsize for a in (*remote, *operands, *leaves))
    return pl.pallas_call(
        kernel,
        out_shape=outs if single else (*(pltpu.HBM(a.shape, a.dtype) for a in leaves[:away]), *leaves[away:]),
        in_specs=far_off(len(remote)) + near_by(len(operands)),
        out_specs=near_by(1)[0] if single else far_off(away) + near_by(len(leaves) - away),
        scratch_shapes=scratch,
        compiler_params=pltpu.CompilerParams(vmem_limit_bytes=limit),
        cost_estimate=pl.CostEstimate(flops=flops, bytes_accessed=moved, transcendentals=0),
    )(*(pltpu.with_memory_space_constraint(a, pltpu.HBM) for a in remote), *operands)


def ask_kernel(
    members, peers, ids_hbm, mask_hbm, pos_hbm, features_hbm, ask_ref, near_ref, far_ref, order_ref, features_ref, ids, mask, pos_ref, sems
):
    degree, rows = ids.shape
    copies = [
        pltpu.make_async_copy(ids_hbm, ids, sems.at[0]),
        pltpu.make_async_copy(mask_hbm, mask, sems.at[1]),
        pltpu.make_async_copy(pos_hbm, pos_ref, sems.at[2]),
    ]
    table = pltpu.make_async_copy(features_hbm, features_ref, sems.at[3])
    for copy in (*copies, table):
        copy.start()
    own = lax.axis_index("grp") * members + lax.axis_index("dev")
    peer = iota((peers, rows), 0)
    prefix = earlier(rows)
    for copy in copies:
        copy.wait()
    slots = jnp.where(mask[...] > 0, ids[...], -1)
    owner = divide(jnp.maximum(slots, 0), rows)
    row = slots - owner * rows
    live = slots >= 0
    here = owner == own
    key = jnp.where(live & jnp.logical_not(here), owner, -1)
    half = CAP // 2
    width = (rows - 1).bit_length()
    top = width * (half - 1)
    low = jnp.zeros((peers, rows), I32)
    high = jnp.zeros((peers, rows), I32)
    total = jnp.zeros((peers, rows), I32)
    for s in range(degree):
        hit = key[s : s + 1] == peer
        high = jnp.where(hit, (high << width) | (low >> top), high)
        low = jnp.where(hit, ((low & ((1 << top) - 1)) << width) | row[s : s + 1], low)
        total += jnp.where(hit, 1, 0)
    before = dot(total.astype(F32).astype(BF16), prefix).astype(I32)
    packed = [jnp.where(before == 0, low, 0), jnp.where(before == 0, high, jnp.where(before == half, low, 0))]
    for k in range(1, half):
        shift, rest = width * k, width * (half - k)
        inside = before == k
        packed[0] = jnp.where(inside, (low & ((1 << rest) - 1)) << shift, packed[0])
        packed[1] = jnp.where(inside, (high << shift) | (low >> rest), packed[1])
        packed[1] = jnp.where(before == half + k, low << shift, packed[1])
    lane = iota((peers, rows), 1)
    wanted = jnp.zeros((peers, rows), I32)
    for w, word in enumerate(packed):
        word = jnp.broadcast_to(jnp.sum(word.astype(F32), axis=1, keepdims=True).astype(I32), (peers, rows))
        for k in range(half):
            wanted = jnp.where(lane == w * half + k, (word >> (width * k)) & ((1 << width) - 1), wanted)
    pos = pos_ref[...]
    place = jnp.where(divide(pos, rows) == peer, pos - divide(pos, rows) * rows + 1, 0)
    ask_ref[...] = (place + wanted * (2 * rows)).reshape(peers, 1, rows)
    local = jnp.where(live & here, row, -1)
    node = iota((rows, rows), 0).astype(F32).astype(BF16)
    local = local.astype(F32).astype(BF16)
    one, none = jnp.ones((rows, rows), BF16), jnp.zeros((rows, rows), BF16)
    near = none
    for s in range(degree):
        near += jnp.where(local[s : s + 1] == node, one, none)
    near_ref[...] = near.astype(F32).T.astype(BF16)
    far = [bits((before <= k) & (k < before + total)).astype(BF16) for k in range(CAP)]
    far = jnp.concatenate(far, axis=0)
    size = peers * CAP
    line = iota((size, size), 0)
    device = divide(line, CAP)
    order = bits(iota((size, size), 1) == (line - device * CAP) * peers + device).astype(BF16)
    order_ref[...] = order
    far_ref[:, :size] = dot(order, far).T.astype(BF16)
    count = jnp.broadcast_to(jnp.sum(bits(live), axis=0, keepdims=True), (rows, rows)).T.astype(BF16)
    far_ref[:, size:] = count[:, : far_ref.shape[1] - size]
    table.wait()


def store_rows(reply_ref, rows):
    peers, pairs, two, width = reply_ref.shape
    reply_ref[...] = rows.reshape(peers, pairs, two, width)


def load_rows(answer_ref):
    peers, pairs, two, width = answer_ref.shape
    return answer_ref[...].reshape(peers * pairs * two, width)


def serve_kernel(asked_ref, order_ref, source_ref, reply_ref, pick_ref):
    peers, _, rows = asked_ref.shape
    asked = asked_ref[...].reshape(peers, rows)
    wanted = divide(asked, 2 * rows)
    lane = iota((peers, rows), 1)
    picks = [bits(wanted[:, k : k + 1] == lane).astype(BF16) for k in range(CAP)]
    pick = dot(order_ref[...], jnp.concatenate(picks, axis=0)).astype(BF16)
    pick_ref[...] = pick
    store_rows(reply_ref, dot(pick, source_ref[...]).astype(BF16))


def over_count(summed, far):
    size = far.shape[1] - 8
    return (summed / far[:, size : size + 1].astype(F32)).astype(BF16)


def layer_one_kernel(
    features_ref, near_ref, answer_ref, far_ref, pick_ref, answer_hbm, mean_hbm, reply_hbm, mean_ref, reply_ref, sems
):
    kept = pltpu.make_async_copy(answer_ref, answer_hbm, sems.at[0])
    kept.start()
    answer = load_rows(answer_ref)
    far = far_ref[...]
    mean = over_count(dot(near_ref[...], features_ref[...]) + dot(far[:, : answer.shape[0]], answer), far)
    mean_ref[...] = mean
    saved = pltpu.make_async_copy(mean_ref, mean_hbm, sems.at[1])
    saved.start()
    store_rows(reply_ref, dot(pick_ref[...], mean).astype(BF16))
    sent = pltpu.make_async_copy(reply_ref, reply_hbm, sems.at[2])
    sent.start()
    kept.wait()
    saved.wait()
    sent.wait()


def between_kernel(
    members, self_one_hbm, neigh_one_hbm, self_two_hbm, neigh_two_hbm, pos_hbm, features_hbm, answer_hbm, mean_hbm,
    near_ref, far_ref, asked_ref,
    final_hbm, place_hbm, base_ref, far_moved_ref, dense_ref, neigh_one_ref, ready_ref,
    held_one, held_two, rest, features_ref, answer_ref, mean_ref, final_ref, place_ref, pos_ref, sems,
):
    ready = ready_ref.shape[0]
    copies = [
        pltpu.make_async_copy(pos_hbm, pos_ref, sems.at[0]),
        pltpu.make_async_copy(self_one_hbm, held_one, sems.at[1]),
        pltpu.make_async_copy(neigh_one_hbm, neigh_one_ref, sems.at[2]),
        pltpu.make_async_copy(self_two_hbm, held_two, sems.at[3]),
        pltpu.make_async_copy(neigh_two_hbm.at[pl.ds(0, ready)], ready_ref, sems.at[4]),
        pltpu.make_async_copy(neigh_two_hbm.at[pl.ds(ready, rest.shape[0])], rest, sems.at[5]),
    ]
    inputs = [
        pltpu.make_async_copy(features_hbm, features_ref, sems.at[6]),
        pltpu.make_async_copy(answer_hbm, answer_ref, sems.at[7]),
        pltpu.make_async_copy(mean_hbm, mean_ref, sems.at[8]),
    ]
    for copy in (*inputs, *copies):
        copy.start()
    rows = features_ref.shape[0]
    capacity = 2 * rows // members
    me = lax.axis_index("dev")
    first = lax.axis_index("grp") * members
    line = iota((rows, rows), 0)
    step = divide(line, capacity)
    rank = line - step * capacity
    target = me ^ (2 * step)
    prefix = earlier(rows)
    copies[0].wait()
    goes = target == divide(pos_ref[...], rows) - first
    before = dot(bits(goes).astype(BF16), prefix).astype(I32)
    move = bits(goes & (before == rank)).astype(BF16)
    near = dot(move, near_ref[...]).astype(BF16)
    far = dot(move, far_ref[...]).astype(BF16)
    size = far.shape[1] - 8
    used = jnp.sum(far_ref[:, :size].astype(F32), axis=0, keepdims=True) > 0.0
    used = jnp.broadcast_to(used, dense_ref.shape)
    seats = dot(bits(used).astype(BF16), earlier(size)).astype(I32)
    dense = bits(used & (seats == iota(used.shape, 0))).astype(BF16)
    dense_ref[...] = dense
    held = dense.shape[0]
    far_moved_ref[:, :held] = dot_lanes(far[:, :size], dense).astype(BF16)
    far_moved_ref[:, held:] = far[:, size:]
    place = jnp.zeros((rows, rows), F32)
    for q in range(members // 2):
        source = first + (me ^ (2 * q))
        sent = asked_ref[source] & (2 * rows - 1)
        valid = jnp.broadcast_to(sent > 0, (rows, rows))
        before = dot(bits(valid).astype(BF16), prefix).astype(I32)
        lands = bits(sent - 1 == line).astype(BF16)
        comes = bits(valid & (step == q) & (before == rank)).astype(BF16)
        place += dot_lanes(lands, comes)
    place_ref[...] = place.astype(BF16)
    placed = pltpu.make_async_copy(place_ref, place_hbm, sems.at[9])
    placed.start()
    for copy in (*inputs, copies[1]):
        copy.wait()
    own = dot(features_ref[...], held_one[...])
    base_ref[...] = dot(dot(dense, load_rows(answer_ref)).astype(BF16), held_one[...]).astype(BF16)
    copies[2].wait()
    hidden = jnp.maximum(own + dot(mean_ref[...], neigh_one_ref[...]), 0.0).astype(BF16)
    mean = over_count(dot(near, hidden), far)
    moved = dot(move, hidden).astype(BF16)
    copies[3].wait()
    final = dot(moved, held_two[...])
    copies[4].wait()
    final += dot(mean[:, :ready], ready_ref[...])
    copies[5].wait()
    final_ref[...] = (final + dot(mean[:, ready:], rest[...])).astype(BF16)
    away = pltpu.make_async_copy(final_ref, final_hbm, sems.at[10])
    away.start()
    away.wait()
    placed.wait()


def layer_two_kernel(neigh_two_hbm, final_hbm, neigh_one_ref, ready_ref, base_ref, answer_ref, far_ref, dense_ref, *refs):
    outs, (held, final_ref, mean_ref, sum_ref, sems) = refs[:-5], refs[-5:]
    ready = ready_ref.shape[0]
    pieces = sems.shape[0] - 1
    last = pltpu.make_async_copy(final_hbm, final_ref, sems.at[pieces])
    depth = held.shape[0] // pieces

    def fetch(i):
        piece = pl.ds(pl.multiple_of(i * depth, 16), depth)
        return pltpu.make_async_copy(neigh_two_hbm.at[pl.ds(ready, held.shape[0])].at[piece], held.at[piece], sems.at[i])

    @pl.loop(0, pieces)
    def _(i):
        fetch(i).start()

        @pl.when(i == pieces - 1)
        def _():
            last.start()

    far = far_ref[...]
    answer = dot(dense_ref[...], load_rows(answer_ref)).astype(BF16)
    other = jnp.maximum(base_ref[...].astype(F32) + dot(answer, neigh_one_ref[...]), 0.0).astype(BF16)
    mean = over_count(dot(far[:, : other.shape[0]], other), far)
    mean_ref[...] = mean[:, ready:]
    sum_ref[...] = dot(mean[:, :ready], ready_ref[...])

    @pl.loop(0, pieces)
    def _(i):
        fetch(i).wait()

    final = sum_ref[...] + dot(mean_ref[...], held[...])
    last.wait()
    final = (final + final_ref[...].astype(F32)).astype(BF16)
    capacity = outs[0].shape[0]
    for q, ref in enumerate(outs):
        ref[...] = final[q * capacity : (q + 1) * capacity]


def scatter_kernel(place_ref, *refs):
    out_ref = refs[-1]
    arrived = jnp.concatenate([ref[...] for ref in refs[:-1]], axis=0)
    out_ref[...] = dot(place_ref[...], arrived).astype(BF16)


def compute(features, neighbours, neighbour_mask, layer2_position, self_weight1, neigh_weight1, self_weight2, neigh_weight2):
    rows, degree = neighbours.shape
    members = lax.axis_size("dev")
    peers = lax.axis_size("grp") * members
    width_in, width = self_weight1.shape
    steps = members // 2
    capacity = rows // steps
    size = peers * CAP
    early = width * 9 // 16
    held = -(-((peers - 1) * CAP // 2) // 16) * 16
    shape = jax.ShapeDtypeStruct
    copies = pltpu.SemaphoreType.DMA

    pos = layer2_position.reshape(1, rows)
    ask, near, far, order, table = call(
        functools.partial(ask_kernel, members, peers),
        (
            shape((peers, 1, rows), I32),
            shape((rows, rows), BF16),
            shape((rows, size + 8), BF16),
            shape((size, size), BF16),
            shape((rows, width_in), BF16),
        ),
        (neighbours.T, neighbour_mask.T, pos, features),
        (),
        [pltpu.VMEM((degree, rows), I32), pltpu.VMEM((degree, rows), I32), pltpu.VMEM((1, rows), I32), copies((4,))],
        2 * size * size * rows,
        limit=40 << 20,
    )
    asked = lax.all_to_all(ask, BOTH, 0, 0, tiled=True)
    reply, pick = call(
        serve_kernel,
        (shape((peers, CAP // 2, 2, width_in), BF16), shape((size, rows), BF16)),
        (),
        (asked, order, table),
        [],
        2 * size * rows * width_in,
    )
    answer = lax.all_to_all(reply, BOTH, 0, 0, tiled=True)
    kept, mean, reply_two = call(
        layer_one_kernel,
        (
            shape((peers, CAP // 2, 2, width_in), BF16),
            shape((rows, width_in), BF16),
            shape((peers, CAP // 2, 2, width_in), BF16),
        ),
        (),
        (table, near, answer, far, pick),
        [pltpu.VMEM((rows, width_in), BF16), pltpu.VMEM((peers, CAP // 2, 2, width_in), BF16), copies((3,))],
        2 * rows * width_in * (size + rows) + 2 * size * rows * width_in,
        away=3,
    )
    answer_two = lax.all_to_all(reply_two, BOTH, 0, 0, tiled=True)
    final, place, base, far_moved, dense, weight, ready = call(
        functools.partial(between_kernel, members),
        (
            shape((rows, width), BF16),
            shape((rows, rows), BF16),
            shape((held, width), BF16),
            shape((rows, held + 8), BF16),
            shape((held, size), BF16),
            shape((width_in, width), BF16),
            shape((early, width), BF16),
        ),
        (self_weight1, neigh_weight1, self_weight2, neigh_weight2, pos, features, kept, mean),
        (near, far, asked),
        [
            pltpu.VMEM((width_in, width), BF16),
            pltpu.VMEM((width, width), BF16),
            pltpu.VMEM((width - early, width), BF16),
            pltpu.VMEM((rows, width_in), BF16),
            pltpu.VMEM((peers, CAP // 2, 2, width_in), BF16),
            pltpu.VMEM((rows, width_in), BF16),
            pltpu.VMEM((rows, width), BF16),
            pltpu.VMEM((rows, rows), BF16),
            pltpu.VMEM((1, rows), I32),
            copies((11,)),
        ],
        2 * width * (rows * (2 * width_in + rows + 2 * width) + size * width_in),
        limit=48 << 20,
        away=2,
    )
    finals = call(
        layer_two_kernel,
        tuple(shape((capacity, width), BF16) for _ in range(steps)),
        (neigh_weight2, final),
        (weight, ready, base, answer_two, far_moved, dense),
        [
            pltpu.VMEM((width - early, width), BF16),
            pltpu.VMEM((rows, width), BF16),
            pltpu.VMEM((rows, width - early), BF16),
            pltpu.VMEM((rows, width), F32),
            copies((3,)),
        ],
        2 * width * (size * width_in + rows * (size + width)),
        limit=48 << 20,
    )
    arrived = [finals[0]]
    for q in range(1, steps):
        arrived.append(lax.ppermute(finals[q], "dev", [(i, i ^ (2 * q)) for i in range(members)]))
    return call(scatter_kernel, shape((rows, width), BF16), (), (place, *arrived), [], 2 * rows * rows * width)


def solution(mesh):
    return jax.shard_map(
        compute,
        mesh=mesh,
        in_specs=(
            P(BOTH, None),
            P(BOTH, None),
            P(BOTH, None),
            P(BOTH),
            P(),
            P(),
            P(),
            P(),
        ),
        out_specs=P(BOTH, None),
        check_vma=False,
    )
```

```python
import functools

import jax
import jax.numpy as jnp
from jax import lax
from jax.experimental import pallas as pl
from jax.experimental.pallas import tpu as pltpu
from jax.sharding import PartitionSpec as P

CAP = 6
BOTH = ("grp", "dev")
F32 = jnp.float32
BF16 = jnp.bfloat16
I32 = jnp.int32


def divide(values, by):
    if by & (by - 1) == 0:
        return values >> (by.bit_length() - 1)
    return (values * (-(-(1 << 16) // by))) >> 16


def iota(shape, dim):
    return lax.broadcasted_iota(I32, shape, dim)


def bits(condition):
    return jnp.where(condition, 1.0, 0.0)


def earlier(count):
    return bits(iota((count, count), 0) < iota((count, count), 1)).astype(BF16)


def dot(left, right):
    return jnp.dot(left, right, preferred_element_type=F32)


def dot_lanes(left, right):
    return lax.dot_general(left, right, (((1,), (1,)), ((), ())), preferred_element_type=F32)


def near_by(n):
    return [pl.BlockSpec(memory_space=pltpu.VMEM)] * n


def far_off(n):
    return [pl.BlockSpec(memory_space=pltpu.HBM)] * n


def call(kernel, outs, remote, operands, scratch, flops, name, limit=24 << 20, away=0):
    single = not isinstance(outs, tuple)
    leaves = (outs,) if single else outs
    moved = sum(a.size * a.dtype.itemsize for a in (*remote, *operands, *leaves))
    return pl.pallas_call(
        kernel,
        out_shape=outs if single else (*(pltpu.HBM(a.shape, a.dtype) for a in leaves[:away]), *leaves[away:]),
        in_specs=far_off(len(remote)) + near_by(len(operands)),
        out_specs=near_by(1)[0] if single else far_off(away) + near_by(len(leaves) - away),
        scratch_shapes=scratch,
        compiler_params=pltpu.CompilerParams(vmem_limit_bytes=limit),
        cost_estimate=pl.CostEstimate(flops=flops, bytes_accessed=moved, transcendentals=0),
        name=name,
    )(*(pltpu.with_memory_space_constraint(a, pltpu.HBM) for a in remote), *operands)


def fetches(weight_ref, held, sems):
    pieces = sems.shape[0]
    depth = weight_ref.shape[0] // pieces
    return [
        pltpu.make_async_copy(
            weight_ref.at[pl.ds(i * depth, depth)], held.at[pl.ds(i * depth, depth)], sems.at[i]
        )
        for i in range(pieces)
    ]


def dot_fetched(left, held, copies):
    depth = held.shape[0] // len(copies)
    result = None
    for i, copy in enumerate(copies):
        copy.wait()
        part = dot(left[:, i * depth : (i + 1) * depth], held[i * depth : (i + 1) * depth])
        result = part if result is None else result + part
    return result


def ask_kernel(
    members, peers, ids_hbm, mask_hbm, pos_hbm, features_hbm, ask_ref, near_ref, far_ref, order_ref, features_ref, ids, mask, pos_ref, sems
):
    degree, rows = ids.shape
    copies = [
        pltpu.make_async_copy(ids_hbm, ids, sems.at[0]),
        pltpu.make_async_copy(mask_hbm, mask, sems.at[1]),
        pltpu.make_async_copy(pos_hbm, pos_ref, sems.at[2]),
    ]
    table = pltpu.make_async_copy(features_hbm, features_ref, sems.at[3])
    for copy in (*copies, table):
        copy.start()
    own = lax.axis_index("grp") * members + lax.axis_index("dev")
    peer = iota((peers, rows), 0)
    size = peers * CAP
    line = iota((size, size), 0)
    device = divide(line, CAP)
    order_ref[...] = bits(iota((size, size), 1) == (line - device * CAP) * peers + device).astype(BF16)

    @pl.loop(0, 2)
    def _(i):
        @pl.when(i == 0)
        def _():
            copies[0].wait()
            copies[1].wait()

        @pl.when(i == 1)
        def _():
            copies[2].wait()

    prefix = earlier(rows)
    slots = jnp.where(mask[...] > 0, ids[...], -1)
    owner = divide(jnp.maximum(slots, 0), rows)
    row = slots - owner * rows
    live = slots >= 0
    here = owner == own
    key = jnp.where(live & jnp.logical_not(here), owner, -1)
    half = CAP // 2
    width = (rows - 1).bit_length()
    top = width * (half - 1)
    low = jnp.zeros((peers, rows), I32)
    high = jnp.zeros((peers, rows), I32)
    total = jnp.zeros((peers, rows), I32)
    for s in range(degree):
        hit = key[s : s + 1] == peer
        high = jnp.where(hit, (high << width) | (low >> top), high)
        low = jnp.where(hit, ((low & ((1 << top) - 1)) << width) | row[s : s + 1], low)
        total += jnp.where(hit, 1, 0)
    before = dot(total.astype(F32).astype(BF16), prefix).astype(I32)
    packed = [jnp.where(before == 0, low, 0), jnp.where(before == 0, high, jnp.where(before == half, low, 0))]
    for k in range(1, half):
        shift, rest = width * k, width * (half - k)
        inside = before == k
        packed[0] = jnp.where(inside, (low & ((1 << rest) - 1)) << shift, packed[0])
        packed[1] = jnp.where(inside, (high << shift) | (low >> rest), packed[1])
        packed[1] = jnp.where(before == half + k, low << shift, packed[1])
    lane = iota((peers, rows), 1)
    wanted = jnp.zeros((peers, rows), I32)
    for w, word in enumerate(packed):
        word = jnp.broadcast_to(jnp.sum(word.astype(F32), axis=1, keepdims=True).astype(I32), (peers, rows))
        for k in range(half):
            wanted = jnp.where(lane == w * half + k, (word >> (width * k)) & ((1 << width) - 1), wanted)
    pos = pos_ref[...]
    place = jnp.where(divide(pos, rows) == peer, pos - divide(pos, rows) * rows + 1, 0)
    ask_ref[...] = (place + wanted * (2 * rows)).reshape(peers, 1, rows)
    local = jnp.where(live & here, row, -1)
    node = iota((rows, rows), 0).astype(F32).astype(BF16)
    local = local.astype(F32).astype(BF16)
    one, none = jnp.ones((rows, rows), BF16), jnp.zeros((rows, rows), BF16)
    near = none
    for s in range(degree):
        near += jnp.where(local[s : s + 1] == node, one, none)
    near_ref[...] = near.astype(F32).T.astype(BF16)
    far = [bits((before <= k) & (k < before + total)).astype(BF16) for k in range(CAP)]
    far = jnp.concatenate(far, axis=0)
    far_ref[:, :size] = dot(order_ref[...], far).T.astype(BF16)
    count = jnp.broadcast_to(jnp.sum(bits(live), axis=0, keepdims=True), (rows, rows)).T.astype(BF16)
    far_ref[:, size:] = count[:, : far_ref.shape[1] - size]
    table.wait()


def store_rows(reply_ref, rows):
    peers, pairs, two, width = reply_ref.shape
    reply_ref[...] = rows.reshape(peers, pairs, two, width)


def load_rows(answer_ref):
    peers, pairs, two, width = answer_ref.shape
    return answer_ref[...].reshape(peers * pairs * two, width)


def serve_kernel(asked_ref, order_ref, source_ref, reply_ref, pick_ref):
    peers, _, rows = asked_ref.shape
    asked = asked_ref[...].reshape(peers, rows)
    wanted = divide(asked, 2 * rows)
    lane = iota((peers, rows), 1)
    picks = [bits(wanted[:, k : k + 1] == lane).astype(BF16) for k in range(CAP)]
    pick = dot(order_ref[...], jnp.concatenate(picks, axis=0)).astype(BF16)
    pick_ref[...] = pick
    store_rows(reply_ref, dot(pick, source_ref[...]).astype(BF16))


def over_count(summed, far):
    size = far.shape[1] - 8
    return (summed / far[:, size : size + 1].astype(F32)).astype(BF16)


def layer_one_kernel(
    features_ref, near_ref, answer_ref, far_ref, pick_ref, answer_hbm, mean_hbm, reply_hbm, mean_ref, reply_ref, sems
):
    kept = pltpu.make_async_copy(answer_ref, answer_hbm, sems.at[0])
    kept.start()
    answer = load_rows(answer_ref)
    far = far_ref[...]
    mean = over_count(dot(near_ref[...], features_ref[...]) + dot(far[:, : answer.shape[0]], answer), far)
    mean_ref[...] = mean
    saved = pltpu.make_async_copy(mean_ref, mean_hbm, sems.at[1])
    saved.start()
    half = reply_ref.shape[0] // 2
    depth = pick_ref.shape[0] // 2
    sent = []
    for i in range(2):
        piece = pl.ds(i * half, half)
        store_rows(reply_ref.at[piece], dot(pick_ref[i * depth : (i + 1) * depth], mean).astype(BF16))
        sent.append(pltpu.make_async_copy(reply_ref.at[piece], reply_hbm.at[piece], sems.at[2 + i]))
        sent[-1].start()
    for copy in (kept, saved, *sent):
        copy.wait()


def between_kernel(
    members, self_one_hbm, neigh_one_hbm, self_two_hbm, neigh_two_hbm, pos_hbm, features_hbm, answer_hbm, mean_hbm,
    near_ref, far_ref, asked_ref,
    final_hbm, place_hbm, base_ref, far_moved_ref, dense_ref, neigh_one_ref, ready_ref,
    held_one, held_two, rest, features_ref, answer_ref, mean_ref, final_ref, place_ref, pos_ref, sems,
):
    ready = ready_ref.shape[0]
    copies = [
        pltpu.make_async_copy(pos_hbm, pos_ref, sems.at[0]),
        pltpu.make_async_copy(self_one_hbm, held_one, sems.at[1]),
        pltpu.make_async_copy(neigh_one_hbm, neigh_one_ref, sems.at[2]),
        pltpu.make_async_copy(self_two_hbm, held_two, sems.at[3]),
        pltpu.make_async_copy(neigh_two_hbm.at[pl.ds(0, ready)], ready_ref, sems.at[4]),
        pltpu.make_async_copy(neigh_two_hbm.at[pl.ds(ready, rest.shape[0])], rest, sems.at[5]),
    ]
    inputs = [
        pltpu.make_async_copy(features_hbm, features_ref, sems.at[6]),
        pltpu.make_async_copy(answer_hbm, answer_ref, sems.at[7]),
        pltpu.make_async_copy(mean_hbm, mean_ref, sems.at[8]),
    ]
    for copy in (*inputs, *copies):
        copy.start()
    rows = features_ref.shape[0]
    capacity = 2 * rows // members
    me = lax.axis_index("dev")
    first = lax.axis_index("grp") * members
    line = iota((rows, rows), 0)
    step = divide(line, capacity)
    rank = line - step * capacity
    target = me + 2 * step
    target = jnp.where(target >= members, target - members, target)
    prefix = earlier(rows)
    copies[0].wait()
    goes = target == divide(pos_ref[...], rows) - first
    before = dot(bits(goes).astype(BF16), prefix).astype(I32)
    move = bits(goes & (before == rank)).astype(BF16)
    near = dot(move, near_ref[...]).astype(BF16)
    far = dot(move, far_ref[...]).astype(BF16)
    size = far.shape[1] - 8
    used = jnp.sum(far_ref[:, :size].astype(F32), axis=0, keepdims=True) > 0.0
    used = jnp.broadcast_to(used, dense_ref.shape)
    seats = dot(bits(used).astype(BF16), earlier(size)).astype(I32)
    dense = bits(used & (seats == iota(used.shape, 0))).astype(BF16)
    dense_ref[...] = dense
    held = dense.shape[0]
    far_moved_ref[:, :held] = dot_lanes(far[:, :size], dense).astype(BF16)
    far_moved_ref[:, held:] = far[:, size:]
    place = jnp.zeros((rows, rows), F32)
    for q in range(members // 2):
        source = me - 2 * q
        source = first + jnp.where(source < 0, source + members, source)
        sent = asked_ref[source] & (2 * rows - 1)
        valid = jnp.broadcast_to(sent > 0, (rows, rows))
        before = dot(bits(valid).astype(BF16), prefix).astype(I32)
        lands = bits(sent - 1 == line).astype(BF16)
        comes = bits(valid & (step == q) & (before == rank)).astype(BF16)
        place += dot_lanes(lands, comes)
    place_ref[...] = place.astype(BF16)
    placed = pltpu.make_async_copy(place_ref, place_hbm, sems.at[9])
    placed.start()
    for copy in (*inputs, copies[1]):
        copy.wait()
    own = dot(features_ref[...], held_one[...])
    base_ref[...] = dot(dot(dense, load_rows(answer_ref)).astype(BF16), held_one[...]).astype(BF16)
    copies[2].wait()
    hidden = jnp.maximum(own + dot(mean_ref[...], neigh_one_ref[...]), 0.0).astype(BF16)
    mean = over_count(dot(near, hidden), far)
    moved = dot(move, hidden).astype(BF16)
    copies[3].wait()
    final = dot(moved, held_two[...])
    copies[4].wait()
    final += dot(mean[:, :ready], ready_ref[...])
    copies[5].wait()
    final_ref[...] = (final + dot(mean[:, ready:], rest[...])).astype(BF16)
    away = pltpu.make_async_copy(final_ref, final_hbm, sems.at[10])
    away.start()
    away.wait()
    placed.wait()


def layer_two_kernel(neigh_two_hbm, final_hbm, neigh_one_ref, ready_ref, base_ref, answer_ref, far_ref, dense_ref, *refs):
    outs, (held, final_ref, mean_ref, sum_ref, sems) = refs[:-5], refs[-5:]
    ready = ready_ref.shape[0]
    pieces = sems.shape[0] - 1
    last = pltpu.make_async_copy(final_hbm, final_ref, sems.at[pieces])
    depth = held.shape[0] // pieces

    def fetch(i):
        piece = pl.ds(pl.multiple_of(i * depth, 16), depth)
        return pltpu.make_async_copy(neigh_two_hbm.at[pl.ds(ready, held.shape[0])].at[piece], held.at[piece], sems.at[i])

    @pl.loop(0, pieces)
    def _(i):
        fetch(i).start()

        @pl.when(i == pieces - 1)
        def _():
            last.start()

    far = far_ref[...]
    answer = dot(dense_ref[...], load_rows(answer_ref)).astype(BF16)
    other = jnp.maximum(base_ref[...].astype(F32) + dot(answer, neigh_one_ref[...]), 0.0).astype(BF16)
    mean = over_count(dot(far[:, : other.shape[0]], other), far)
    mean_ref[...] = mean[:, ready:]
    sum_ref[...] = dot(mean[:, :ready], ready_ref[...])

    @pl.loop(0, pieces)
    def _(i):
        fetch(i).wait()

    final = sum_ref[...] + dot(mean_ref[...], held[...])
    last.wait()
    final = (final + final_ref[...].astype(F32)).astype(BF16)
    capacity = outs[0].shape[0]
    for q, ref in enumerate(outs):
        ref[...] = final[q * capacity : (q + 1) * capacity]


def scatter_kernel(place_ref, *refs):
    out_ref = refs[-1]
    arrived = jnp.concatenate([ref[...] for ref in refs[:-1]], axis=0)
    out_ref[...] = dot(place_ref[...], arrived).astype(BF16)


def body(features, neighbours, neighbour_mask, layer2_position, self_weight1, neigh_weight1, self_weight2, neigh_weight2):
    rows, degree = neighbours.shape
    members = lax.axis_size("dev")
    peers = lax.axis_size("grp") * members
    width_in, width = self_weight1.shape
    steps = members // 2
    capacity = rows // steps
    size = peers * CAP
    early = width * 9 // 16
    held = -(-((peers - 1) * CAP // 2) // 16) * 16
    shape = jax.ShapeDtypeStruct
    copies = pltpu.SemaphoreType.DMA

    pos = layer2_position.reshape(1, rows)
    ask, near, far, order, table = call(
        functools.partial(ask_kernel, members, peers),
        (
            shape((peers, 1, rows), I32),
            shape((rows, rows), BF16),
            shape((rows, size + 8), BF16),
            shape((size, size), BF16),
            shape((rows, width_in), BF16),
        ),
        (neighbours.T, neighbour_mask.T, pos, features),
        (),
        [pltpu.VMEM((degree, rows), I32), pltpu.VMEM((degree, rows), I32), pltpu.VMEM((1, rows), I32), copies((4,))],
        2 * size * size * rows,
        "ask",
        limit=40 << 20,
    )
    asked = lax.all_to_all(ask, BOTH, 0, 0, tiled=True)
    reply, pick = call(
        serve_kernel,
        (shape((peers, CAP // 2, 2, width_in), BF16), shape((size, rows), BF16)),
        (),
        (asked, order, table),
        [],
        2 * size * rows * width_in,
        "serve",
    )
    answer = lax.all_to_all(reply, BOTH, 0, 0, tiled=True)
    kept, mean, reply_two = call(
        layer_one_kernel,
        (
            shape((peers, CAP // 2, 2, width_in), BF16),
            shape((rows, width_in), BF16),
            shape((peers, CAP // 2, 2, width_in), BF16),
        ),
        (),
        (table, near, answer, far, pick),
        [pltpu.VMEM((rows, width_in), BF16), pltpu.VMEM((peers, CAP // 2, 2, width_in), BF16), copies((4,))],
        2 * rows * width_in * (size + rows) + 2 * size * rows * width_in,
        "layer_one",
        away=3,
    )
    answer_two = lax.all_to_all(reply_two, BOTH, 0, 0, tiled=True)
    final, place, base, far_moved, dense, weight, ready = call(
        functools.partial(between_kernel, members),
        (
            shape((rows, width), BF16),
            shape((rows, rows), BF16),
            shape((held, width), BF16),
            shape((rows, held + 8), BF16),
            shape((held, size), BF16),
            shape((width_in, width), BF16),
            shape((early, width), BF16),
        ),
        (self_weight1, neigh_weight1, self_weight2, neigh_weight2, pos, features, kept, mean),
        (near, far, asked),
        [
            pltpu.VMEM((width_in, width), BF16),
            pltpu.VMEM((width, width), BF16),
            pltpu.VMEM((width - early, width), BF16),
            pltpu.VMEM((rows, width_in), BF16),
            pltpu.VMEM((peers, CAP // 2, 2, width_in), BF16),
            pltpu.VMEM((rows, width_in), BF16),
            pltpu.VMEM((rows, width), BF16),
            pltpu.VMEM((rows, rows), BF16),
            pltpu.VMEM((1, rows), I32),
            copies((11,)),
        ],
        2 * width * (rows * (2 * width_in + rows + 2 * width) + size * width_in),
        "between",
        limit=48 << 20,
        away=2,
    )
    finals = call(
        layer_two_kernel,
        tuple(shape((capacity, width), BF16) for _ in range(steps)),
        (neigh_weight2, final),
        (weight, ready, base, answer_two, far_moved, dense),
        [
            pltpu.VMEM((width - early, width), BF16),
            pltpu.VMEM((rows, width), BF16),
            pltpu.VMEM((rows, width - early), BF16),
            pltpu.VMEM((rows, width), F32),
            copies((3,)),
        ],
        2 * width * (size * width_in + rows * (size + width)),
        "layer_two",
        limit=48 << 20,
    )
    arrived = [finals[0]]
    for q in range(1, steps):
        arrived.append(lax.ppermute(finals[q], "dev", [(i, (i + 2 * q) % members) for i in range(members)]))
    return call(
        scatter_kernel,
        shape((rows, width), BF16),
        (),
        (place, *arrived),
        [],
        2 * rows * rows * width,
        "scatter",
    )


def solution(mesh):
    return jax.shard_map(
        body,
        mesh=mesh,
        in_specs=(
            P(BOTH, None),
            P(BOTH, None),
            P(BOTH, None),
            P(BOTH),
            P(),
            P(),
            P(),
            P(),
        ),
        out_specs=P(BOTH, None),
        check_vma=False,
    )
```
